128 devices in a mesh: dp: 4 (over y), label: 32 (over z, x, core).
Axes of the slice: x: 4, y: 4, z: 4, core: 2. Of those that a mesh axis runs over, the one named last changes fastest.
Arguments:
- queries: bfloat16 [32768, 768], P(('dp', 'label')), may hold values from -6 to 6
- weights: bfloat16 [32, 4096, 768], P('label'), as said below
- beam: int32 [256, 4], P(('dp', 'label')), may hold values from -1 to 31, as said below
- positives: int32 [32768], P(('dp', 'label')), may hold values from 0 to 131071, as said below
- owner: int32 [32], replicated, may hold values from 0 to 31, each once
Outputs:
- loss: float32 [32768], P(('dp', 'label'))
- grad_queries: float32 [32768, 768], P(('dp', 'label'))
- grad_weights: float32 [32, 4096, 768], P('label', 'dp')
The draws below stay inside these ranges and needn't reach their ends.
Inputs may be any that keep to these rules, and one draw needn't show every extreme that they name: `beam`: each row lists 3 or 4 distinct block ids, then -1 entries. The query blocks of one device list pairwise different ids. Within each aligned group of 64 rows (the query blocks of one dp index) no id stands in more than 8 rows, and some id stands in exactly 8 rows. `positives`: the positive label id of query n lies in a block listed in the beam row of n // 128. `weights`: entries lie within -18 / sqrt(768) to 18 / sqrt(768).
All inputs are finite; a program needn't handle non-finite values.
Results may differ from the reference program's by a relative error of at most 0.013.
Values may be sent and summed in bfloat16 or wider, within the bound.
No kernel may reach another device: no remote copies, remote signals or barrier semaphores. Data moves between devices by JAX's collectives and lax.ppermute only.
A program may use at most 128 MiB of HBM per device.

```python
import math
import jax
import jax.numpy as jnp
from jax import lax

D = 768
LBLK = 4096
QROWS = 128
KMAX = 4
QB_DEV = 2
NBLK = 32
QB = 256
QUERIES = 32768


def make_beams(key):
    groups = QB // (QB_DEV * NBLK)
    sets_count = QB_DEV * KMAX
    hottest = jax.random.randint(jax.random.fold_in(key, 1), (groups,), 0, NBLK, dtype=jnp.int32)
    subkeys = jax.random.split(jax.random.fold_in(key, 2), groups * sets_count)
    orders = jax.vmap(lambda subkey: jax.random.permutation(subkey, NBLK - 1))(subkeys).astype(jnp.int32)
    orders = orders.reshape(groups, sets_count, NBLK - 1)
    hot_wide = hottest[:, None, None]
    mapped = orders + (orders >= hot_wide).astype(jnp.int32)
    leading = jnp.broadcast_to(hot_wide, (groups, sets_count, 1))
    complete = jnp.concatenate([leading, mapped], axis=2)
    candidate = complete.reshape(QB, KMAX)
    counts = jax.random.randint(jax.random.fold_in(key, 3), (QB, 1), KMAX - 1, KMAX + 1, dtype=jnp.int32)
    columns = jnp.arange(KMAX, dtype=jnp.int32)[None, :]
    return jnp.where(columns < counts, candidate, -1).astype(jnp.int32)


def draw_beam(key, part):
    return make_beams(key)


def draw_positives(key, part):
    beams = make_beams(key)
    counts = jnp.sum((beams >= 0).astype(jnp.int32), axis=1)
    choose = jax.random.randint(jax.random.fold_in(key, 5), (QB, QROWS), 0, counts[:, None], dtype=jnp.int32)
    blocks = jnp.take_along_axis(beams, choose, axis=1)
    within = jax.random.randint(jax.random.fold_in(key, 6), (QB, QROWS), 0, LBLK, dtype=jnp.int32)
    return (blocks * LBLK + within).reshape(QUERIES).astype(jnp.int32)


def draw_queries(key, part):
    first = jax.random.fold_in(jax.random.fold_in(key, 21), 0)
    values = jnp.clip(jax.random.normal(first, (QUERIES, D), jnp.float32), -6.0, 6.0)
    return values.astype(jnp.bfloat16)


def draw_weights(key, part):
    first = jax.random.fold_in(jax.random.fold_in(key, 31), 0)
    inverse = 1.0 / math.sqrt(D)
    values = jnp.clip(jax.random.normal(first, (NBLK, LBLK, D), jnp.float32), -6.0, 6.0) * 3.0 * inverse
    return values.astype(jnp.bfloat16)


def setup_inputs(seed: int = 0) -> dict:
    arg_keys = jax.random.split(jax.random.key(seed), 6)
    queries = draw_queries(jax.random.fold_in(arg_keys[5], 71), 0)
    weights = draw_weights(jax.random.fold_in(arg_keys[5], 71), 0)
    beam = draw_beam(jax.random.fold_in(arg_keys[5], 71), 0)
    positives = draw_positives(jax.random.fold_in(arg_keys[5], 71), 0)
    owner = jax.random.permutation(arg_keys[4], NBLK).astype(jnp.int32)
    return {"queries": queries, "weights": weights, "beam": beam, "positives": positives, "owner": owner}


def reference(queries, weights, beam, positives, owner):
    block_total = beam.shape[0]
    block_size = weights.shape[1]
    label_rows = jnp.arange(block_size, dtype=jnp.int32)

    def advance(accum, position):
        block_list = beam[position]
        active = block_list >= 0
        stored = owner[jnp.maximum(block_list, 0)]
        ranker = weights[stored].astype(jnp.float32)
        query_rows = lax.dynamic_slice_in_dim(queries, position * QROWS, QROWS, 0).astype(jnp.float32)
        wanted = lax.dynamic_slice_in_dim(positives, position * QROWS, QROWS, 0)
        scores = jnp.einsum("rd,kld->rkl", query_rows, ranker)
        scores = jnp.where(active[None, :, None], scores, -jnp.inf)
        highest = jnp.max(scores, axis=(1, 2))
        exp_total = jnp.sum(jnp.exp(scores - highest[:, None, None]), axis=(1, 2))
        normal = highest + jnp.log(exp_total)
        target = (block_list[None, :, None] == (wanted // block_size)[:, None, None]) & (label_rows[None, None, :] == (wanted % block_size)[:, None, None]) & active[None, :, None]
        positive = jnp.sum(jnp.where(target, scores, 0.0), axis=(1, 2))
        slope = jnp.where(active[None, :, None], jnp.exp(scores - normal[:, None, None]) - target.astype(jnp.float32), 0.0).astype(jnp.bfloat16)
        slope_wide = slope.astype(jnp.float32)
        partial_bf = lax.optimization_barrier(jnp.einsum("rkl,kld->krd", slope_wide, ranker).astype(jnp.bfloat16))
        grad_rows = jnp.sum(partial_bf.astype(jnp.float32), axis=0)
        grad_table = jnp.einsum("rkl,rd->kld", slope_wide, query_rows)
        accum = accum.at[stored].add(grad_table)
        return accum, (normal - positive, grad_rows)

    start_grads = jnp.zeros(weights.shape, jnp.float32)
    grads, (losses, grad_parts) = lax.scan(advance, start_grads, jnp.arange(block_total, dtype=jnp.int32))
    return losses.reshape(-1), grad_parts.reshape(-1, weights.shape[2]), grads
```

```python
import functools

import jax
import jax.numpy as jnp
from jax import lax
from jax.experimental import pallas as pl
from jax.experimental.pallas import tpu as pltpu
from jax.sharding import PartitionSpec as P

F32 = jnp.float32
BF16 = jnp.bfloat16
NDEV = 32
SLOTS = 8
ROWS = 128
FEAT = 768
HALF = 384
LABELS = 4096
TILE = 512
NEG = -1e30
BIG = 1e30


def iota(shape, dim):
    return lax.broadcasted_iota(jnp.int32, shape, dim)


def dot(a, b, dims):
    return lax.dot_general(a, b, (dims, ((), ())), preferred_element_type=F32)


def ones_where(mask):
    return jnp.where(mask, 1.0, 0.0).astype(BF16)


def slot_table(meta, held):
    n = held.shape[0]
    r = iota((256, 64), 0)
    q = iota((256, 64), 1)
    pick = ones_where((r // 8 == q % 32) & (r % 8 == 6 + q // 32))
    beams = dot(meta, pick, ((0,), (0,)))
    hit = held == beams[0:1, :]
    for k in range(1, 4):
        hit = hit | (held == beams[k : k + 1, :])
    hit = hit & (iota((n, 64), 1) >= 0)
    before = ones_where(iota((64, 64), 0) < iota((64, 64), 1))
    rank = dot(ones_where(hit), before, ((1,), (0,)))
    slot = (iota((n, 64), 0) % SLOTS).astype(F32)
    return jnp.where(hit & (rank == slot), 1.0, 0.0)


def piece_matrix(table):
    e = iota((64, 512), 1)
    spread = ones_where(iota((64, 512), 0) == e // 8)
    wide = dot(table.astype(BF16), spread, ((1,), (0,)))
    full = jnp.broadcast_to(wide[:, None, :], (256, 8, 512))
    same = iota((256, 8, 512), 1) == iota((256, 8, 512), 2) % 8
    return jnp.where(same, full, 0.0).reshape(2048, 512).astype(BF16)


def route_kernel(got_ref, held_ref, out_ref):
    got = got_ref[...]
    table = slot_table(got[:, FEAT:], held_ref[...][:, :1])
    m = piece_matrix(table)
    out = dot(m[:, :256], got[:, :HALF], ((1,), (0,)))
    out += dot(m[:, 256:], got[:, HALF:FEAT], ((1,), (0,)))
    out_ref[...] = out.astype(BF16)


def table_kernel(got_ref, held_ref, mine_ref, sel_ref, mask_ref, col_ref):
    meta = got_ref[...][:, FEAT:]
    table = slot_table(meta, held_ref[...][:, :1])
    sel_ref[...] = piece_matrix(table)
    mine = mine_ref[...]
    own = slot_table(meta, mine[:, 0:1])
    row = iota((16, 64), 0)
    q = iota((16, 64), 1).astype(F32)
    home = jnp.where(q == (row.astype(F32) - 8.0) * 32.0 + mine[:, 1:2], 1.0, 0.0)
    own = jnp.where(row < 8, own, jnp.where(row < 10, home, 0.0)).astype(BF16)
    mask = dot(table.astype(BF16), own, ((1,), (1,)))
    mask_ref[...] = jnp.concatenate([mask, jnp.zeros((256, 112), F32)], axis=1)
    qq = iota((64, 256), 0)
    rr = iota((64, 256), 1)
    part = []
    for c in range(3):
        pick = ones_where((rr // 8 == qq % 32) & (rr % 8 == 3 * (qq // 32) + c))
        where_c = dot(own, pick, ((1,), (0,))).astype(BF16)
        part.append(dot(where_c, meta, ((1,), (0,))))
    inside = part[0] == mine[:, 0:1] + 1.0
    col = jnp.where(inside, part[1] * 64.0 + part[2], -1.0).astype(jnp.int32)
    for s in range(SLOTS):
        col_ref[:, s * ROWS : (s + 1) * ROWS] = jnp.broadcast_to(col[s : s + 1, :], (8, ROWS))


def scores_kernel(q_ref, w_ref, s_ref, lse_ref, top, total):
    step = pl.program_id(0)

    @pl.when(step == 0)
    def _():
        top[...] = jnp.full_like(top, NEG)
        total[...] = jnp.zeros_like(total)

    sub = 256
    for i in range(TILE // sub):
        s = dot(w_ref[i * sub : (i + 1) * sub, :], q_ref[...], ((1,), (1,)))
        s_ref[i * sub : (i + 1) * sub, :] = s
        blocks = s.reshape(sub // 8, 8, s.shape[1])
        old = top[...]
        new = jnp.maximum(old, jnp.max(blocks, axis=0))
        total[...] = total[...] * jnp.exp(old - new) + jnp.sum(jnp.exp(blocks - new[None]), axis=0)
        top[...] = new

    @pl.when(step == pl.num_programs(0) - 1)
    def _():
        m = top[...]
        high = jnp.max(m, axis=0, keepdims=True)
        tot = jnp.sum(total[...] * jnp.exp(m - high), axis=0, keepdims=True)
        lse = high + jnp.log(tot)
        for s in range(SLOTS):
            piece = lse[:, s * ROWS : (s + 1) * ROWS]
            lse_ref[:, s : s + 1, :] = jnp.broadcast_to(piece[None], (NDEV, 1, ROWS))


def normal_kernel(lse_ref, mask_ref, norm_ref, home_ref):
    lse = lse_ref[...]
    mask = mask_ref[...]
    for s in range(SLOTS + 2):
        use = mask[:, s : s + 1] > 0.5
        kept = jnp.where(use, lse, NEG)
        high = jnp.max(kept, axis=0, keepdims=True)
        tot = jnp.sum(jnp.where(use, jnp.exp(kept - high), 0.0), axis=0, keepdims=True)
        value = jnp.where(high > 0.5 * NEG, high + jnp.log(tot), BIG)
        if s < SLOTS:
            norm_ref[:, s * ROWS : (s + 1) * ROWS] = jnp.broadcast_to(value, (8, ROWS))
        else:
            home_ref[s - SLOTS : s - SLOTS + 1, :] = value


def slope_of(s, norm_ref, col_ref, first):
    target = iota(s.shape, 0) + first == col_ref[0:1, :]
    return jnp.exp(s - norm_ref[0:1, :]) - jnp.where(target, 1.0, 0.0), target


def table_grad_kernel(tiles_ref, q_ref, s_ref, norm_ref, col_ref, *out_refs):
    step = pl.program_id(0)
    slope, _ = slope_of(s_ref[...], norm_ref, col_ref, tiles_ref[step] * TILE)
    value = dot(slope.astype(BF16), q_ref[...], ((1,), (0,)))
    for i, ref in enumerate(out_refs):

        @pl.when(step == i)
        def _(ref=ref):
            ref[...] = value.astype(ref.dtype)


def query_grad_kernel(w_ref, s_ref, norm_ref, col_ref, part_ref, pick_ref, acc, pick):
    step = pl.program_id(0)

    @pl.when(step == 0)
    def _():
        acc[...] = jnp.zeros_like(acc)
        pick[...] = jnp.zeros_like(pick)

    s = s_ref[...]
    slope, target = slope_of(s, norm_ref, col_ref, step * TILE)
    found = jnp.where(target, s, 0.0)
    pick[...] += jnp.sum(found.reshape(TILE // 8, 8, s.shape[1]), axis=0)
    acc[...] += dot(slope.astype(BF16), w_ref[...], ((0,), (0,)))

    @pl.when(step == pl.num_programs(0) - 1)
    def _():
        part_ref[...] = acc[...].astype(BF16)
        chosen = jnp.sum(pick[...], axis=0, keepdims=True)
        for s in range(SLOTS):
            piece = chosen[:, s * ROWS : (s + 1) * ROWS]
            pick_ref[:, s : s + 1, :] = jnp.broadcast_to(piece[None], (NDEV, 1, ROWS))


def params(limit=48):
    return pltpu.CompilerParams(vmem_limit_bytes=limit << 20)


def whole(kernel, out_shape, *args):
    return pl.pallas_call(kernel, out_shape=out_shape, compiler_params=params())(*args)


def shape(dims, dtype):
    return jax.ShapeDtypeStruct(dims, dtype)


def fixed(dims):
    return pl.BlockSpec(dims, lambda *_: (0,) * len(dims))


def table_grads(tiles, q, s, norm, col, dtypes):
    n = len(dtypes)
    rows = q.shape[0]
    spec = pltpu.PrefetchScalarGridSpec(
        num_scalar_prefetch=1,
        grid=(n,),
        in_specs=[
            fixed((rows, FEAT)),
            pl.BlockSpec((TILE, rows), lambda i, t: (t[i], 0)),
            fixed((8, rows)),
            fixed((8, rows)),
        ],
        out_specs=[fixed((TILE, FEAT)) for _ in dtypes],
    )
    return pl.pallas_call(
        table_grad_kernel,
        grid_spec=spec,
        out_shape=[shape((TILE, FEAT), d) for d in dtypes],
        compiler_params=params(),
        cost_estimate=pl.CostEstimate(
            flops=2 * n * TILE * rows * FEAT,
            transcendentals=n * TILE * rows,
            bytes_accessed=n * TILE * rows * 4 + rows * FEAT * 2,
        ),
    )(tiles, q, s, norm, col)


def per_device(queries, weights, beam, positives, owner):
    me = lax.axis_index("label")
    y = lax.axis_index("dp")
    rows = SLOTS * ROWS
    ranker = weights[0]

    def swap(x):
        return lax.all_to_all(x, "label", split_axis=0, concat_axis=0, tiled=True)

    ids = jnp.arange(NDEV, dtype=jnp.int32)
    held = jnp.sum(jnp.where(owner[None, :] == ids[:, None], ids[None, :], 0), axis=1).astype(F32)
    held_rows = jnp.broadcast_to(held[:, None, None], (NDEV, SLOTS, 128)).reshape(256, 128)
    my_block = jnp.sum(jnp.where(owner == me, ids, 0)).astype(F32)
    mine = jnp.where(iota((16, 128), 1) == 0, my_block, me.astype(F32))

    low = positives & (LABELS - 1)
    coded = jnp.stack([(positives >> 12) + 1, low >> 6, low & 63], axis=0).reshape(3, 2, ROWS)
    coded = coded.transpose(1, 0, 2).reshape(6, ROWS)
    wide_beam = jnp.pad(beam, ((0, 0), (0, ROWS - beam.shape[1])), constant_values=-1)
    meta = jnp.concatenate([coded, wide_beam], axis=0).astype(BF16)
    pieces = queries.reshape(2, 16, 8, 2, HALF).transpose(1, 3, 2, 0, 4).reshape(NDEV, 8, FEAT)
    pieces = jnp.concatenate([pieces, jnp.broadcast_to(meta[None], (NDEV, 8, ROWS))], axis=2)
    got = swap(pieces).reshape(256, FEAT + ROWS)

    sent = whole(route_kernel, shape((2048, HALF), BF16), got, held_rows)
    arrived = swap(sent.reshape(NDEV, 64, HALF))
    sel, mask, col = whole(
        table_kernel,
        (shape((2048, 512), BF16), shape((256, 128), F32), shape((8, rows), jnp.int32)),
        got,
        held_rows,
        mine,
    )
    q = arrived.reshape(16, 2, SLOTS, 8, HALF).transpose(2, 0, 3, 1, 4).reshape(rows, FEAT)

    steps = LABELS // TILE
    scores, lse = pl.pallas_call(
        scores_kernel,
        grid=(steps,),
        in_specs=[fixed((rows, FEAT)), pl.BlockSpec((TILE, FEAT), lambda i: (i, 0))],
        out_specs=[pl.BlockSpec((TILE, rows), lambda i: (i, 0)), fixed((NDEV, SLOTS, ROWS))],
        out_shape=[shape((LABELS, rows), F32), shape((NDEV, SLOTS, ROWS), F32)],
        scratch_shapes=[pltpu.VMEM((8, rows), F32), pltpu.VMEM((8, rows), F32)],
        compiler_params=params(),
        cost_estimate=pl.CostEstimate(
            flops=2 * LABELS * rows * FEAT,
            transcendentals=LABELS * rows,
            bytes_accessed=LABELS * rows * 4 + LABELS * FEAT * 2,
        ),
    )(q, ranker)
    all_lse = swap(lse).reshape(256, ROWS)
    norm, home_norm = whole(
        normal_kernel, (shape((8, rows), F32), shape((2, ROWS), F32)), all_lse, mask
    )

    up = [(i, (i + 1) % 4) for i in range(4)]
    down = [(i, (i + 3) % 4) for i in range(4)]
    across, ahead, behind = (y + 2) % 4 * 2, (y + 1) % 4 * 2, (y + 3) % 4 * 2
    own = y * 2

    def tiles(*names):
        return jnp.stack(names).astype(jnp.int32)

    far_a, far_b = table_grads(tiles(across, across + 1), q, scores, norm, col, (BF16, BF16))
    via_up = lax.ppermute(far_a, "dp", up)
    via_down = lax.ppermute(far_b, "dp", down)
    next_b, prev_a = table_grads(tiles(ahead + 1, behind), q, scores, norm, col, (BF16, BF16))
    from_prev_b = lax.ppermute(next_b, "dp", up)
    from_next_a = lax.ppermute(prev_a, "dp", down)
    next_a, prev_b, own_a, own_b = table_grads(
        tiles(ahead, behind + 1, own, own + 1), q, scores, norm, col, (F32, F32, F32, F32)
    )
    norm_late, next_a, prev_b, own_a, own_b = lax.optimization_barrier(
        (norm, next_a, prev_b, own_a, own_b)
    )

    part, picked = pl.pallas_call(
        query_grad_kernel,
        grid=(steps,),
        in_specs=[
            pl.BlockSpec((TILE, FEAT), lambda i: (i, 0)),
            pl.BlockSpec((TILE, rows), lambda i: (i, 0)),
            fixed((8, rows)),
            fixed((8, rows)),
        ],
        out_specs=[fixed((rows, FEAT)), fixed((NDEV, SLOTS, ROWS))],
        out_shape=[shape((rows, FEAT), BF16), shape((NDEV, SLOTS, ROWS), F32)],
        scratch_shapes=[pltpu.VMEM((rows, FEAT), F32), pltpu.VMEM((8, rows), F32)],
        compiler_params=params(),
        cost_estimate=pl.CostEstimate(
            flops=2 * LABELS * rows * FEAT,
            transcendentals=LABELS * rows,
            bytes_accessed=LABELS * rows * 4 + LABELS * FEAT * 2,
        ),
    )(ranker, scores, norm_late, col)
    back = part.reshape(SLOTS, 16, 8, 2, HALF).transpose(1, 3, 0, 2, 4).reshape(NDEV, 64, HALF)
    parts = swap(back).reshape(2048, HALF)
    summed = dot(sel, parts, ((0,), (0,))).astype(BF16)
    homeward = summed.reshape(2, NDEV, 8, HALF).transpose(1, 2, 0, 3).reshape(NDEV, 8, FEAT)
    home = swap(homeward).reshape(16, 2, 8, 2, HALF)
    grad_queries = home.transpose(3, 0, 2, 1, 4).reshape(256, FEAT).astype(F32)

    all_picked = swap(picked).reshape(256, ROWS)
    home_mask = mask[:, SLOTS : SLOTS + 2]
    positive = jnp.sum(home_mask[:, :, None] * all_picked[:, None, :], axis=0)
    loss = (home_norm - positive).reshape(-1)

    relay_up = (next_a + via_up.astype(F32)).astype(BF16)
    relay_down = (prev_b + via_down.astype(F32)).astype(BF16)
    from_prev_a = lax.ppermute(relay_up, "dp", up)
    from_next_b = lax.ppermute(relay_down, "dp", down)
    grad_a = own_a + from_prev_a.astype(F32) + from_next_a.astype(F32)
    grad_b = own_b + from_prev_b.astype(F32) + from_next_b.astype(F32)
    grad_table = jnp.concatenate([grad_a, grad_b], axis=0)
    return loss, grad_queries, grad_table[None]


def solution(mesh):
    placed = (
        P(("dp", "label"), None),
        P("label", None, None),
        P(("dp", "label"), None),
        P(("dp", "label")),
        P(),
    )
    return jax.shard_map(
        per_device,
        mesh=mesh,
        in_specs=placed,
        out_specs=(P(("dp", "label")), P(("dp", "label"), None), P("label", "dp", None)),
        check_vma=False,
    )
```

```python
import functools

import jax
import jax.numpy as jnp
from jax import lax
from jax.experimental import pallas as pl
from jax.experimental.pallas import tpu as pltpu
from jax.sharding import PartitionSpec as P

F32 = jnp.float32
BF16 = jnp.bfloat16
NDEV = 32
SLOTS = 8
ROWS = 128
FEAT = 768
HALF = 384
LABELS = 4096
TILE = 512
NEG = -1e30
BIG = 1e30

def iota(shape, dim):
    return lax.broadcasted_iota(jnp.int32, shape, dim)

def dot(a, b, dims):
    return lax.dot_general(a, b, (dims, ((), ())), preferred_element_type=F32)

def ones_where(mask):
    return jnp.where(mask, 1.0, 0.0).astype(BF16)

def slot_table(meta, held):
    n = held.shape[0]
    r = iota((256, 64), 0)
    q = iota((256, 64), 1)
    pick = ones_where((r // 8 == q % 32) & (r % 8 == 6 + q // 32))
    beams = dot(meta, pick, ((0,), (0,)))
    hit = held == beams[0:1, :]
    for k in range(1, 4):
        hit = hit | (held == beams[k : k + 1, :])
    hit = hit & (iota((n, 64), 1) >= 0)
    before = ones_where(iota((64, 64), 0) < iota((64, 64), 1))
    rank = dot(ones_where(hit), before, ((1,), (0,)))
    slot = (iota((n, 64), 0) % SLOTS).astype(F32)
    return jnp.where(hit & (rank == slot), 1.0, 0.0)

def piece_matrix(table):
    e = iota((64, 512), 1)
    spread = ones_where(iota((64, 512), 0) == e // 8)
    wide = dot(table.astype(BF16), spread, ((1,), (0,)))
    full = jnp.broadcast_to(wide[:, None, :], (256, 8, 512))
    same = iota((256, 8, 512), 1) == iota((256, 8, 512), 2) % 8
    return jnp.where(same, full, 0.0).reshape(2048, 512).astype(BF16)

def route_kernel(got_ref, held_ref, out_ref):
    got = got_ref[...]
    table = slot_table(got[:, FEAT:], held_ref[...][:, :1])
    m = piece_matrix(table)
    out = dot(m[:, :256], got[:, :HALF], ((1,), (0,)))
    out += dot(m[:, 256:], got[:, HALF:FEAT], ((1,), (0,)))
    out_ref[...] = out.astype(BF16)

def table_kernel(got_ref, held_ref, mine_ref, sel_ref, mask_ref, col_ref, slots_ref):
    meta = got_ref[...][:, FEAT:]
    table = slot_table(meta, held_ref[...][:, :1])
    sel_ref[...] = piece_matrix(table).T
    mine = mine_ref[...]
    own = slot_table(meta, mine[:, 0:1])
    row = iota((16, 64), 0)
    q = iota((16, 64), 1).astype(F32)
    home = jnp.where(q == (row.astype(F32) - 8.0) * 32.0 + mine[:, 1:2], 1.0, 0.0)
    own = jnp.where(row < 8, own, jnp.where(row < 10, home, 0.0)).astype(BF16)
    mask = dot(table.astype(BF16), own, ((1,), (1,)))
    mask_ref[...] = jnp.concatenate([mask, jnp.zeros((256, 112), F32)], axis=1)
    qq = iota((64, 256), 0)
    rr = iota((64, 256), 1)
    part = []
    for c in range(3):
        pick = ones_where((rr // 8 == qq % 32) & (rr % 8 == 3 * (qq // 32) + c))
        where_c = dot(own, pick, ((1,), (0,))).astype(BF16)
        part.append(dot(where_c, meta, ((1,), (0,))))
    inside = part[0] == mine[:, 0:1] + 1.0
    col = jnp.where(inside, part[1] * 64.0 + part[2], -1.0)
    slots_ref[...] = col[:SLOTS]
    for s in range(SLOTS):
        piece = col[s : s + 1].astype(jnp.int32)
        col_ref[:, s * ROWS : (s + 1) * ROWS] = jnp.broadcast_to(piece, (8, ROWS))

def start(copies):
    for c in copies:
        c.start()
    return copies

def pieces_kernel(q_hbm, pos_hbm, beam_hbm, out_ref, q_ref, pos_ref, beam_ref, sems):
    small = start(
        [
            pltpu.make_async_copy(pos_hbm, pos_ref, sems.at[0]),
            pltpu.make_async_copy(beam_hbm, beam_ref, sems.at[1]),
        ]
    )
    large = start(
        [
            pltpu.make_async_copy(q_hbm.at[:, pl.ds(8 * i, 8)], q_ref.at[:, pl.ds(8 * i, 8)], sems.at[2 + i])
            for i in range(2)
        ]
    )
    for c in small:
        c.wait()
    pos = pos_ref[...]
    beam = beam_ref[...]
    high, low = (pos >> 12) + 1, pos & (LABELS - 1)
    codes = (high, low >> 6, low & 63)
    row = iota((8, ROWS), 0)
    lane = iota((8, ROWS), 1)
    meta = jnp.full((8, ROWS), -1, jnp.int32)
    for b in range(2):
        for c in range(3):
            meta = jnp.where(row == 3 * b + c, codes[c][b : b + 1, :], meta)
        for k in range(beam.shape[1]):
            meta = jnp.where((row == 6 + b) & (lane == k), beam[b : b + 1, k : k + 1], meta)
    meta = meta.astype(F32).astype(BF16)
    out_ref[:, :, :, FEAT:] = jnp.broadcast_to(meta[None, None], (16, 2, 8, ROWS))
    for i in range(2):
        large[i].wait()
        g = slice(8 * i, 8 * i + 8)
        for h in range(2):
            for b in range(2):
                out_ref[g, h, :, b * HALF : (b + 1) * HALF] = q_ref[b, g, :, h * HALF : (h + 1) * HALF]

def by_slot(lanes):
    row = iota((SLOTS, ROWS), 0)
    out = jnp.zeros((SLOTS, ROWS), F32)
    for s in range(SLOTS):
        out = jnp.where(row == s, lanes[:, s * ROWS : (s + 1) * ROWS], out)
    return out

def rows_in(src, dst, sems, tile, first=0):
    return [
        pltpu.make_async_copy(
            src.at[pl.ds(first + i * tile, tile)], dst.at[pl.ds(i * tile, tile)], sems.at[i]
        )
        for i in range(dst.shape[0] // tile)
    ]

def scores_kernel(got_ref, col_ref, w_hbm, s_hbm, q_hbm, stat_ref, row_ref, w_ref, s_ref, q_ref, w_sems, s_sems, q_sem):
    tile = 256
    n = LABELS // tile
    w_in = start(rows_in(w_hbm, w_ref, w_sems, tile))
    for g in range(16):
        for h in range(2):
            q_ref[:, g, :, h * HALF : (h + 1) * HALF] = got_ref[g, h]
    q_out = pltpu.make_async_copy(q_ref, q_hbm, q_sem)
    q_out.start()
    rows = s_ref.shape[1]
    q = q_ref[...].reshape(rows, FEAT)
    top = jnp.full((8, rows), NEG, F32)
    total = jnp.zeros((8, rows), F32)
    found = jnp.zeros((8, rows), F32)
    s_out = [
        pltpu.make_async_copy(s_ref.at[pl.ds(i * tile, tile)], s_hbm.at[pl.ds(i * tile, tile)], s_sems.at[i])
        for i in range(n)
    ]
    for i in range(n + 1):
        if i < n:
            w_in[i].wait()
            s_ref[i * tile : (i + 1) * tile, :] = dot(w_ref[i * tile : (i + 1) * tile, :], q, ((1,), (1,)))
            s_out[i].start()
        if i > 0:
            s = s_ref[(i - 1) * tile : i * tile, :]
            target = iota(s.shape, 0) + (i - 1) * tile == col_ref[0:1, :]
            found += jnp.sum(jnp.where(target, s, 0.0).reshape(tile // 8, 8, rows), axis=0)
            s = s.reshape(tile // 8, 8, rows)
            new = jnp.maximum(top, jnp.max(s, axis=0))
            total = total * jnp.exp(top - new) + jnp.sum(jnp.exp(s - new[None]), axis=0)
            top = new
    high = jnp.max(top, axis=0, keepdims=True)
    lse = high + jnp.log(jnp.sum(total * jnp.exp(top - high), axis=0, keepdims=True))
    row_ref[...] = jnp.broadcast_to(lse, (8, rows))
    chosen = jnp.sum(found, axis=0, keepdims=True)
    stat_ref[:, :SLOTS, :] = jnp.broadcast_to(by_slot(lse)[None], (NDEV, SLOTS, ROWS))
    stat_ref[:, SLOTS:, :] = jnp.broadcast_to(by_slot(chosen)[None], (NDEV, SLOTS, ROWS))
    q_out.wait()
    for c in s_out:
        c.wait()

def normal_kernel(stat_ref, mask_ref, norm_ref, slots_ref, loss_ref):
    lse = stat_ref[:, :SLOTS, :].reshape(NDEV * SLOTS, ROWS)
    found = stat_ref[:, SLOTS:, :].reshape(NDEV * SLOTS, ROWS)
    mask = mask_ref[...]
    for s in range(SLOTS + 2):
        use = mask[:, s : s + 1] > 0.5
        kept = jnp.where(use, lse, NEG)
        high = jnp.max(kept, axis=0, keepdims=True)
        tot = jnp.sum(jnp.where(use, jnp.exp(kept - high), 0.0), axis=0, keepdims=True)
        value = jnp.where(high > 0.5 * NEG, high + jnp.log(tot), BIG)
        if s < SLOTS:
            norm_ref[:, s * ROWS : (s + 1) * ROWS] = jnp.broadcast_to(value, (8, ROWS))
            slots_ref[s : s + 1, :] = value
        else:
            positive = jnp.sum(jnp.where(use, found, 0.0), axis=0, keepdims=True)
            loss_ref[s - SLOTS : s - SLOTS + 1, :] = value - positive

def rows_out(acc, out_v, out_hbm, sems):
    copies = []
    for s in range(SLOTS):
        here = pl.ds(s * ROWS, ROWS)
        out_v[s * ROWS : (s + 1) * ROWS, :] = acc[:, s * ROWS : (s + 1) * ROWS].T.astype(out_v.dtype)
        c = pltpu.make_async_copy(out_v.at[here], out_hbm.at[here], sems.at[s])
        c.start()
        copies.append(c)
    for c in copies:
        c.wait()

def positive_kernel(w_hbm, col_ref, out_hbm, w_ref, acc, out_v, w_sems, out_sems):
    rows = col_ref.shape[1]
    tile = 512
    w_in = start(rows_in(w_hbm, w_ref, w_sems, tile))
    for i in range(LABELS // tile):
        target = iota((tile, rows), 0) + i * tile == col_ref[0:1, :]
        w_in[i].wait()
        term = dot(w_ref[i * tile : (i + 1) * tile, :], ones_where(target), ((0,), (0,)))
        if i == 0:
            acc[...] = term
        else:
            acc[...] += term
    rows_out(acc, out_v, out_hbm, out_sems)

def others_kernel(w_hbm, s_hbm, row_ref, col_ref, out_hbm, w_ref, s_ref, acc, out_v, w_sems, s_sems, out_sems):
    rows = s_ref.shape[1]
    tile = 512
    s_in = rows_in(s_hbm, s_ref, s_sems, tile)
    w_in = rows_in(w_hbm, w_ref, w_sems, tile)
    for a, b in zip(s_in, w_in):
        a.start()
        b.start()
    for i in range(LABELS // tile):
        s_in[i].wait()
        s = s_ref[i * tile : (i + 1) * tile, :]
        target = iota((tile, rows), 0) + i * tile == col_ref[0:1, :]
        p = jnp.where(target, 0.0, jnp.exp(s - row_ref[0:1, :])).astype(BF16)
        w_in[i].wait()
        term = dot(w_ref[i * tile : (i + 1) * tile, :], p, ((0,), (0,)))
        if i == 0:
            acc[...] = term
        else:
            acc[...] += term
    rows_out(acc, out_v, out_hbm, out_sems)

def part_kernel(u_hbm, r_hbm, stat_ref, norm_ref, col_ref, out_ref, u_ref, r_ref, u_sems, r_sems):
    u_in = rows_in(u_hbm, u_ref, u_sems, ROWS)
    r_in = rows_in(r_hbm, r_ref, r_sems, ROWS)
    for a, b in zip(u_in, r_in):
        a.start()
        b.start()
    norm = norm_ref[...]
    scale = jnp.exp(stat_ref[0, :SLOTS, :] - norm).T
    rest = jnp.where(col_ref[...] >= 0.0, jnp.exp(stat_ref[0, SLOTS:, :] - norm) - 1.0, 0.0).T
    for s in range(SLOTS):
        u_in[s].wait()
        r_in[s].wait()
        u = u_ref[s * ROWS : (s + 1) * ROWS, :]
        r = r_ref[s * ROWS : (s + 1) * ROWS, :].astype(F32)
        part = (scale[:, s : s + 1] * u + rest[:, s : s + 1] * r).astype(BF16).reshape(16, 8, FEAT)
        for h in range(2):
            out_ref[:, h, s * 8 : (s + 1) * 8, :] = part[:, :, h * HALF : (h + 1) * HALF]

def table_grad_kernel(n, tiles_ref, q_hbm, s_hbm, norm_ref, col_ref, *refs):
    outs, (q_ref, s_ref, out_v, q_sem, s_sems, out_sems) = refs[:n], refs[n:]
    tile = 256
    per = TILE // tile
    s_in = []
    for i in range(n):
        for k in range(per):
            first = pl.multiple_of(tiles_ref[i] * TILE + k * tile, tile)
            j = i * per + k
            s_in.append(
                pltpu.make_async_copy(s_hbm.at[pl.ds(first, tile)], s_ref.at[pl.ds(j * tile, tile)], s_sems.at[j])
            )
    s_in[0].start()
    q_in = pltpu.make_async_copy(q_hbm, q_ref, q_sem)
    q_in.start()
    start(s_in[1:])
    out = []
    for i in range(n):
        for k in range(per):
            j = i * per + k
            s_in[j].wait()
            s = s_ref[j * tile : (j + 1) * tile, :]
            target = iota(s.shape, 0) + (tiles_ref[i] * TILE + k * tile) == col_ref[0:1, :]
            slope = jnp.exp(s - norm_ref[0:1, :]) - jnp.where(target, 1.0, 0.0)
            if j == 0:
                q_in.wait()
            value = dot(slope.astype(BF16), q_ref[...], ((1,), (0,)))
            out_v[j * tile : (j + 1) * tile, :] = value.astype(out_v.dtype)
            c = pltpu.make_async_copy(
                out_v.at[pl.ds(j * tile, tile)], outs[i].at[pl.ds(k * tile, tile)], out_sems.at[j]
            )
            c.start()
            out.append(c)
    for c in out:
        c.wait()

def sum_kernel(sel_ref, parts_ref, out_ref):
    out = dot(sel_ref[...], parts_ref[...], ((1,), (0,))).astype(BF16)
    for b in range(2):
        out_ref[:, :, b * HALF : (b + 1) * HALF] = out[b * 256 : (b + 1) * 256].reshape(NDEV, 8, HALF)

def home_kernel(got_ref, out_ref):
    for h in range(2):
        for b in range(2):
            out_ref[b, :, :, h * HALF : (h + 1) * HALF] = got_ref[:, h, :, b * HALF : (b + 1) * HALF].astype(F32)

def finish_kernel(base_ref, a_hbm, b_hbm, out_hbm, got, out_v, in_sems, out_sems):
    tile = 256
    per = TILE // tile
    copies = [
        pltpu.make_async_copy(src.at[pl.ds(k * tile, tile)], got.at[pl.ds((i * per + k) * tile, tile)], in_sems.at[i * per + k])
        for i, src in enumerate((a_hbm, b_hbm))
        for k in range(per)
    ]
    start(copies)
    out = []
    for j in range(2 * per):
        here = pl.ds(j * tile, tile)
        copies[j].wait()
        out_v[j * tile : (j + 1) * tile, :] = base_ref[j * tile : (j + 1) * tile, :] + got[j * tile : (j + 1) * tile, :].astype(F32)
        c = pltpu.make_async_copy(out_v.at[here], out_hbm.at[here], out_sems.at[j])
        c.start()
        out.append(c)
    for c in out:
        c.wait()

def shape(dims, dtype):
    return jax.ShapeDtypeStruct(dims, dtype)

def whole(kernel, out, *args, hbm=(), smem=(), hbm_out=(), limit=60, scratch=()):
    def place(i, far, scalar=()):
        space = pltpu.HBM if i in far else pltpu.SMEM if i in scalar else pltpu.VMEM
        return pl.BlockSpec(memory_space=space)

    single = not isinstance(out, tuple)
    outs = (out,) if single else out
    results = pl.pallas_call(
        kernel,
        out_shape=outs,
        in_specs=[place(i, hbm, smem) for i in range(len(args))],
        out_specs=tuple(place(i, hbm_out) for i in range(len(outs))),
        scratch_shapes=list(scratch),
        compiler_params=pltpu.CompilerParams(vmem_limit_bytes=limit << 20),
        cost_estimate=pl.CostEstimate(flops=1024, transcendentals=0, bytes_accessed=1024),
    )(*args)
    return results[0] if single else results

def sems(n):
    return pltpu.SemaphoreType.DMA((n,))

def per_device(queries, weights, beam, positives, owner):
    me = lax.axis_index("label")
    y = lax.axis_index("dp")
    rows = SLOTS * ROWS
    ranker = weights[0]

    def swap(x):
        return lax.all_to_all(x, "label", split_axis=0, concat_axis=0, tiled=True)

    ids = jnp.arange(NDEV, dtype=jnp.int32)
    held = jnp.sum(jnp.where(owner[None, :] == ids[:, None], ids[None, :], 0), axis=1).astype(F32)
    held_rows = jnp.broadcast_to(held[:, None, None], (NDEV, SLOTS, 128)).reshape(256, 128)
    my_block = jnp.sum(jnp.where(owner == me, ids, 0)).astype(F32)
    mine = jnp.where(iota((16, 128), 1) == 0, my_block, me.astype(F32))

    pieces = whole(
        pieces_kernel,
        shape((16, 2, 8, FEAT + ROWS), BF16),
        queries.reshape(2, 16, 8, FEAT),
        positives.reshape(2, ROWS),
        beam,
        hbm=(0, 1, 2),
        scratch=(
            pltpu.VMEM((2, 16, 8, FEAT), BF16),
            pltpu.VMEM((2, ROWS), jnp.int32),
            pltpu.VMEM(beam.shape, jnp.int32),
            sems(4),
        ),
    )
    got = swap(pieces.reshape(NDEV, 8, FEAT + ROWS)).reshape(256, FEAT + ROWS)

    sent = whole(route_kernel, shape((2048, HALF), BF16), got, held_rows, limit=16)
    arrived = swap(sent.reshape(NDEV, 64, HALF))
    sel, mask, col, col_slots = whole(
        table_kernel,
        (
            shape((512, 2048), BF16),
            shape((256, 128), F32),
            shape((8, rows), jnp.int32),
            shape((SLOTS, ROWS), F32),
        ),
        got,
        held_rows,
        mine,
    )
    positive_rows = whole(
        positive_kernel,
        shape((rows, FEAT), BF16),
        ranker,
        col,
        hbm=(0,),
        hbm_out=(0,),
        scratch=(
            pltpu.VMEM((LABELS, FEAT), BF16),
            pltpu.VMEM((FEAT, rows), F32),
            pltpu.VMEM((rows, FEAT), BF16),
            sems(8),
            sems(8),
        ),
    )
    arrived, positive_rows, col = lax.optimization_barrier((arrived, positive_rows, col))

    scores, q, stats, lse_row = whole(
        scores_kernel,
        (
            shape((LABELS, rows), F32),
            shape((SLOTS, 16, 8, FEAT), BF16),
            shape((NDEV, 2 * SLOTS, ROWS), F32),
            shape((8, rows), F32),
        ),
        arrived.reshape(16, 2, SLOTS, 8, HALF),
        col,
        ranker,
        limit=59,
        hbm=(2,),
        hbm_out=(0, 1),

        scratch=(
            pltpu.VMEM((LABELS, FEAT), BF16),
            pltpu.VMEM((LABELS, rows), F32),
            pltpu.VMEM((SLOTS, 16, 8, FEAT), BF16),
            sems(16),
            sems(16),
            pltpu.SemaphoreType.DMA,
        ),
    )
    q = q.reshape(rows, FEAT)
    all_stats = swap(stats)
    others = whole(
        others_kernel,
        shape((rows, FEAT), F32),
        ranker,
        scores,
        lse_row,
        col,
        hbm=(0, 1),
        hbm_out=(0,),

        scratch=(
            pltpu.VMEM((LABELS, FEAT), BF16),
            pltpu.VMEM((LABELS, rows), F32),
            pltpu.VMEM((FEAT, rows), F32),
            pltpu.VMEM((rows, FEAT), F32),
            sems(8),
            sems(8),
            sems(8),
        ),
    )
    all_stats, others = lax.optimization_barrier((all_stats, others))
    norm, norm_slots, loss = whole(
        normal_kernel,
        (shape((8, rows), F32), shape((SLOTS, ROWS), F32), shape((2, ROWS), F32)),
        all_stats,
        mask,
        limit=16,
    )

    up = [(i, (i + 1) % 4) for i in range(4)]
    down = [(i, (i + 3) % 4) for i in range(4)]
    across, ahead, behind = (y + 2) % 4 * 2, (y + 1) % 4 * 2, (y + 3) % 4 * 2
    tiles = jnp.stack([across, across + 1, ahead + 1, behind, ahead, behind + 1, y * 2, y * 2 + 1])
    tiles = tiles.astype(jnp.int32)

    def table_grads(first, norm, dtypes):
        n = len(dtypes)
        return whole(
            functools.partial(table_grad_kernel, n),
            tuple(shape((TILE, FEAT), d) for d in dtypes),
            tiles[first : first + n],
            q,
            scores,
            norm,
            col,
            smem=(0,),
            hbm=(1, 2),
            hbm_out=tuple(range(n)),

            scratch=(
                pltpu.VMEM((rows, FEAT), BF16),
                pltpu.VMEM((n * TILE, rows), F32),
                pltpu.VMEM((n * TILE, FEAT), dtypes[0]),
                pltpu.SemaphoreType.DMA,
                sems(2 * n),
                sems(2 * n),
            ),
        )

    far_a, far_b = table_grads(0, norm, (BF16, BF16))
    far_a, far_b, norm_slots, norm = lax.optimization_barrier((far_a, far_b, norm_slots, norm))
    via_up = lax.ppermute(far_a, "dp", up)
    via_down = lax.ppermute(far_b, "dp", down)
    part = whole(
        part_kernel,
        shape((16, 2, 64, HALF), BF16),
        others,
        positive_rows,
        stats,
        norm_slots,
        col_slots,
        hbm=(0, 1),
        scratch=(
            pltpu.VMEM((rows, FEAT), F32),
            pltpu.VMEM((rows, FEAT), BF16),
            sems(8),
            sems(8),
        ),
    )
    part, norm = lax.optimization_barrier((part, norm))
    parts = swap(part.reshape(NDEV, 64, HALF)).reshape(2048, HALF)
    next_b, prev_a = table_grads(2, norm, (BF16, BF16))
    next_b, prev_a, norm = lax.optimization_barrier((next_b, prev_a, norm))
    from_prev_b = lax.ppermute(next_b, "dp", up)
    from_next_a = lax.ppermute(prev_a, "dp", down)
    next_a, prev_b, own_a, own_b = table_grads(4, norm, (F32, F32, F32, F32))

    relay_up = (next_a + via_up.astype(F32)).astype(BF16)
    relay_down = (prev_b + via_down.astype(F32)).astype(BF16)
    from_prev_a = lax.ppermute(relay_up, "dp", up)
    from_next_b = lax.ppermute(relay_down, "dp", down)

    homeward = whole(sum_kernel, shape((NDEV, 8, FEAT), BF16), sel, parts, limit=16)
    home = swap(homeward).reshape(16, 2, 8, FEAT)
    grad_queries = whole(home_kernel, shape((2, 16, 8, FEAT), F32), home, limit=16).reshape(256, FEAT)
    base = jnp.concatenate(
        [own_a + from_next_a.astype(F32), own_b + from_prev_b.astype(F32)], axis=0
    )
    grad_table = whole(
        finish_kernel,
        shape((2 * TILE, FEAT), F32),
        base,
        from_prev_a,
        from_next_b,
        hbm=(1, 2),
        hbm_out=(0,),
        scratch=(
            pltpu.VMEM((2 * TILE, FEAT), BF16),
            pltpu.VMEM((2 * TILE, FEAT), F32),
            sems(4),
            sems(4),
        ),
    )
    return loss.reshape(256), grad_queries, grad_table[None]

def solution(mesh):
    placed = (
        P(("dp", "label"), None),
        P("label", None, None),
        P(("dp", "label"), None),
        P(("dp", "label")),
        P(),
    )
    return jax.shard_map(
        per_device,
        mesh=mesh,
        in_specs=placed,
        out_specs=(P(("dp", "label")), P(("dp", "label"), None), P("label", "dp", None)),
        check_vma=False,
    )
```

```python
import functools

import jax
import jax.numpy as jnp
from jax import lax
from jax.experimental import pallas as pl
from jax.experimental.pallas import tpu as pltpu
from jax.sharding import PartitionSpec as P

F32 = jnp.float32
BF16 = jnp.bfloat16
NDEV = 32
SLOTS = 8
ROWS = 128
FEAT = 768
HALF = 384
LABELS = 4096
TILE = 512
NEG = -1e30
BIG = 1e30

def iota(shape, dim):
    return lax.broadcasted_iota(jnp.int32, shape, dim)

def dot(a, b, dims):
    return lax.dot_general(a, b, (dims, ((), ())), preferred_element_type=F32)

def ones_where(mask):
    return jnp.where(mask, 1.0, 0.0).astype(BF16)

def slot_table(meta, held):
    n = held.shape[0]
    r = iota((256, 64), 0)
    q = iota((256, 64), 1)
    pick = ones_where((r // 8 == q % 32) & (r % 8 == 6 + q // 32))
    beams = dot(meta, pick, ((0,), (0,)))
    hit = held == beams[0:1, :]
    for k in range(1, 4):
        hit = hit | (held == beams[k : k + 1, :])
    hit = hit & (iota((n, 64), 1) >= 0)
    before = ones_where(iota((64, 64), 0) < iota((64, 64), 1))
    rank = dot(ones_where(hit), before, ((1,), (0,)))
    slot = (iota((n, 64), 0) % SLOTS).astype(F32)
    return jnp.where(hit & (rank == slot), 1.0, 0.0)

def piece_matrix(table):
    e = iota((64, 512), 1)
    spread = ones_where(iota((64, 512), 0) == e // 8)
    wide = dot(table.astype(BF16), spread, ((1,), (0,)))
    full = jnp.broadcast_to(wide[:, None, :], (256, 8, 512))
    same = iota((256, 8, 512), 1) == iota((256, 8, 512), 2) % 8
    return jnp.where(same, full, 0.0).reshape(2048, 512).astype(BF16)

def route_kernel(got_ref, held_ref, out_ref):
    got = got_ref[...]
    table = slot_table(got[:, FEAT:], held_ref[...][:, :1])
    m = piece_matrix(table)
    out = dot(m[:, :256], got[:, :HALF], ((1,), (0,)))
    out += dot(m[:, 256:], got[:, HALF:FEAT], ((1,), (0,)))
    out_ref[...] = out.astype(BF16)

def table_kernel(got_ref, held_ref, mine_ref, sel_ref, mask_ref, col_ref, slots_ref):
    meta = got_ref[...][:, FEAT:]
    table = slot_table(meta, held_ref[...][:, :1])
    sel_ref[...] = piece_matrix(table).T
    mine = mine_ref[...]
    own = slot_table(meta, mine[:, 0:1])
    row = iota((16, 64), 0)
    q = iota((16, 64), 1).astype(F32)
    home = jnp.where(q == (row.astype(F32) - 8.0) * 32.0 + mine[:, 1:2], 1.0, 0.0)
    own = jnp.where(row < 8, own, jnp.where(row < 10, home, 0.0)).astype(BF16)
    mask = dot(table.astype(BF16), own, ((1,), (1,)))
    mask_ref[...] = jnp.concatenate([mask, jnp.zeros((256, 112), F32)], axis=1)
    qq = iota((64, 256), 0)
    rr = iota((64, 256), 1)
    part = []
    for c in range(3):
        pick = ones_where((rr // 8 == qq % 32) & (rr % 8 == 3 * (qq // 32) + c))
        where_c = dot(own, pick, ((1,), (0,))).astype(BF16)
        part.append(dot(where_c, meta, ((1,), (0,))))
    inside = part[0] == mine[:, 0:1] + 1.0
    col = jnp.where(inside, part[1] * 64.0 + part[2], -1.0)
    slots_ref[...] = col[:SLOTS]
    for s in range(SLOTS):
        piece = col[s : s + 1].astype(jnp.int32)
        col_ref[:, s * ROWS : (s + 1) * ROWS] = jnp.broadcast_to(piece, (8, ROWS))

def start(copies):
    for c in copies:
        c.start()
    return copies

def pieces_kernel(q_hbm, pos_hbm, beam_hbm, out_ref, q_ref, pos_ref, beam_ref, sems):
    small = start(
        [
            pltpu.make_async_copy(pos_hbm, pos_ref, sems.at[0]),
            pltpu.make_async_copy(beam_hbm, beam_ref, sems.at[1]),
        ]
    )
    large = start(
        [
            pltpu.make_async_copy(q_hbm.at[:, pl.ds(8 * i, 8)], q_ref.at[:, pl.ds(8 * i, 8)], sems.at[2 + i])
            for i in range(2)
        ]
    )
    for c in small:
        c.wait()
    pos = pos_ref[...]
    beam = beam_ref[...]
    high, low = (pos >> 12) + 1, pos & (LABELS - 1)
    codes = (high, low >> 6, low & 63)
    row = iota((8, ROWS), 0)
    lane = iota((8, ROWS), 1)
    meta = jnp.full((8, ROWS), -1, jnp.int32)
    for b in range(2):
        for c in range(3):
            meta = jnp.where(row == 3 * b + c, codes[c][b : b + 1, :], meta)
        for k in range(beam.shape[1]):
            meta = jnp.where((row == 6 + b) & (lane == k), beam[b : b + 1, k : k + 1], meta)
    meta = meta.astype(F32).astype(BF16)
    out_ref[:, :, :, FEAT:] = jnp.broadcast_to(meta[None, None], (16, 2, 8, ROWS))
    for i in range(2):
        large[i].wait()
        g = slice(8 * i, 8 * i + 8)
        for h in range(2):
            for b in range(2):
                out_ref[g, h, :, b * HALF : (b + 1) * HALF] = q_ref[b, g, :, h * HALF : (h + 1) * HALF]

def by_slot(lanes):
    row = iota((SLOTS, ROWS), 0)
    out = jnp.zeros((SLOTS, ROWS), F32)
    for s in range(SLOTS):
        out = jnp.where(row == s, lanes[:, s * ROWS : (s + 1) * ROWS], out)
    return out

def rows_in(src, dst, sems, tile, first=0):
    return [
        pltpu.make_async_copy(
            src.at[pl.ds(first + i * tile, tile)], dst.at[pl.ds(i * tile, tile)], sems.at[i]
        )
        for i in range(dst.shape[0] // tile)
    ]

def scores_kernel(got_ref, col_ref, w_hbm, s_hbm, q_hbm, stat_ref, row_ref, w_ref, s_ref, q_ref, w_sems, s_sems, q_sem):
    big, tile = 1024, 256
    n = LABELS // big
    w_in = start(rows_in(w_hbm, w_ref, w_sems, big))
    for g in range(16):
        for h in range(2):
            q_ref[:, g, :, h * HALF : (h + 1) * HALF] = got_ref[g, h]
    q_out = pltpu.make_async_copy(q_ref, q_hbm, q_sem)
    q_out.start()
    rows = s_ref.shape[1]
    q = q_ref[...].reshape(rows, FEAT)
    top = jnp.full((8, rows), NEG, F32)
    total = jnp.zeros((8, rows), F32)
    found = jnp.zeros((8, rows), F32)
    s_out = [
        pltpu.make_async_copy(s_ref.at[pl.ds(i * big, big)], s_hbm.at[pl.ds(i * big, big)], s_sems.at[i])
        for i in range(n)
    ]
    for i in range(n + 1):
        if i < n:
            w_in[i].wait()
        for k in range(big // tile):
            if i < n:
                first = i * big + k * tile
                s_ref[first : first + tile, :] = dot(w_ref[first : first + tile, :], q, ((1,), (1,)))
            if i > 0:
                first = (i - 1) * big + k * tile
                s = s_ref[first : first + tile, :]
                target = iota(s.shape, 0) + first == col_ref[0:1, :]
                found += jnp.sum(jnp.where(target, s, 0.0).reshape(tile // 8, 8, rows), axis=0)
                s = s.reshape(tile // 8, 8, rows)
                new = jnp.maximum(top, jnp.max(s, axis=0))
                total = total * jnp.exp(top - new) + jnp.sum(jnp.exp(s - new[None]), axis=0)
                top = new
        if i < n:
            s_out[i].start()
    high = jnp.max(top, axis=0, keepdims=True)
    lse = high + jnp.log(jnp.sum(total * jnp.exp(top - high), axis=0, keepdims=True))
    row_ref[...] = jnp.broadcast_to(lse, (8, rows))
    chosen = jnp.sum(found, axis=0, keepdims=True)
    stat_ref[:, :SLOTS, :] = jnp.broadcast_to(by_slot(lse)[None], (NDEV, SLOTS, ROWS))
    stat_ref[:, SLOTS:, :] = jnp.broadcast_to(by_slot(chosen)[None], (NDEV, SLOTS, ROWS))
    q_out.wait()
    for c in s_out:
        c.wait()


def normal_kernel(stat_ref, mask_ref, row_ref, scale_ref, rest_ref, slots_ref, loss_ref):
    lse = stat_ref[:, :SLOTS, :].reshape(NDEV * SLOTS, ROWS)
    found = stat_ref[:, SLOTS:, :].reshape(NDEV * SLOTS, ROWS)
    mask = mask_ref[...]
    for s in range(SLOTS + 2):
        use = mask[:, s : s + 1] > 0.5
        kept = jnp.where(use, lse, NEG)
        high = jnp.max(kept, axis=0, keepdims=True)
        tot = jnp.sum(jnp.where(use, jnp.exp(kept - high), 0.0), axis=0, keepdims=True)
        value = jnp.where(high > 0.5 * NEG, high + jnp.log(tot), BIG)
        if s < SLOTS:
            here = slice(s * ROWS, (s + 1) * ROWS)
            scale_ref[:, here] = jnp.exp(row_ref[:, here] - value)
            positive = jnp.sum(jnp.where(use, found, 0.0), axis=0, keepdims=True)
            rest_ref[:, here] = jnp.broadcast_to(jnp.exp(positive - value) - 1.0, (8, ROWS))
            slots_ref[s : s + 1, :] = value
        else:
            positive = jnp.sum(jnp.where(use, found, 0.0), axis=0, keepdims=True)
            loss_ref[s - SLOTS : s - SLOTS + 1, :] = value - positive


def rows_out(acc, out_v, out_hbm, sem):
    for s in range(SLOTS):
        out_v[s * ROWS : (s + 1) * ROWS, :] = acc[:, s * ROWS : (s + 1) * ROWS].T.astype(out_v.dtype)
    c = pltpu.make_async_copy(out_v, out_hbm, sem)
    c.start()
    c.wait()


def positive_kernel(w_hbm, col_ref, out_hbm, w_ref, acc, out_v, w_sems, out_sem):
    rows = col_ref.shape[1]
    tile = 1024
    w_in = start(rows_in(w_hbm, w_ref, w_sems, tile))
    for i in range(LABELS // tile):
        w_in[i].wait()
        target = iota((tile, rows), 0) + i * tile == col_ref[0:1, :]
        term = dot(w_ref[i * tile : (i + 1) * tile, :], ones_where(target), ((0,), (0,)))
        if i == 0:
            acc[...] = term
        else:
            acc[...] += term
    rows_out(acc, out_v, out_hbm, out_sem)


def others_kernel(w_hbm, s_hbm, row_ref, col_ref, out_hbm, p_hbm, w_ref, s_ref, p_ref, acc, out_v, w_sems, s_sems, p_sems, out_sem):
    rows = s_ref.shape[1]
    tile = 512
    n = LABELS // tile
    s_in = rows_in(s_hbm, s_ref, s_sems, tile)
    w_in = rows_in(w_hbm, w_ref, w_sems, tile)
    for a, b in zip(s_in, w_in):
        a.start()
        b.start()
    edges = [0, 1, 2, 4, 6, 8]
    p_out = []
    for e in range(len(edges)):
        if e < len(edges) - 1:
            for i in range(edges[e], edges[e + 1]):
                s_in[i].wait()
                w_in[i].wait()
            a, b = edges[e] * tile, edges[e + 1] * tile
            s = s_ref[a:b, :]
            target = iota(s.shape, 0) + a == col_ref[0:1, :]
            p_ref[a:b, :] = jnp.where(target, 0.0, jnp.exp(s - row_ref[0:1, :])).astype(BF16)
        if e > 0:
            a, b = edges[e - 1] * tile, edges[e] * tile
            term = dot(w_ref[a:b, :], p_ref[a:b, :], ((0,), (0,)))
            if e == 1:
                acc[...] = term
            else:
                acc[...] += term
        if e < len(edges) - 1:
            a, b = edges[e] * tile, edges[e + 1] * tile
            c = pltpu.make_async_copy(p_ref.at[pl.ds(a, b - a)], p_hbm.at[pl.ds(a, b - a)], p_sems.at[e])
            c.start()
            p_out.append(c)
    rows_out(acc, out_v, out_hbm, out_sem)
    for c in p_out:
        c.wait()


def part_kernel(u_hbm, r_hbm, stat_ref, norm_ref, col_ref, out_ref, u_ref, r_ref, u_sems, r_sems):
    half = u_ref.shape[0] // 2
    u_in = start(rows_in(u_hbm, u_ref, u_sems, half))
    r_in = start(rows_in(r_hbm, r_ref, r_sems, half))
    norm = norm_ref[...]
    scale = jnp.exp(stat_ref[0, :SLOTS, :] - norm).T
    rest = jnp.where(col_ref[...] >= 0.0, jnp.exp(stat_ref[0, SLOTS:, :] - norm) - 1.0, 0.0).T
    for s in range(SLOTS):
        if s % (SLOTS // 2) == 0:
            u_in[s // (SLOTS // 2)].wait()
            r_in[s // (SLOTS // 2)].wait()
        u = u_ref[s * ROWS : (s + 1) * ROWS, :]
        r = r_ref[s * ROWS : (s + 1) * ROWS, :].astype(F32)
        part = (scale[:, s : s + 1] * u + rest[:, s : s + 1] * r).astype(BF16).reshape(16, 8, FEAT)
        for h in range(2):
            out_ref[:, h, s * 8 : (s + 1) * 8, :] = part[:, :, h * HALF : (h + 1) * HALF]


def table_grad_kernel(first, n, tiles_ref, q_hbm, p_hbm, scale_ref, rest_ref, col_ref, *refs):
    outs, (q_ref, p_ref, out_v, q_sem, p_sems, out_sems) = refs[:n], refs[n:]
    tile = 256
    p_in = [
        pltpu.make_async_copy(
            p_hbm.at[pl.ds(pl.multiple_of(tiles_ref[first + i] * TILE, TILE), TILE)],
            p_ref.at[pl.ds(i * TILE, TILE)],
            p_sems.at[i],
        )
        for i in range(n)
    ]
    q_in = pltpu.make_async_copy(q_hbm, q_ref, q_sem)
    p_in[0].start()
    q_in.start()
    start(p_in[1:])
    q_in.wait()
    out = []
    for i in range(n):
        p_in[i].wait()
        for k in range(TILE // tile):
            here = slice(i * TILE + k * tile, i * TILE + (k + 1) * tile)
            p = p_ref[here, :].astype(F32)
            target = iota(p.shape, 0) + (tiles_ref[first + i] * TILE + k * tile) == col_ref[0:1, :]
            slope = jnp.where(target, rest_ref[0:1, :], p * scale_ref[0:1, :])
            out_v[here, :] = dot(slope.astype(BF16), q_ref[...], ((1,), (0,))).astype(out_v.dtype)
        c = pltpu.make_async_copy(out_v.at[pl.ds(i * TILE, TILE)], outs[i], out_sems.at[i])
        c.start()
        out.append(c)
    for c in out:
        c.wait()


def sum_kernel(sel_ref, parts_ref, out_ref):
    out = dot(sel_ref[...], parts_ref[...], ((1,), (0,))).astype(BF16)
    for b in range(2):
        out_ref[:, :, b * HALF : (b + 1) * HALF] = out[b * 256 : (b + 1) * 256].reshape(NDEV, 8, HALF)

def home_kernel(got_ref, out_ref):
    for h in range(2):
        for b in range(2):
            out_ref[b, :, :, h * HALF : (h + 1) * HALF] = got_ref[:, h, :, b * HALF : (b + 1) * HALF].astype(F32)

def relay_kernel(up_ref, down_ref, got_up_ref, got_down_ref, out_up_ref, out_down_ref):
    out_up_ref[...] = (up_ref[...] + got_up_ref[...].astype(F32)).astype(BF16)
    out_down_ref[...] = (down_ref[...] + got_down_ref[...].astype(F32)).astype(BF16)


def base_kernel(own_a_ref, own_b_ref, a_ref, b_ref, out_ref):
    out_ref[:TILE, :] = own_a_ref[...] + a_ref[...].astype(F32)
    out_ref[TILE:, :] = own_b_ref[...] + b_ref[...].astype(F32)


def finish_kernel(base_ref, a_ref, b_ref, out_hbm, out_v, out_sems):
    copies = []
    for i, ref in enumerate((a_ref, b_ref)):
        here = pl.ds(i * TILE, TILE)
        out_v[i * TILE : (i + 1) * TILE, :] = base_ref[i * TILE : (i + 1) * TILE, :] + ref[...].astype(F32)
        c = pltpu.make_async_copy(out_v.at[here], out_hbm.at[here], out_sems.at[i])
        c.start()
        copies.append(c)
    for c in copies:
        c.wait()


def shape(dims, dtype):
    return jax.ShapeDtypeStruct(dims, dtype)

def whole(kernel, out, *args, hbm=(), smem=(), hbm_out=(), limit=60, cost=1024, scratch=()):
    def place(i, far, scalar=()):
        space = pltpu.HBM if i in far else pltpu.SMEM if i in scalar else pltpu.VMEM
        return pl.BlockSpec(memory_space=space)

    single = not isinstance(out, tuple)
    outs = (out,) if single else out
    results = pl.pallas_call(
        kernel,
        out_shape=outs,
        in_specs=[place(i, hbm, smem) for i in range(len(args))],
        out_specs=tuple(place(i, hbm_out) for i in range(len(outs))),
        scratch_shapes=list(scratch),
        compiler_params=pltpu.CompilerParams(vmem_limit_bytes=limit << 20),
        cost_estimate=pl.CostEstimate(flops=cost, transcendentals=0, bytes_accessed=1024),
    )(*args)
    return results[0] if single else results

def sems(n):
    return pltpu.SemaphoreType.DMA((n,))

def per_device(queries, weights, beam, positives, owner):
    me = lax.axis_index("label")
    y = lax.axis_index("dp")
    rows = SLOTS * ROWS
    ranker = weights[0]

    def swap(x):
        return lax.all_to_all(x, "label", split_axis=0, concat_axis=0, tiled=True)

    ids = jnp.arange(NDEV, dtype=jnp.int32)
    held = jnp.sum(jnp.where(owner[None, :] == ids[:, None], ids[None, :], 0), axis=1).astype(F32)
    held_rows = jnp.broadcast_to(held[:, None, None], (NDEV, SLOTS, 128)).reshape(256, 128)
    my_block = jnp.sum(jnp.where(owner == me, ids, 0)).astype(F32)
    mine = jnp.where(iota((16, 128), 1) == 0, my_block, me.astype(F32))

    pieces = whole(
        pieces_kernel,
        shape((16, 2, 8, FEAT + ROWS), BF16),
        queries.reshape(2, 16, 8, FEAT),
        positives.reshape(2, ROWS),
        beam,
        hbm=(0, 1, 2),
        scratch=(
            pltpu.VMEM((2, 16, 8, FEAT), BF16),
            pltpu.VMEM((2, ROWS), jnp.int32),
            pltpu.VMEM(beam.shape, jnp.int32),
            sems(4),
        ),
    )
    got = swap(pieces.reshape(NDEV, 8, FEAT + ROWS)).reshape(256, FEAT + ROWS)

    sent = whole(route_kernel, shape((2048, HALF), BF16), got, held_rows, limit=16)
    arrived = swap(sent.reshape(NDEV, 64, HALF))
    sel, mask, col, col_slots = whole(
        table_kernel,
        (
            shape((512, 2048), BF16),
            shape((256, 128), F32),
            shape((8, rows), jnp.int32),
            shape((SLOTS, ROWS), F32),
        ),
        got,
        held_rows,
        mine,
    )
    positive_rows = whole(
        positive_kernel,
        shape((rows, FEAT), BF16),
        ranker,
        col,
        hbm=(0,),
        hbm_out=(0,),
        scratch=(
            pltpu.VMEM((LABELS, FEAT), BF16),
            pltpu.VMEM((FEAT, rows), F32),
            pltpu.VMEM((rows, FEAT), BF16),
            sems(4),
            pltpu.SemaphoreType.DMA,
        ),
    )
    arrived, positive_rows, col = lax.optimization_barrier((arrived, positive_rows, col))

    scores, q, stats, lse_row = whole(
        scores_kernel,
        (
            shape((LABELS, rows), F32),
            shape((SLOTS, 16, 8, FEAT), BF16),
            shape((NDEV, 2 * SLOTS, ROWS), F32),
            shape((8, rows), F32),
        ),
        arrived.reshape(16, 2, SLOTS, 8, HALF),
        col,
        ranker,
        limit=58,
        hbm=(2,),
        hbm_out=(0, 1),

        scratch=(
            pltpu.VMEM((LABELS, FEAT), BF16),
            pltpu.VMEM((LABELS, rows), F32),
            pltpu.VMEM((SLOTS, 16, 8, FEAT), BF16),
            sems(4),
            sems(4),
            pltpu.SemaphoreType.DMA,
        ),
    )
    q = q.reshape(rows, FEAT)
    all_stats = swap(stats)
    others, p = whole(
        others_kernel,
        (shape((rows, FEAT), F32), shape((LABELS, rows), BF16)),
        ranker,
        scores,
        lse_row,
        col,
        hbm=(0, 1),
        hbm_out=(0, 1),
        scratch=(
            pltpu.VMEM((LABELS, FEAT), BF16),
            pltpu.VMEM((LABELS, rows), F32),
            pltpu.VMEM((LABELS, rows), BF16),
            pltpu.VMEM((FEAT, rows), F32),
            pltpu.VMEM((rows, FEAT), F32),
            sems(8),
            sems(8),
            sems(5),
            pltpu.SemaphoreType.DMA,
        ),
    )
    all_stats, others, p = lax.optimization_barrier((all_stats, others, p))
    lanes = shape((8, rows), F32)
    scale, rest, norm_slots, loss = whole(
        normal_kernel,
        (lanes, lanes, shape((SLOTS, ROWS), F32), shape((2, ROWS), F32)),
        all_stats,
        mask,
        lse_row,
        limit=16,
    )

    up = [(i, (i + 1) % 4) for i in range(4)]
    down = [(i, (i + 3) % 4) for i in range(4)]
    across, ahead, behind = (y + 2) % 4 * 2, (y + 1) % 4 * 2, (y + 3) % 4 * 2
    tiles = jnp.stack([across, across + 1, ahead + 1, behind, ahead, behind + 1, y * 2, y * 2 + 1])
    tiles = tiles.astype(jnp.int32)

    def table_grads(first, scale, dtypes):
        n = len(dtypes)
        return whole(
            functools.partial(table_grad_kernel, first, n),
            tuple(shape((TILE, FEAT), d) for d in dtypes),
            tiles,
            q,
            p,
            scale,
            rest,
            col,
            smem=(0,),
            hbm=(1, 2),
            hbm_out=tuple(range(n)),
            limit=57,
            scratch=(
                pltpu.VMEM((rows, FEAT), BF16),
                pltpu.VMEM((n * TILE, rows), BF16),
                pltpu.VMEM((n * TILE, FEAT), dtypes[0]),
                pltpu.SemaphoreType.DMA,
                sems(n),
                sems(n),
            ),
        )

    far_a, far_b = table_grads(0, scale, (BF16, BF16))
    far_a, far_b, norm_slots, scale = lax.optimization_barrier((far_a, far_b, norm_slots, scale))
    via_up = lax.ppermute(far_a, "dp", up)
    via_down = lax.ppermute(far_b, "dp", down)
    part = whole(
        part_kernel,
        shape((16, 2, 64, HALF), BF16),
        others,
        positive_rows,
        stats,
        norm_slots,
        col_slots,
        hbm=(0, 1),
        scratch=(
            pltpu.VMEM((rows, FEAT), F32),
            pltpu.VMEM((rows, FEAT), BF16),
            sems(2),
            sems(2),
        ),
    )
    part, scale = lax.optimization_barrier((part, scale))
    parts = swap(part.reshape(NDEV, 64, HALF)).reshape(2048, HALF)
    next_b, prev_a = table_grads(2, scale, (BF16, BF16))
    next_b, prev_a, scale = lax.optimization_barrier((next_b, prev_a, scale))
    from_prev_b = lax.ppermute(next_b, "dp", up)
    from_next_a = lax.ppermute(prev_a, "dp", down)
    next_a, prev_b, own_a, own_b = table_grads(4, scale, (F32, F32, F32, F32))

    relay_up, relay_down = whole(
        relay_kernel,
        (shape((TILE, FEAT), BF16), shape((TILE, FEAT), BF16)),
        next_a,
        prev_b,
        via_up,
        via_down,
        limit=16,
        cost=50_000_000_000,
    )
    from_prev_a = lax.ppermute(relay_up, "dp", up)
    from_next_b = lax.ppermute(relay_down, "dp", down)

    homeward = whole(sum_kernel, shape((NDEV, 8, FEAT), BF16), sel, parts, limit=16)
    home = swap(homeward).reshape(16, 2, 8, FEAT)
    grad_queries = whole(home_kernel, shape((2, 16, 8, FEAT), F32), home, limit=16).reshape(256, FEAT)
    base = whole(
        base_kernel,
        shape((2 * TILE, FEAT), F32),
        own_a,
        own_b,
        from_next_a,
        from_prev_b,
        limit=16,
    )
    base, grad_queries = lax.optimization_barrier((base, grad_queries))
    grad_table = whole(
        finish_kernel,
        shape((2 * TILE, FEAT), F32),
        base,
        from_prev_a,
        from_next_b,
        hbm_out=(0,),
        limit=16,
        scratch=(pltpu.VMEM((2 * TILE, FEAT), F32), sems(2)),
    )
    return loss.reshape(256), grad_queries, grad_table[None]

def solution(mesh):
    placed = (
        P(("dp", "label"), None),
        P("label", None, None),
        P(("dp", "label"), None),
        P(("dp", "label")),
        P(),
    )
    return jax.shard_map(
        per_device,
        mesh=mesh,
        in_specs=placed,
        out_specs=(P(("dp", "label")), P(("dp", "label"), None), P("label", "dp", None)),
        check_vma=False,
    )
```

```python
import functools

import jax
import jax.numpy as jnp
from jax import lax
from jax.experimental import pallas as pl
from jax.experimental.pallas import tpu as pltpu
from jax.sharding import PartitionSpec as P

F32 = jnp.float32
BF16 = jnp.bfloat16
NDEV = 32
SLOTS = 8
ROWS = 128
FEAT = 768
HALF = 384
LABELS = 4096
TILE = 512
BIG_TILE = 1024
PART_TILE = 256
NEG = -1e30
BIG = 1e30
LIMIT = 24

def iota(shape, dim):
    return lax.broadcasted_iota(jnp.int32, shape, dim)

def dot(a, b, dims):
    return lax.dot_general(a, b, (dims, ((), ())), preferred_element_type=F32)

def ones_where(mask):
    return jnp.where(mask, 1.0, 0.0).astype(BF16)

def slot_table(meta, held):
    n = held.shape[0]
    r = iota((256, 64), 0)
    q = iota((256, 64), 1)
    pick = ones_where((r // 8 == q % 32) & (r % 8 == 6 + q // 32))
    beams = dot(meta, pick, ((0,), (0,)))
    hit = held == beams[0:1, :]
    for k in range(1, 4):
        hit = hit | (held == beams[k : k + 1, :])
    hit = hit & (iota((n, 64), 1) >= 0)
    before = ones_where(iota((64, 64), 0) < iota((64, 64), 1))
    rank = dot(ones_where(hit), before, ((1,), (0,)))
    slot = (iota((n, 64), 0) % SLOTS).astype(F32)
    return jnp.where(hit & (rank == slot), 1.0, 0.0)

def piece_matrix(table):
    e = iota((64, 512), 1)
    spread = ones_where(iota((64, 512), 0) == e // 8)
    wide = dot(table.astype(BF16), spread, ((1,), (0,)))
    full = jnp.broadcast_to(wide[:, None, :], (256, 8, 512))
    same = iota((256, 8, 512), 1) == iota((256, 8, 512), 2) % 8
    return jnp.where(same, full, 0.0).reshape(2048, 512).astype(BF16)

def route_kernel(got_ref, held_ref, out_ref):
    got = got_ref[...]
    table = slot_table(got[:, FEAT:], held_ref[...][:, :1])
    m = piece_matrix(table)
    out = dot(m[:, :256], got[:, :HALF], ((1,), (0,)))
    out += dot(m[:, 256:], got[:, HALF:FEAT], ((1,), (0,)))
    out_ref[...] = out.astype(BF16)

def table_kernel(got_ref, held_ref, mine_ref, sel_ref, mask_ref, col_ref, slots_ref):
    meta = got_ref[...][:, FEAT:]
    table = slot_table(meta, held_ref[...][:, :1])
    sel_ref[...] = piece_matrix(table).T
    mine = mine_ref[...]
    own = slot_table(meta, mine[:, 0:1])
    row = iota((16, 64), 0)
    q = iota((16, 64), 1).astype(F32)
    home = jnp.where(q == (row.astype(F32) - 8.0) * 32.0 + mine[:, 1:2], 1.0, 0.0)
    own = jnp.where(row < 8, own, jnp.where(row < 10, home, 0.0)).astype(BF16)
    mask = dot(table.astype(BF16), own, ((1,), (1,)))
    mask_ref[...] = jnp.concatenate([mask, jnp.zeros((256, 112), F32)], axis=1)
    qq = iota((64, 256), 0)
    rr = iota((64, 256), 1)
    part = []
    for c in range(3):
        pick = ones_where((rr // 8 == qq % 32) & (rr % 8 == 3 * (qq // 32) + c))
        where_c = dot(own, pick, ((1,), (0,))).astype(BF16)
        part.append(dot(where_c, meta, ((1,), (0,))))
    inside = part[0] == mine[:, 0:1] + 1.0
    col = jnp.where(inside, part[1] * 64.0 + part[2], -1.0)
    slots_ref[...] = col[:SLOTS]
    for s in range(SLOTS):
        piece = col[s : s + 1].astype(jnp.int32)
        col_ref[:, s * ROWS : (s + 1) * ROWS] = jnp.broadcast_to(piece, (8, ROWS))

def start(copies):
    for c in copies:
        c.start()
    return copies

def pieces_kernel(q_hbm, pos_hbm, beam_hbm, out_ref, q_ref, pos_ref, beam_ref, sems):
    small = start(
        [
            pltpu.make_async_copy(pos_hbm, pos_ref, sems.at[0]),
            pltpu.make_async_copy(beam_hbm, beam_ref, sems.at[1]),
        ]
    )
    large = start(
        [
            pltpu.make_async_copy(q_hbm.at[:, pl.ds(8 * i, 8)], q_ref.at[:, pl.ds(8 * i, 8)], sems.at[2 + i])
            for i in range(2)
        ]
    )
    for c in small:
        c.wait()
    pos = pos_ref[...]
    beam = beam_ref[...]
    high, low = (pos >> 12) + 1, pos & (LABELS - 1)
    codes = (high, low >> 6, low & 63)
    row = iota((8, ROWS), 0)
    lane = iota((8, ROWS), 1)
    meta = jnp.full((8, ROWS), -1, jnp.int32)
    for b in range(2):
        for c in range(3):
            meta = jnp.where(row == 3 * b + c, codes[c][b : b + 1, :], meta)
        for k in range(beam.shape[1]):
            meta = jnp.where((row == 6 + b) & (lane == k), beam[b : b + 1, k : k + 1], meta)
    meta = meta.astype(F32).astype(BF16)
    out_ref[:, :, :, FEAT:] = jnp.broadcast_to(meta[None, None], (16, 2, 8, ROWS))
    for i in range(2):
        large[i].wait()
        g = slice(8 * i, 8 * i + 8)
        for h in range(2):
            for b in range(2):
                out_ref[g, h, :, b * HALF : (b + 1) * HALF] = q_ref[b, g, :, h * HALF : (h + 1) * HALF]

def by_slot(lanes):
    row = iota((SLOTS, ROWS), 0)
    out = jnp.zeros((SLOTS, ROWS), F32)
    for s in range(SLOTS):
        out = jnp.where(row == s, lanes[:, s * ROWS : (s + 1) * ROWS], out)
    return out

def scores_kernel(got_ref, col_ref, w_ref, p_ref, q_ref, top_ref, stat_ref, row_ref, s_ref, high, total, found):
    step = pl.program_id(0)
    rows = s_ref.shape[1]

    @pl.when(step == 0)
    def _():
        for g in range(16):
            for h in range(2):
                for s in range(SLOTS):
                    here = slice(s * ROWS + g * 8, s * ROWS + g * 8 + 8)
                    q_ref[here, h * HALF : (h + 1) * HALF] = got_ref[g, h, s]
        high[...] = jnp.full_like(high, NEG)
        total[...] = jnp.zeros_like(total)
        found[...] = jnp.zeros_like(found)

    n = BIG_TILE // PART_TILE
    top, tot, pick = high[...], total[...], found[...]
    for k in range(n + 1):
        if k < n:
            here = slice(k * PART_TILE, (k + 1) * PART_TILE)
            s_ref[here, :] = dot(w_ref[here, :], q_ref[...], ((1,), (1,)))
        if k > 0:
            here = slice((k - 1) * PART_TILE, k * PART_TILE)
            s = s_ref[here, :]
            target = iota(s.shape, 0) + (step * BIG_TILE + (k - 1) * PART_TILE) == col_ref[0:1, :]
            pick += jnp.sum(jnp.where(target, s, 0.0).reshape(PART_TILE // 8, 8, rows), axis=0)
            best = jnp.max(jnp.max(s.reshape(PART_TILE // 8, 8, rows), axis=0), axis=0, keepdims=True)
            best = jnp.broadcast_to(best, (8, rows))
            e = jnp.exp(s - best[0:1, :])
            p_ref[here, :] = jnp.where(target, 0.0, e).astype(BF16)
            new = jnp.maximum(top, best)
            add = jnp.sum(e.reshape(PART_TILE // 8, 8, rows), axis=0)
            tot = tot * jnp.exp(top - new) + add * jnp.exp(best - new)
            top = new
            top_ref[k - 1] = best
    high[...], total[...], found[...] = top, tot, pick

    @pl.when(step == pl.num_programs(0) - 1)
    def _():
        lse = top[0:1, :] + jnp.log(jnp.sum(tot, axis=0, keepdims=True))
        row_ref[...] = jnp.broadcast_to(lse, (8, rows))
        chosen = jnp.sum(pick, axis=0, keepdims=True)
        stat_ref[:, :SLOTS, :] = jnp.broadcast_to(by_slot(lse)[None], (NDEV, SLOTS, ROWS))
        stat_ref[:, SLOTS:, :] = jnp.broadcast_to(by_slot(chosen)[None], (NDEV, SLOTS, ROWS))


def normal_kernel(stat_ref, mask_ref, norm_ref, rest_ref, slots_ref, loss_ref):
    lse = stat_ref[:, :SLOTS, :].reshape(NDEV * SLOTS, ROWS)
    found = stat_ref[:, SLOTS:, :].reshape(NDEV * SLOTS, ROWS)
    mask = mask_ref[...]
    for s in range(SLOTS + 2):
        use = mask[:, s : s + 1] > 0.5
        kept = jnp.where(use, lse, NEG)
        high = jnp.max(kept, axis=0, keepdims=True)
        tot = jnp.sum(jnp.where(use, jnp.exp(kept - high), 0.0), axis=0, keepdims=True)
        value = jnp.where(high > 0.5 * NEG, high + jnp.log(tot), BIG)
        positive = jnp.sum(jnp.where(use, found, 0.0), axis=0, keepdims=True)
        if s < SLOTS:
            here = slice(s * ROWS, (s + 1) * ROWS)
            norm_ref[:, here] = jnp.broadcast_to(value, (8, ROWS))
            rest_ref[:, here] = jnp.broadcast_to(jnp.exp(positive - value) - 1.0, (8, ROWS))
            slots_ref[s : s + 1, :] = value
        else:
            loss_ref[s - SLOTS : s - SLOTS + 1, :] = value - positive


def rows_from(acc, out_ref):
    for s in range(SLOTS):
        here = slice(s * ROWS, (s + 1) * ROWS)
        out_ref[here, :] = acc[:, here].T.astype(out_ref.dtype)


def add_to(acc, term, first):
    @pl.when(first)
    def _():
        acc[...] = term

    @pl.when(jnp.logical_not(first))
    def _():
        acc[...] += term


def positive_kernel(col_ref, w_ref, out_ref, acc):
    step = pl.program_id(0)
    target = iota((BIG_TILE, acc.shape[1]), 0) + step * BIG_TILE == col_ref[0:1, :]
    add_to(acc, dot(w_ref[...], ones_where(target), ((0,), (0,))), step == 0)

    @pl.when(step == pl.num_programs(0) - 1)
    def _():
        rows_from(acc, out_ref)


def others_kernel(top_ref, row_ref, w_ref, p_ref, out_ref, acc):
    step = pl.program_id(0)
    term = None
    for k in range(0, BIG_TILE // PART_TILE, 2):
        pair = []
        for i in (k, k + 1):
            scale = jnp.exp(top_ref[i][0:1, :] - row_ref[0:1, :])
            here = slice(i * PART_TILE, (i + 1) * PART_TILE)
            pair.append((p_ref[here, :].astype(F32) * scale).astype(BF16))
        here = slice(k * PART_TILE, (k + 2) * PART_TILE)
        one = dot(w_ref[here, :], jnp.concatenate(pair, axis=0), ((0,), (0,)))
        term = one if term is None else term + one
    add_to(acc, term, step == 0)

    @pl.when(step == pl.num_programs(0) - 1)
    def _():
        rows_from(acc, out_ref)


def part_kernel(u_ref, r_ref, stat_ref, norm_ref, col_ref, out_ref):
    norm = norm_ref[...]
    scale = jnp.exp(stat_ref[0, :SLOTS, :] - norm).T
    rest = jnp.where(col_ref[...] >= 0.0, jnp.exp(stat_ref[0, SLOTS:, :] - norm) - 1.0, 0.0).T
    for s in range(SLOTS):
        u = u_ref[s * ROWS : (s + 1) * ROWS, :].astype(F32)
        r = r_ref[s * ROWS : (s + 1) * ROWS, :].astype(F32)
        part = (scale[:, s : s + 1] * u + rest[:, s : s + 1] * r).astype(BF16).reshape(16, 8, FEAT)
        for h in range(2):
            out_ref[:, h, s * 8 : (s + 1) * 8, :] = part[:, :, h * HALF : (h + 1) * HALF]


def table_grad_kernel(base, tiles_ref, q_ref, top_ref, norm_ref, rest_ref, col_ref, p_ref, *out_refs):
    step = pl.program_id(0)
    first = tiles_ref[base + step] * TILE
    for k in range(TILE // PART_TILE):
        here = slice(k * PART_TILE, (k + 1) * PART_TILE)
        scale = jnp.exp(top_ref[tiles_ref[base + step] * (TILE // PART_TILE) + k][0:1, :] - norm_ref[0:1, :])
        p = p_ref[here, :].astype(F32)
        target = iota(p.shape, 0) + (first + k * PART_TILE) == col_ref[0:1, :]
        slope = jnp.where(target, rest_ref[0:1, :], p * scale).astype(BF16)
        value = dot(slope, q_ref[...], ((1,), (0,)))
        for i, ref in enumerate(out_refs):

            @pl.when(step == i)
            def _(ref=ref):
                ref[here, :] = value.astype(ref.dtype)


def sum_kernel(sel_ref, parts_ref, out_ref):
    out = dot(sel_ref[...], parts_ref[...], ((1,), (0,))).astype(BF16)
    for b in range(2):
        out_ref[:, :, b * HALF : (b + 1) * HALF] = out[b * 256 : (b + 1) * 256].reshape(NDEV, 8, HALF)

def home_kernel(got_ref, out_ref):
    for h in range(2):
        for b in range(2):
            out_ref[b, :, :, h * HALF : (h + 1) * HALF] = got_ref[:, h, :, b * HALF : (b + 1) * HALF].astype(F32)

def relay_kernel(up_ref, down_ref, got_up_ref, got_down_ref, out_up_ref, out_down_ref):
    out_up_ref[...] = (up_ref[...] + got_up_ref[...].astype(F32)).astype(BF16)
    out_down_ref[...] = (down_ref[...] + got_down_ref[...].astype(F32)).astype(BF16)


def base_kernel(own_a_ref, own_b_ref, a_ref, b_ref, out_ref):
    out_ref[:TILE, :] = own_a_ref[...] + a_ref[...].astype(F32)
    out_ref[TILE:, :] = own_b_ref[...] + b_ref[...].astype(F32)


def finish_kernel(base_ref, a_ref, b_ref, out_hbm, out_v, out_sems):
    copies = []
    for i, ref in enumerate((a_ref, b_ref)):
        here = pl.ds(i * TILE, TILE)
        out_v[i * TILE : (i + 1) * TILE, :] = base_ref[i * TILE : (i + 1) * TILE, :] + ref[...].astype(F32)
        c = pltpu.make_async_copy(out_v.at[here], out_hbm.at[here], out_sems.at[i])
        c.start()
        copies.append(c)
    for c in copies:
        c.wait()


def shape(dims, dtype):
    return jax.ShapeDtypeStruct(dims, dtype)

def whole(kernel, out, *args, hbm=(), smem=(), hbm_out=(), limit=60, cost=1024, scratch=()):
    def place(i, far, scalar=()):
        space = pltpu.HBM if i in far else pltpu.SMEM if i in scalar else pltpu.VMEM
        return pl.BlockSpec(memory_space=space)

    single = not isinstance(out, tuple)
    outs = (out,) if single else out
    results = pl.pallas_call(
        kernel,
        out_shape=outs,
        in_specs=[place(i, hbm, smem) for i in range(len(args))],
        out_specs=tuple(place(i, hbm_out) for i in range(len(outs))),
        scratch_shapes=list(scratch),
        compiler_params=pltpu.CompilerParams(vmem_limit_bytes=limit << 20),
        cost_estimate=pl.CostEstimate(flops=cost, transcendentals=0, bytes_accessed=1024),
    )(*args)
    return results[0] if single else results

def fixed(dims):
    return pl.BlockSpec(dims, lambda *_: (0,) * len(dims))


def tiled(dims):
    return pl.BlockSpec(dims, lambda i, *_: (i,) + (0,) * (len(dims) - 1))


def stepped(kernel, grid, in_specs, outs, out_specs, scratch, *args, limit=LIMIT, scalars=0, cost=1024):
    spec = pltpu.PrefetchScalarGridSpec(
        num_scalar_prefetch=scalars,
        grid=(grid,),
        in_specs=in_specs,
        out_specs=out_specs,
        scratch_shapes=list(scratch),
    )
    return pl.pallas_call(
        kernel,
        grid_spec=spec,
        out_shape=outs,
        compiler_params=pltpu.CompilerParams(vmem_limit_bytes=limit << 20),
        cost_estimate=pl.CostEstimate(flops=cost, transcendentals=0, bytes_accessed=1024),
    )(*args)


def sems(n):
    return pltpu.SemaphoreType.DMA((n,))


def per_device(queries, weights, beam, positives, owner):
    me = lax.axis_index("label")
    y = lax.axis_index("dp")
    rows = SLOTS * ROWS
    ranker = pltpu.with_memory_space_constraint(weights[0], pltpu.HBM)

    def swap(x):
        return lax.all_to_all(x, "label", split_axis=0, concat_axis=0, tiled=True)

    ids = jnp.arange(NDEV, dtype=jnp.int32)
    held = jnp.sum(jnp.where(owner[None, :] == ids[:, None], ids[None, :], 0), axis=1).astype(F32)
    held_rows = jnp.broadcast_to(held[:, None, None], (NDEV, SLOTS, 128)).reshape(256, 128)
    my_block = jnp.sum(jnp.where(owner == me, ids, 0)).astype(F32)
    mine = jnp.where(iota((16, 128), 1) == 0, my_block, me.astype(F32))

    pieces = whole(
        pieces_kernel,
        shape((16, 2, 8, FEAT + ROWS), BF16),
        queries.reshape(2, 16, 8, FEAT),
        positives.reshape(2, ROWS),
        beam,
        hbm=(0, 1, 2),
        scratch=(
            pltpu.VMEM((2, 16, 8, FEAT), BF16),
            pltpu.VMEM((2, ROWS), jnp.int32),
            pltpu.VMEM(beam.shape, jnp.int32),
            sems(4),
        ),
    )
    got = swap(pieces.reshape(NDEV, 8, FEAT + ROWS)).reshape(256, FEAT + ROWS)

    sent = whole(route_kernel, shape((2048, HALF), BF16), got, held_rows, limit=16)
    arrived = swap(sent.reshape(NDEV, 64, HALF))
    sel, mask, col, col_slots = whole(
        table_kernel,
        (
            shape((512, 2048), BF16),
            shape((256, 128), F32),
            shape((8, rows), jnp.int32),
            shape((SLOTS, ROWS), F32),
        ),
        got,
        held_rows,
        mine,
    )
    steps = LABELS // BIG_TILE
    w_spec = tiled((BIG_TILE, FEAT))
    lanes = shape((8, rows), F32)
    positive_rows = stepped(
        positive_kernel,
        steps,
        [fixed((8, rows)), w_spec],
        shape((rows, FEAT), BF16),
        fixed((rows, FEAT)),
        (pltpu.VMEM((FEAT, rows), F32),),
        col,
        ranker,
    )
    arrived, positive_rows, col = lax.optimization_barrier((arrived, positive_rows, col))

    parts_each = BIG_TILE // PART_TILE
    p, q, tops, stats, lse_row = stepped(
        scores_kernel,
        steps,
        [fixed((16, 2, SLOTS, 8, HALF)), fixed((8, rows)), w_spec],
        (
            pltpu.HBM((LABELS, rows), BF16),
            shape((rows, FEAT), BF16),
            shape((LABELS // PART_TILE, 8, rows), F32),
            shape((NDEV, 2 * SLOTS, ROWS), F32),
            lanes,
        ),
        (
            tiled((BIG_TILE, rows)),
            fixed((rows, FEAT)),
            tiled((parts_each, 8, rows)),
            fixed((NDEV, 2 * SLOTS, ROWS)),
            fixed((8, rows)),
        ),
        (
            pltpu.VMEM((BIG_TILE, rows), F32),
            pltpu.VMEM((8, rows), F32),
            pltpu.VMEM((8, rows), F32),
            pltpu.VMEM((8, rows), F32),
        ),
        pltpu.with_memory_space_constraint(arrived.reshape(16, 2, SLOTS, 8, HALF), pltpu.HBM),
        col,
        ranker,
    )
    all_stats = swap(stats)
    p = pltpu.with_memory_space_constraint(p, pltpu.HBM)
    others = stepped(
        others_kernel,
        steps,
        [tiled((parts_each, 8, rows)), fixed((8, rows)), w_spec, tiled((BIG_TILE, rows))],
        pltpu.HBM((rows, FEAT), BF16),
        fixed((rows, FEAT)),
        (pltpu.VMEM((FEAT, rows), F32),),
        tops,
        lse_row,
        ranker,
        p,
    )
    all_stats, others = lax.optimization_barrier((all_stats, others))
    norm, rest, norm_slots, loss = whole(
        normal_kernel,
        (lanes, lanes, shape((SLOTS, ROWS), F32), shape((2, ROWS), F32)),
        all_stats,
        mask,
        limit=16,
    )

    up = [(i, (i + 1) % 4) for i in range(4)]
    down = [(i, (i + 3) % 4) for i in range(4)]
    across, ahead, behind = (y + 2) % 4 * 2, (y + 1) % 4 * 2, (y + 3) % 4 * 2
    tiles = jnp.stack([across, across + 1, ahead + 1, behind, ahead, behind + 1, y * 2, y * 2 + 1])
    tiles = tiles.astype(jnp.int32)

    def table_grads(first, norm, dtypes):
        n = len(dtypes)
        return stepped(
            functools.partial(table_grad_kernel, first),
            n,
            [
                fixed((rows, FEAT)),
                fixed((LABELS // PART_TILE, 8, rows)),
                fixed((8, rows)),
                fixed((8, rows)),
                fixed((8, rows)),
                pl.BlockSpec((TILE, rows), lambda i, t: (t[first + i], 0)),
            ],
            tuple(pltpu.HBM((TILE, FEAT), d) for d in dtypes),
            tuple(fixed((TILE, FEAT)) for _ in dtypes),
            (),
            tiles,
            q,
            tops,
            norm,
            rest,
            col,
            p,
            scalars=1,
        )

    far_a, far_b = table_grads(0, norm, (BF16, BF16))
    far_a, far_b, norm_slots, norm = lax.optimization_barrier((far_a, far_b, norm_slots, norm))
    via_up = lax.ppermute(far_a, "dp", up)
    via_down = lax.ppermute(far_b, "dp", down)
    part = whole(
        part_kernel,
        pltpu.HBM((16, 2, 64, HALF), BF16),
        others,
        positive_rows,
        stats,
        norm_slots,
        col_slots,
        limit=16,
    )
    part, norm = lax.optimization_barrier((part, norm))
    parts = swap(part.reshape(NDEV, 64, HALF)).reshape(2048, HALF)
    next_b, prev_a = table_grads(2, norm, (BF16, BF16))
    next_b, prev_a, norm = lax.optimization_barrier((next_b, prev_a, norm))
    from_prev_b = lax.ppermute(next_b, "dp", up)
    from_next_a = lax.ppermute(prev_a, "dp", down)
    next_a, prev_b, own_a, own_b = table_grads(4, norm, (F32, F32, F32, F32))

    relay_up, relay_down = whole(
        relay_kernel,
        (shape((TILE, FEAT), BF16), shape((TILE, FEAT), BF16)),
        next_a,
        prev_b,
        via_up,
        via_down,
        limit=16,
        cost=50_000_000_000,
    )
    from_prev_a = lax.ppermute(relay_up, "dp", up)
    from_next_b = lax.ppermute(relay_down, "dp", down)

    homeward = whole(sum_kernel, shape((NDEV, 8, FEAT), BF16), sel, parts, limit=16)
    home = swap(homeward).reshape(16, 2, 8, FEAT)
    grad_queries = whole(home_kernel, shape((2, 16, 8, FEAT), F32), home, limit=16).reshape(256, FEAT)
    base = whole(
        base_kernel,
        shape((2 * TILE, FEAT), F32),
        own_a,
        own_b,
        from_next_a,
        from_prev_b,
        limit=16,
    )
    base, grad_queries = lax.optimization_barrier((base, grad_queries))
    grad_table = whole(
        finish_kernel,
        shape((2 * TILE, FEAT), F32),
        base,
        from_prev_a,
        from_next_b,
        hbm_out=(0,),
        limit=16,
        scratch=(pltpu.VMEM((2 * TILE, FEAT), F32), sems(2)),
    )
    return loss.reshape(256), grad_queries, grad_table[None]

def solution(mesh):
    placed = (
        P(("dp", "label"), None),
        P("label", None, None),
        P(("dp", "label"), None),
        P(("dp", "label")),
        P(),
    )
    return jax.shard_map(
        per_device,
        mesh=mesh,
        in_specs=placed,
        out_specs=(P(("dp", "label")), P(("dp", "label"), None), P("label", "dp", None)),
        check_vma=False,
    )
```

```python
import functools

import jax
import jax.numpy as jnp
from jax import lax
from jax.experimental import pallas as pl
from jax.experimental.pallas import tpu as pltpu
from jax.sharding import PartitionSpec as P

F32 = jnp.float32
BF16 = jnp.bfloat16
NDEV = 32
SLOTS = 8
ROWS = 128
FEAT = 768
HALF = 384
LABELS = 4096
TILE = 512
BIG_TILE = 1024
PART_TILE = 256
NEG = -1e30
BIG = 1e30
LIMIT = 24

def iota(shape, dim):
    return lax.broadcasted_iota(jnp.int32, shape, dim)

def dot(a, b, dims):
    return lax.dot_general(a, b, (dims, ((), ())), preferred_element_type=F32)

def ones_where(mask):
    return jnp.where(mask, 1.0, 0.0).astype(BF16)

def slot_table(meta, held):
    n = held.shape[0]
    r = iota((256, 64), 0)
    q = iota((256, 64), 1)
    pick = ones_where((r // 8 == q % 32) & (r % 8 == 6 + q // 32))
    beams = dot(meta, pick, ((0,), (0,)))
    hit = held == beams[0:1, :]
    for k in range(1, 4):
        hit = hit | (held == beams[k : k + 1, :])
    hit = hit & (iota((n, 64), 1) >= 0)
    before = ones_where(iota((64, 64), 0) < iota((64, 64), 1))
    rank = dot(ones_where(hit), before, ((1,), (0,)))
    slot = (iota((n, 64), 0) % SLOTS).astype(F32)
    return jnp.where(hit & (rank == slot), 1.0, 0.0)

def piece_matrix(table):
    e = iota((64, 512), 1)
    spread = ones_where(iota((64, 512), 0) == e // 8)
    wide = dot(table.astype(BF16), spread, ((1,), (0,)))
    full = jnp.broadcast_to(wide[:, None, :], (256, 8, 512))
    same = iota((256, 8, 512), 1) == iota((256, 8, 512), 2) % 8
    return jnp.where(same, full, 0.0).reshape(2048, 512).astype(BF16)

def route_kernel(got_ref, held_ref, out_ref):
    got = got_ref[...]
    table = slot_table(got[:, FEAT:], held_ref[...][:, :1])
    m = piece_matrix(table)
    out = dot(m[:, :256], got[:, :HALF], ((1,), (0,)))
    out += dot(m[:, 256:], got[:, HALF:FEAT], ((1,), (0,)))
    out_ref[...] = out.astype(BF16)

def table_kernel(got_ref, held_ref, mine_ref, sel_ref, mask_ref, col_ref, slots_ref):
    meta = got_ref[...][:, FEAT:]
    table = slot_table(meta, held_ref[...][:, :1])
    sel_ref[...] = piece_matrix(table).T
    mine = mine_ref[...]
    own = slot_table(meta, mine[:, 0:1])
    row = iota((16, 64), 0)
    q = iota((16, 64), 1).astype(F32)
    home = jnp.where(q == (row.astype(F32) - 8.0) * 32.0 + mine[:, 1:2], 1.0, 0.0)
    own = jnp.where(row < 8, own, jnp.where(row < 10, home, 0.0)).astype(BF16)
    mask = dot(table.astype(BF16), own, ((1,), (1,)))
    mask_ref[...] = jnp.concatenate([mask, jnp.zeros((256, 112), F32)], axis=1)
    qq = iota((64, 256), 0)
    rr = iota((64, 256), 1)
    part = []
    for c in range(3):
        pick = ones_where((rr // 8 == qq % 32) & (rr % 8 == 3 * (qq // 32) + c))
        where_c = dot(own, pick, ((1,), (0,))).astype(BF16)
        part.append(dot(where_c, meta, ((1,), (0,))))
    inside = part[0] == mine[:, 0:1] + 1.0
    col = jnp.where(inside, part[1] * 64.0 + part[2], -1.0)
    slots_ref[...] = col[:SLOTS]
    for s in range(SLOTS):
        piece = col[s : s + 1].astype(jnp.int32)
        col_ref[:, s * ROWS : (s + 1) * ROWS] = jnp.broadcast_to(piece, (8, ROWS))

def start(copies):
    for c in copies:
        c.start()
    return copies

def pieces_kernel(q_hbm, pos_hbm, beam_hbm, out_ref, q_ref, pos_ref, beam_ref, sems):
    small = start(
        [
            pltpu.make_async_copy(pos_hbm, pos_ref, sems.at[0]),
            pltpu.make_async_copy(beam_hbm, beam_ref, sems.at[1]),
        ]
    )
    large = start(
        [
            pltpu.make_async_copy(q_hbm.at[:, pl.ds(8 * i, 8)], q_ref.at[:, pl.ds(8 * i, 8)], sems.at[2 + i])
            for i in range(2)
        ]
    )
    for c in small:
        c.wait()
    pos = pos_ref[...]
    beam = beam_ref[...]
    high, low = (pos >> 12) + 1, pos & (LABELS - 1)
    codes = (high, low >> 6, low & 63)
    row = iota((8, ROWS), 0)
    lane = iota((8, ROWS), 1)
    meta = jnp.full((8, ROWS), -1, jnp.int32)
    for b in range(2):
        for c in range(3):
            meta = jnp.where(row == 3 * b + c, codes[c][b : b + 1, :], meta)
        for k in range(beam.shape[1]):
            meta = jnp.where((row == 6 + b) & (lane == k), beam[b : b + 1, k : k + 1], meta)
    meta = meta.astype(F32).astype(BF16)
    out_ref[:, :, :, FEAT:] = jnp.broadcast_to(meta[None, None], (16, 2, 8, ROWS))
    for i in range(2):
        large[i].wait()
        g = slice(8 * i, 8 * i + 8)
        for h in range(2):
            for b in range(2):
                out_ref[g, h, :, b * HALF : (b + 1) * HALF] = q_ref[b, g, :, h * HALF : (h + 1) * HALF]

def by_slot(lanes):
    row = iota((SLOTS, ROWS), 0)
    out = jnp.zeros((SLOTS, ROWS), F32)
    for s in range(SLOTS):
        out = jnp.where(row == s, lanes[:, s * ROWS : (s + 1) * ROWS], out)
    return out

def scores_kernel(got_ref, col_ref, w_ref, r_ref, p_ref, q_ref, top_ref, stat_ref, row_ref, s_ref, high, total, found):
    step = pl.program_id(0)
    rows = s_ref.shape[1]

    @pl.when(step == 0)
    def _():
        for g in range(16):
            for h in range(2):
                for s in range(SLOTS):
                    here = slice(s * ROWS + g * 8, s * ROWS + g * 8 + 8)
                    q_ref[here, h * HALF : (h + 1) * HALF] = got_ref[g, h, s]
        high[...] = jnp.full_like(high, NEG)
        total[...] = jnp.zeros_like(total)

    n = BIG_TILE // PART_TILE
    top, tot = high[...], total[...]
    for k in range(n + 1):
        if k < n:
            here = slice(k * PART_TILE, (k + 1) * PART_TILE)
            s_ref[here, :] = dot(w_ref[here, :], q_ref[...], ((1,), (1,)))
        if k > 0:
            here = slice((k - 1) * PART_TILE, k * PART_TILE)
            s = s_ref[here, :]
            best = jnp.max(jnp.max(s.reshape(PART_TILE // 8, 8, rows), axis=0), axis=0, keepdims=True)
            best = jnp.broadcast_to(best, (8, rows))
            e = jnp.exp(s - best[0:1, :])
            target = iota(s.shape, 0) == col_ref[0:1, :] - (step * BIG_TILE + (k - 1) * PART_TILE)
            p_ref[here, :] = jnp.where(target, 0.0, e).astype(BF16)
            new = jnp.maximum(top, best)
            add = jnp.sum(e.reshape(PART_TILE // 8, 8, rows), axis=0)
            tot = tot * jnp.exp(top - new) + add * jnp.exp(best - new)
            top = new
            top_ref[k - 1] = best
    high[...], total[...] = top, tot

    two = 2 * ROWS
    mine = q_ref[pl.ds(pl.multiple_of(step * two, two), two), :].astype(F32) * r_ref[...].astype(F32)
    folded = mine[:, :ROWS]
    for c in range(1, FEAT // ROWS):
        folded += mine[:, c * ROWS : (c + 1) * ROWS]
    for i in range(2):
        one = jnp.sum(folded[i * ROWS : (i + 1) * ROWS].T, axis=0, keepdims=True)
        found[step, i : i + 1, :] = one

    @pl.when(step == pl.num_programs(0) - 1)
    def _():
        lse = top[0:1, :] + jnp.log(jnp.sum(tot, axis=0, keepdims=True))
        row_ref[...] = jnp.broadcast_to(lse, (8, rows))
        stat_ref[:, :SLOTS, :] = jnp.broadcast_to(by_slot(lse)[None], (NDEV, SLOTS, ROWS))
        for i in range(SLOTS // 2):
            here = slice(SLOTS + 2 * i, SLOTS + 2 * i + 2)
            stat_ref[:, here, :] = jnp.broadcast_to(found[i][None], (NDEV, 2, ROWS))


def normal_kernel(stat_ref, mask_ref, norm_ref, rest_ref, slots_ref, loss_ref):
    lse = stat_ref[:, :SLOTS, :].reshape(NDEV * SLOTS, ROWS)
    found = stat_ref[:, SLOTS:, :].reshape(NDEV * SLOTS, ROWS)
    mask = mask_ref[...]
    for s in range(SLOTS + 2):
        use = mask[:, s : s + 1] > 0.5
        kept = jnp.where(use, lse, NEG)
        high = jnp.max(kept, axis=0, keepdims=True)
        tot = jnp.sum(jnp.where(use, jnp.exp(kept - high), 0.0), axis=0, keepdims=True)
        value = jnp.where(high > 0.5 * NEG, high + jnp.log(tot), BIG)
        positive = jnp.sum(jnp.where(use, found, 0.0), axis=0, keepdims=True)
        if s < SLOTS:
            here = slice(s * ROWS, (s + 1) * ROWS)
            norm_ref[:, here] = jnp.broadcast_to(value, (8, ROWS))
            rest_ref[:, here] = jnp.broadcast_to(jnp.exp(positive - value) - 1.0, (8, ROWS))
            slots_ref[s : s + 1, :] = value
        else:
            loss_ref[s - SLOTS : s - SLOTS + 1, :] = value - positive


def rows_from(acc, out_ref):
    for s in range(SLOTS):
        here = slice(s * ROWS, (s + 1) * ROWS)
        out_ref[here, :] = acc[:, here].T.astype(out_ref.dtype)


def add_to(acc, term, first):
    @pl.when(first)
    def _():
        acc[...] = term

    @pl.when(jnp.logical_not(first))
    def _():
        acc[...] += term


def positive_kernel(col_ref, w_ref, out_ref, acc):
    step = pl.program_id(0)
    target = iota((BIG_TILE, acc.shape[1]), 0) + step * BIG_TILE == col_ref[0:1, :]
    add_to(acc, dot(w_ref[...], ones_where(target), ((0,), (0,))), step == 0)

    @pl.when(step == pl.num_programs(0) - 1)
    def _():
        rows_from(acc, out_ref)


def others_kernel(top_ref, row_ref, w_ref, p_ref, out_ref, acc, scaled):
    step = pl.program_id(0)
    for i in range(BIG_TILE // PART_TILE):
        scale = jnp.exp(top_ref[i][0:1, :] - row_ref[0:1, :])
        here = slice(i * PART_TILE, (i + 1) * PART_TILE)
        scaled[here, :] = (p_ref[here, :].astype(F32) * scale).astype(BF16)
    add_to(acc, dot(w_ref[...], scaled[...], ((0,), (0,))), step == 0)

    @pl.when(step == pl.num_programs(0) - 1)
    def _():
        rows_from(acc, out_ref)


def part_kernel(u_ref, r_ref, stat_ref, norm_ref, col_ref, out_ref):
    norm = norm_ref[...]
    scale = jnp.exp(stat_ref[0, :SLOTS, :] - norm).T
    rest = jnp.where(col_ref[...] >= 0.0, jnp.exp(stat_ref[0, SLOTS:, :] - norm) - 1.0, 0.0).T
    for s in range(SLOTS):
        u = u_ref[s * ROWS : (s + 1) * ROWS, :].astype(F32)
        r = r_ref[s * ROWS : (s + 1) * ROWS, :].astype(F32)
        part = (scale[:, s : s + 1] * u + rest[:, s : s + 1] * r).astype(BF16).reshape(16, 8, FEAT)
        for h in range(2):
            out_ref[:, h, s * 8 : (s + 1) * 8, :] = part[:, :, h * HALF : (h + 1) * HALF]


def table_grad_kernel(base, tiles_ref, q_ref, top_ref, norm_ref, rest_ref, col_ref, *refs):
    n = len(refs) // 2
    for i in range(n):
        p_ref, out_ref = refs[i], refs[n + i]
        tile = tiles_ref[base + i]
        for k in range(TILE // PART_TILE):
            here = slice(k * PART_TILE, (k + 1) * PART_TILE)
            scale = jnp.exp(top_ref[tile * (TILE // PART_TILE) + k][0:1, :] - norm_ref[0:1, :])
            p = p_ref[here, :].astype(F32)
            target = iota(p.shape, 0) == col_ref[0:1, :] - (tile * TILE + k * PART_TILE)
            slope = jnp.where(target, rest_ref[0:1, :], p * scale).astype(BF16)
            out_ref[here, :] = dot(slope, q_ref[...], ((1,), (0,))).astype(out_ref.dtype)


def sum_kernel(sel_ref, parts_ref, out_ref):
    out = dot(sel_ref[...], parts_ref[...], ((1,), (0,))).astype(BF16)
    for b in range(2):
        out_ref[:, :, b * HALF : (b + 1) * HALF] = out[b * 256 : (b + 1) * 256].reshape(NDEV, 8, HALF)

def home_kernel(got_ref, out_ref):
    for h in range(2):
        for b in range(2):
            out_ref[b, :, :, h * HALF : (h + 1) * HALF] = got_ref[:, h, :, b * HALF : (b + 1) * HALF].astype(F32)

def relay_kernel(up_ref, down_ref, got_up_ref, got_down_ref, out_up_ref, out_down_ref):
    out_up_ref[...] = (up_ref[...] + got_up_ref[...].astype(F32)).astype(BF16)
    out_down_ref[...] = (down_ref[...] + got_down_ref[...].astype(F32)).astype(BF16)


def base_kernel(own_a_ref, own_b_ref, a_ref, b_ref, out_ref):
    out_ref[:TILE, :] = own_a_ref[...] + a_ref[...].astype(F32)
    out_ref[TILE:, :] = own_b_ref[...] + b_ref[...].astype(F32)


def finish_kernel(base_ref, a_ref, b_ref, out_hbm, out_v, out_sems):
    copies = []
    for i, ref in enumerate((a_ref, b_ref)):
        here = pl.ds(i * TILE, TILE)
        out_v[i * TILE : (i + 1) * TILE, :] = base_ref[i * TILE : (i + 1) * TILE, :] + ref[...].astype(F32)
        c = pltpu.make_async_copy(out_v.at[here], out_hbm.at[here], out_sems.at[i])
        c.start()
        copies.append(c)
    for c in copies:
        c.wait()


def shape(dims, dtype):
    return jax.ShapeDtypeStruct(dims, dtype)

def whole(kernel, out, *args, hbm=(), smem=(), hbm_out=(), limit=60, cost=1024, scratch=()):
    def place(i, far, scalar=()):
        space = pltpu.HBM if i in far else pltpu.SMEM if i in scalar else pltpu.VMEM
        return pl.BlockSpec(memory_space=space)

    single = not isinstance(out, tuple)
    outs = (out,) if single else out
    results = pl.pallas_call(
        kernel,
        out_shape=outs,
        in_specs=[place(i, hbm, smem) for i in range(len(args))],
        out_specs=tuple(place(i, hbm_out) for i in range(len(outs))),
        scratch_shapes=list(scratch),
        compiler_params=pltpu.CompilerParams(vmem_limit_bytes=limit << 20),
        cost_estimate=pl.CostEstimate(flops=cost, transcendentals=0, bytes_accessed=1024),
    )(*args)
    return results[0] if single else results

def fixed(dims):
    return pl.BlockSpec(dims, lambda *_: (0,) * len(dims))


def tiled(dims):
    return pl.BlockSpec(dims, lambda i, *_: (i,) + (0,) * (len(dims) - 1))


def stepped(kernel, grid, in_specs, outs, out_specs, scratch, *args, limit=LIMIT, scalars=0, cost=1024):
    spec = pltpu.PrefetchScalarGridSpec(
        num_scalar_prefetch=scalars,
        grid=(grid,),
        in_specs=in_specs,
        out_specs=out_specs,
        scratch_shapes=list(scratch),
    )
    return pl.pallas_call(
        kernel,
        grid_spec=spec,
        out_shape=outs,
        compiler_params=pltpu.CompilerParams(vmem_limit_bytes=limit << 20),
        cost_estimate=pl.CostEstimate(flops=cost, transcendentals=0, bytes_accessed=1024),
    )(*args)


def sems(n):
    return pltpu.SemaphoreType.DMA((n,))


def per_device(queries, weights, beam, positives, owner):
    me = lax.axis_index("label")
    y = lax.axis_index("dp")
    rows = SLOTS * ROWS
    ranker = pltpu.with_memory_space_constraint(weights[0], pltpu.HBM)

    def swap(x):
        return lax.all_to_all(x, "label", split_axis=0, concat_axis=0, tiled=True)

    ids = jnp.arange(NDEV, dtype=jnp.int32)
    held = jnp.sum(jnp.where(owner[None, :] == ids[:, None], ids[None, :], 0), axis=1).astype(F32)
    held_rows = jnp.broadcast_to(held[:, None, None], (NDEV, SLOTS, 128)).reshape(256, 128)
    my_block = jnp.sum(jnp.where(owner == me, ids, 0)).astype(F32)
    mine = jnp.where(iota((16, 128), 1) == 0, my_block, me.astype(F32))

    pieces = whole(
        pieces_kernel,
        shape((16, 2, 8, FEAT + ROWS), BF16),
        queries.reshape(2, 16, 8, FEAT),
        positives.reshape(2, ROWS),
        beam,
        hbm=(0, 1, 2),
        scratch=(
            pltpu.VMEM((2, 16, 8, FEAT), BF16),
            pltpu.VMEM((2, ROWS), jnp.int32),
            pltpu.VMEM(beam.shape, jnp.int32),
            sems(4),
        ),
    )
    got = swap(pieces.reshape(NDEV, 8, FEAT + ROWS)).reshape(256, FEAT + ROWS)

    sent = whole(route_kernel, shape((2048, HALF), BF16), got, held_rows, limit=16)
    arrived = swap(sent.reshape(NDEV, 64, HALF))
    sel, mask, col, col_slots = whole(
        table_kernel,
        (
            shape((512, 2048), BF16),
            shape((256, 128), F32),
            shape((8, rows), jnp.int32),
            shape((SLOTS, ROWS), F32),
        ),
        got,
        held_rows,
        mine,
    )
    steps = LABELS // BIG_TILE
    w_spec = tiled((BIG_TILE, FEAT))
    lanes = shape((8, rows), F32)
    positive_rows = stepped(
        positive_kernel,
        steps,
        [fixed((8, rows)), w_spec],
        shape((rows, FEAT), BF16),
        fixed((rows, FEAT)),
        (pltpu.VMEM((FEAT, rows), F32),),
        col,
        ranker,
    )
    arrived, positive_rows, col = lax.optimization_barrier((arrived, positive_rows, col))

    parts_each = BIG_TILE // PART_TILE
    p, q, tops, stats, lse_row = stepped(
        scores_kernel,
        steps,
        [fixed((16, 2, SLOTS, 8, HALF)), fixed((8, rows)), w_spec, tiled((2 * ROWS, FEAT))],
        (
            pltpu.HBM((LABELS, rows), BF16),
            shape((rows, FEAT), BF16),
            pltpu.HBM((LABELS // PART_TILE, 8, rows), F32),
            shape((NDEV, 2 * SLOTS, ROWS), F32),
            lanes,
        ),
        (
            tiled((BIG_TILE, rows)),
            fixed((rows, FEAT)),
            tiled((parts_each, 8, rows)),
            fixed((NDEV, 2 * SLOTS, ROWS)),
            fixed((8, rows)),
        ),
        (
            pltpu.VMEM((BIG_TILE, rows), F32),
            pltpu.VMEM((8, rows), F32),
            pltpu.VMEM((8, rows), F32),
            pltpu.VMEM((SLOTS // 2, 2, ROWS), F32),
        ),
        pltpu.with_memory_space_constraint(arrived.reshape(16, 2, SLOTS, 8, HALF), pltpu.HBM),
        col,
        ranker,
        positive_rows,
    )
    all_stats = swap(stats)
    p = pltpu.with_memory_space_constraint(p, pltpu.HBM)
    tops = pltpu.with_memory_space_constraint(tops, pltpu.HBM)
    others = stepped(
        others_kernel,
        steps,
        [tiled((parts_each, 8, rows)), fixed((8, rows)), w_spec, tiled((BIG_TILE, rows))],
        pltpu.HBM((rows, FEAT), BF16),
        fixed((rows, FEAT)),
        (pltpu.VMEM((FEAT, rows), F32), pltpu.VMEM((BIG_TILE, rows), BF16)),
        tops,
        lse_row,
        ranker,
        p,
    )
    all_stats, others = lax.optimization_barrier((all_stats, others))
    norm, rest, norm_slots, loss = whole(
        normal_kernel,
        (lanes, lanes, shape((SLOTS, ROWS), F32), shape((2, ROWS), F32)),
        all_stats,
        mask,
        limit=16,
    )

    up = [(i, (i + 1) % 4) for i in range(4)]
    down = [(i, (i + 3) % 4) for i in range(4)]
    across, ahead, behind = (y + 2) % 4 * 2, (y + 1) % 4 * 2, (y + 3) % 4 * 2
    tiles = jnp.stack([across, across + 1, ahead + 1, behind, ahead, behind + 1, y * 2, y * 2 + 1])
    tiles = tiles.astype(jnp.int32)

    def table_grads(first, norm, dtypes, place=pltpu.HBM):
        n = len(dtypes)
        return stepped(
            functools.partial(table_grad_kernel, first),
            1,
            [
                fixed((rows, FEAT)),
                fixed((LABELS // PART_TILE, 8, rows)),
                fixed((8, rows)),
                fixed((8, rows)),
                fixed((8, rows)),
                *(pl.BlockSpec((TILE, rows), lambda _, t, i=i: (t[first + i], 0)) for i in range(n)),
            ],
            tuple(place((TILE, FEAT), d) for d in dtypes),
            tuple(fixed((TILE, FEAT)) for _ in dtypes),
            (),
            tiles,
            q,
            tops,
            norm,
            rest,
            col,
            *([p] * n),
            scalars=1,
        )

    far_a, far_b = table_grads(0, norm, (BF16, BF16))
    far_a, far_b, norm_slots, norm = lax.optimization_barrier((far_a, far_b, norm_slots, norm))
    via_up = lax.ppermute(far_a, "dp", up)
    via_down = lax.ppermute(far_b, "dp", down)
    part = whole(
        part_kernel,
        pltpu.HBM((16, 2, 64, HALF), BF16),
        others,
        positive_rows,
        stats,
        norm_slots,
        col_slots,
        limit=16,
    )
    part, norm = lax.optimization_barrier((part, norm))
    parts = swap(part.reshape(NDEV, 64, HALF)).reshape(2048, HALF)
    next_b, prev_a = table_grads(2, norm, (BF16, BF16))
    next_b, prev_a, norm = lax.optimization_barrier((next_b, prev_a, norm))
    from_prev_b = lax.ppermute(next_b, "dp", up)
    from_next_a = lax.ppermute(prev_a, "dp", down)
    next_a, prev_b = table_grads(4, norm, (F32, F32), shape)
    next_a, prev_b, norm = lax.optimization_barrier((next_a, prev_b, norm))
    own_a, own_b = table_grads(6, norm, (F32, F32))

    relay_up, relay_down = whole(
        relay_kernel,
        (shape((TILE, FEAT), BF16), shape((TILE, FEAT), BF16)),
        next_a,
        prev_b,
        via_up,
        via_down,
        limit=16,
        cost=50_000_000_000,
    )
    from_prev_a = lax.ppermute(relay_up, "dp", up)
    from_next_b = lax.ppermute(relay_down, "dp", down)

    homeward = whole(sum_kernel, shape((NDEV, 8, FEAT), BF16), sel, parts, limit=16)
    home = swap(homeward).reshape(16, 2, 8, FEAT)
    grad_queries = whole(home_kernel, shape((2, 16, 8, FEAT), F32), home, limit=16).reshape(256, FEAT)
    base = whole(
        base_kernel,
        shape((2 * TILE, FEAT), F32),
        own_a,
        own_b,
        from_next_a,
        from_prev_b,
        limit=16,
        cost=50_000_000_000,
    )
    base, grad_queries = lax.optimization_barrier((base, grad_queries))
    grad_table = whole(
        finish_kernel,
        shape((2 * TILE, FEAT), F32),
        base,
        from_prev_a,
        from_next_b,
        hbm_out=(0,),
        limit=16,
        scratch=(pltpu.VMEM((2 * TILE, FEAT), F32), sems(2)),
    )
    return loss.reshape(256), grad_queries, grad_table[None]

def solution(mesh):
    placed = (
        P(("dp", "label"), None),
        P("label", None, None),
        P(("dp", "label"), None),
        P(("dp", "label")),
        P(),
    )
    return jax.shard_map(
        per_device,
        mesh=mesh,
        in_specs=placed,
        out_specs=(P(("dp", "label")), P(("dp", "label"), None), P("label", "dp", None)),
        check_vma=False,
    )
```

```python
import functools

import jax
import jax.numpy as jnp
from jax import lax
from jax.experimental import pallas as pl
from jax.experimental.pallas import tpu as pltpu
from jax.sharding import PartitionSpec as P

F32 = jnp.float32
BF16 = jnp.bfloat16
NDEV = 32
SLOTS = 8
ROWS = 128
FEAT = 768
HALF = 384
LABELS = 4096
TILE = 512
BIG_TILE = 1024
PART_TILE = 256
NEG = -1e30
BIG = 1e30
LIMIT = 24

def iota(shape, dim):
    return lax.broadcasted_iota(jnp.int32, shape, dim)

def dot(a, b, dims):
    return lax.dot_general(a, b, (dims, ((), ())), preferred_element_type=F32)

def ones_where(mask):
    return jnp.where(mask, 1.0, 0.0).astype(BF16)

def slot_table(meta, held):
    n = held.shape[0]
    r = iota((256, 64), 0)
    q = iota((256, 64), 1)
    pick = ones_where((r // 8 == q % 32) & (r % 8 == 6 + q // 32))
    beams = dot(meta, pick, ((0,), (0,)))
    hit = held == beams[0:1, :]
    for k in range(1, 4):
        hit = hit | (held == beams[k : k + 1, :])
    hit = hit & (iota((n, 64), 1) >= 0)
    before = ones_where(iota((64, 64), 0) < iota((64, 64), 1))
    rank = dot(ones_where(hit), before, ((1,), (0,)))
    slot = (iota((n, 64), 0) % SLOTS).astype(F32)
    return jnp.where(hit & (rank == slot), 1.0, 0.0)

def piece_matrix(table):
    e = iota((64, 512), 1)
    spread = ones_where(iota((64, 512), 0) == e // 8)
    wide = dot(table.astype(BF16), spread, ((1,), (0,)))
    full = jnp.broadcast_to(wide[:, None, :], (256, 8, 512))
    same = iota((256, 8, 512), 1) == iota((256, 8, 512), 2) % 8
    return jnp.where(same, full, 0.0).reshape(2048, 512).astype(BF16)

def route_kernel(got_ref, held_ref, out_ref):
    got = got_ref[...]
    table = slot_table(got[:, FEAT:], held_ref[...][:, :1])
    m = piece_matrix(table)
    out = dot(m[:, :256], got[:, :HALF], ((1,), (0,)))
    out += dot(m[:, 256:], got[:, HALF:FEAT], ((1,), (0,)))
    out_ref[...] = out.astype(BF16)

def table_kernel(got_ref, held_ref, mine_ref, sel_ref, mask_ref, col_ref, slots_ref):
    meta = got_ref[...][:, FEAT:]
    table = slot_table(meta, held_ref[...][:, :1])
    sel_ref[...] = piece_matrix(table).T
    mine = mine_ref[...]
    own = slot_table(meta, mine[:, 0:1])
    row = iota((16, 64), 0)
    q = iota((16, 64), 1).astype(F32)
    home = jnp.where(q == (row.astype(F32) - 8.0) * 32.0 + mine[:, 1:2], 1.0, 0.0)
    own = jnp.where(row < 8, own, jnp.where(row < 10, home, 0.0)).astype(BF16)
    mask = dot(table.astype(BF16), own, ((1,), (1,)))
    mask_ref[...] = jnp.concatenate([mask, jnp.zeros((256, 112), F32)], axis=1)
    qq = iota((64, 256), 0)
    rr = iota((64, 256), 1)
    part = []
    for c in range(3):
        pick = ones_where((rr // 8 == qq % 32) & (rr % 8 == 3 * (qq // 32) + c))
        where_c = dot(own, pick, ((1,), (0,))).astype(BF16)
        part.append(dot(where_c, meta, ((1,), (0,))))
    inside = part[0] == mine[:, 0:1] + 1.0
    col = jnp.where(inside, part[1] * 64.0 + part[2], -1.0)
    slots_ref[...] = col[:SLOTS]
    for s in range(SLOTS):
        piece = col[s : s + 1].astype(jnp.int32)
        col_ref[:, s * ROWS : (s + 1) * ROWS] = jnp.broadcast_to(piece, (8, ROWS))

def start(copies):
    for c in copies:
        c.start()
    return copies

def pieces_kernel(q_hbm, pos_hbm, beam_hbm, out_ref, q_ref, pos_ref, beam_ref, sems):
    small = start(
        [
            pltpu.make_async_copy(pos_hbm, pos_ref, sems.at[0]),
            pltpu.make_async_copy(beam_hbm, beam_ref, sems.at[1]),
        ]
    )
    large = start(
        [
            pltpu.make_async_copy(q_hbm.at[:, pl.ds(8 * i, 8)], q_ref.at[:, pl.ds(8 * i, 8)], sems.at[2 + i])
            for i in range(2)
        ]
    )
    for c in small:
        c.wait()
    pos = pos_ref[...]
    beam = beam_ref[...]
    high, low = (pos >> 12) + 1, pos & (LABELS - 1)
    codes = (high, low >> 6, low & 63)
    row = iota((8, ROWS), 0)
    lane = iota((8, ROWS), 1)
    meta = jnp.full((8, ROWS), -1, jnp.int32)
    for b in range(2):
        for c in range(3):
            meta = jnp.where(row == 3 * b + c, codes[c][b : b + 1, :], meta)
        for k in range(beam.shape[1]):
            meta = jnp.where((row == 6 + b) & (lane == k), beam[b : b + 1, k : k + 1], meta)
    meta = meta.astype(F32).astype(BF16)
    out_ref[:, :, :, FEAT:] = jnp.broadcast_to(meta[None, None], (16, 2, 8, ROWS))
    for i in range(2):
        large[i].wait()
        g = slice(8 * i, 8 * i + 8)
        for h in range(2):
            for b in range(2):
                out_ref[g, h, :, b * HALF : (b + 1) * HALF] = q_ref[b, g, :, h * HALF : (h + 1) * HALF]

def label_iota(rows):
    return iota((PART_TILE, rows), 0).reshape(PART_TILE // 8, 8, rows)


def by_slot(lanes):
    row = iota((SLOTS, ROWS), 0)
    out = jnp.zeros((SLOTS, ROWS), F32)
    for s in range(SLOTS):
        out = jnp.where(row == s, lanes[:, s * ROWS : (s + 1) * ROWS], out)
    return out

def scores_kernel(got_ref, col_ref, w_ref, r_ref, p_ref, q_ref, top_ref, stat_ref, row_ref, s_ref, high, total, found):
    step = pl.program_id(0)
    rows = s_ref.shape[1]

    @pl.when(step == 0)
    def _():
        for g in range(16):
            for h in range(2):
                for s in range(SLOTS):
                    here = slice(s * ROWS + g * 8, s * ROWS + g * 8 + 8)
                    q_ref[here, h * HALF : (h + 1) * HALF] = got_ref[g, h, s]
        high[...] = jnp.full_like(high, NEG)
        total[...] = jnp.zeros_like(total)

    n = BIG_TILE // PART_TILE
    top, tot = high[...], total[...]
    for k in range(n + 1):
        if k < n:
            here = slice(k * PART_TILE, (k + 1) * PART_TILE)
            s_ref[here, :] = dot(w_ref[here, :], q_ref[...], ((1,), (1,)))
        if k > 0:
            here = slice((k - 1) * PART_TILE, k * PART_TILE)
            s = s_ref[here, :].reshape(PART_TILE // 8, 8, rows)
            best = jnp.max(jnp.max(s, axis=0), axis=0, keepdims=True)
            best = jnp.broadcast_to(best, (8, rows))
            e = jnp.exp(s - best[None])
            target = label_iota(rows) == (col_ref[...] - (step * BIG_TILE + (k - 1) * PART_TILE))[None]
            p_ref[here, :] = jnp.where(target, 0.0, e).reshape(PART_TILE, rows).astype(BF16)
            new = jnp.maximum(top, best)
            tot = tot * jnp.exp(top - new) + jnp.sum(e, axis=0) * jnp.exp(best - new)
            top = new
            top_ref[k - 1] = best
    high[...], total[...] = top, tot

    two = 2 * ROWS
    mine = q_ref[pl.ds(pl.multiple_of(step * two, two), two), :].astype(F32) * r_ref[...].astype(F32)
    folded = mine[:, :ROWS]
    for c in range(1, FEAT // ROWS):
        folded += mine[:, c * ROWS : (c + 1) * ROWS]
    for i in range(2):
        one = jnp.sum(folded[i * ROWS : (i + 1) * ROWS].T, axis=0, keepdims=True)
        found[step, i : i + 1, :] = one

    @pl.when(step == pl.num_programs(0) - 1)
    def _():
        lse = top[0:1, :] + jnp.log(jnp.sum(tot, axis=0, keepdims=True))
        row_ref[...] = jnp.broadcast_to(lse, (8, rows))
        stat_ref[:, :SLOTS, :] = jnp.broadcast_to(by_slot(lse)[None], (NDEV, SLOTS, ROWS))
        for i in range(SLOTS // 2):
            here = slice(SLOTS + 2 * i, SLOTS + 2 * i + 2)
            stat_ref[:, here, :] = jnp.broadcast_to(found[i][None], (NDEV, 2, ROWS))


def normal_kernel(stat_ref, mask_ref, norm_ref, rest_ref, slots_ref, loss_ref):
    lse = stat_ref[:, :SLOTS, :].reshape(NDEV * SLOTS, ROWS)
    found = stat_ref[:, SLOTS:, :].reshape(NDEV * SLOTS, ROWS)
    mask = mask_ref[...]
    for s in range(SLOTS + 2):
        use = mask[:, s : s + 1] > 0.5
        kept = jnp.where(use, lse, NEG)
        high = jnp.max(kept, axis=0, keepdims=True)
        tot = jnp.sum(jnp.where(use, jnp.exp(kept - high), 0.0), axis=0, keepdims=True)
        value = jnp.where(high > 0.5 * NEG, high + jnp.log(tot), BIG)
        positive = jnp.sum(jnp.where(use, found, 0.0), axis=0, keepdims=True)
        if s < SLOTS:
            here = slice(s * ROWS, (s + 1) * ROWS)
            norm_ref[:, here] = jnp.broadcast_to(value, (8, ROWS))
            rest_ref[:, here] = jnp.broadcast_to(jnp.exp(positive - value) - 1.0, (8, ROWS))
            slots_ref[s : s + 1, :] = value
        else:
            loss_ref[s - SLOTS : s - SLOTS + 1, :] = value - positive


def rows_from(acc, out_ref):
    for s in range(SLOTS):
        here = slice(s * ROWS, (s + 1) * ROWS)
        out_ref[here, :] = acc[:, here].T.astype(out_ref.dtype)


def add_to(acc, term, first):
    @pl.when(first)
    def _():
        acc[...] = term

    @pl.when(jnp.logical_not(first))
    def _():
        acc[...] += term


def positive_kernel(col_ref, w_ref, out_ref, acc):
    step = pl.program_id(0)
    target = iota((BIG_TILE, acc.shape[1]), 0) + step * BIG_TILE == col_ref[0:1, :]
    add_to(acc, dot(w_ref[...], ones_where(target), ((0,), (0,))), step == 0)

    @pl.when(step == pl.num_programs(0) - 1)
    def _():
        rows_from(acc, out_ref)


def others_kernel(top_ref, row_ref, w_ref, p_ref, out_ref, acc, scaled):
    step = pl.program_id(0)
    for i in range(BIG_TILE // PART_TILE):
        scale = jnp.exp(top_ref[i] - row_ref[...])
        here = slice(i * PART_TILE, (i + 1) * PART_TILE)
        p = p_ref[here, :].astype(F32).reshape(PART_TILE // 8, 8, scale.shape[1])
        scaled[here, :] = (p * scale[None]).reshape(PART_TILE, scale.shape[1]).astype(BF16)
    add_to(acc, dot(w_ref[...], scaled[...], ((0,), (0,))), step == 0)

    @pl.when(step == pl.num_programs(0) - 1)
    def _():
        rows_from(acc, out_ref)


def part_kernel(u_ref, r_ref, stat_ref, norm_ref, col_ref, out_ref):
    norm = norm_ref[...]
    scale = jnp.exp(stat_ref[0, :SLOTS, :] - norm).T
    rest = jnp.where(col_ref[...] >= 0.0, jnp.exp(stat_ref[0, SLOTS:, :] - norm) - 1.0, 0.0).T
    for s in range(SLOTS):
        u = u_ref[s * ROWS : (s + 1) * ROWS, :].astype(F32)
        r = r_ref[s * ROWS : (s + 1) * ROWS, :].astype(F32)
        part = (scale[:, s : s + 1] * u + rest[:, s : s + 1] * r).astype(BF16).reshape(16, 8, FEAT)
        for h in range(2):
            out_ref[:, h, s * 8 : (s + 1) * 8, :] = part[:, :, h * HALF : (h + 1) * HALF]


def table_grad_kernel(base, tiles_ref, q_ref, top_ref, norm_ref, rest_ref, col_ref, *refs):
    n = len(refs) // 2
    for i in range(n):
        p_ref, out_ref = refs[i], refs[n + i]
        tile = tiles_ref[base + i]
        for k in range(TILE // PART_TILE):
            here = slice(k * PART_TILE, (k + 1) * PART_TILE)
            scale = jnp.exp(top_ref[tile * (TILE // PART_TILE) + k] - norm_ref[...])
            rows = scale.shape[1]
            p = p_ref[here, :].astype(F32).reshape(PART_TILE // 8, 8, rows)
            target = label_iota(rows) == (col_ref[...] - (tile * TILE + k * PART_TILE))[None]
            slope = jnp.where(target, rest_ref[...][None], p * scale[None])
            slope = slope.reshape(PART_TILE, rows).astype(BF16)
            out_ref[here, :] = dot(slope, q_ref[...], ((1,), (0,))).astype(out_ref.dtype)


def sum_kernel(sel_ref, parts_ref, out_ref):
    out = dot(sel_ref[...], parts_ref[...], ((1,), (0,))).astype(BF16)
    for b in range(2):
        out_ref[:, :, b * HALF : (b + 1) * HALF] = out[b * 256 : (b + 1) * 256].reshape(NDEV, 8, HALF)

def home_kernel(got_ref, out_ref):
    for h in range(2):
        for b in range(2):
            out_ref[b, :, :, h * HALF : (h + 1) * HALF] = got_ref[:, h, :, b * HALF : (b + 1) * HALF].astype(F32)

def relay_kernel(up_ref, down_ref, got_up_ref, got_down_ref, out_up_ref, out_down_ref):
    out_up_ref[...] = (up_ref[...] + got_up_ref[...].astype(F32)).astype(BF16)
    out_down_ref[...] = (down_ref[...] + got_down_ref[...].astype(F32)).astype(BF16)


def base_kernel(own_a_ref, own_b_ref, a_ref, b_ref, out_ref):
    out_ref[:TILE, :] = own_a_ref[...] + a_ref[...].astype(F32)
    out_ref[TILE:, :] = own_b_ref[...] + b_ref[...].astype(F32)


def finish_kernel(base_ref, a_ref, b_ref, out_hbm, out_v, out_sems):
    copies = []
    for i, ref in enumerate((a_ref, b_ref)):
        here = pl.ds(i * TILE, TILE)
        out_v[i * TILE : (i + 1) * TILE, :] = base_ref[i * TILE : (i + 1) * TILE, :] + ref[...].astype(F32)
        c = pltpu.make_async_copy(out_v.at[here], out_hbm.at[here], out_sems.at[i])
        c.start()
        copies.append(c)
    for c in copies:
        c.wait()


def shape(dims, dtype):
    return jax.ShapeDtypeStruct(dims, dtype)

def whole(kernel, out, *args, hbm=(), smem=(), hbm_out=(), limit=60, cost=1024, scratch=()):
    def place(i, far, scalar=()):
        space = pltpu.HBM if i in far else pltpu.SMEM if i in scalar else pltpu.VMEM
        return pl.BlockSpec(memory_space=space)

    single = not isinstance(out, tuple)
    outs = (out,) if single else out
    results = pl.pallas_call(
        kernel,
        out_shape=outs,
        in_specs=[place(i, hbm, smem) for i in range(len(args))],
        out_specs=tuple(place(i, hbm_out) for i in range(len(outs))),
        scratch_shapes=list(scratch),
        compiler_params=pltpu.CompilerParams(vmem_limit_bytes=limit << 20),
        cost_estimate=pl.CostEstimate(flops=cost, transcendentals=0, bytes_accessed=1024),
    )(*args)
    return results[0] if single else results

def fixed(dims):
    return pl.BlockSpec(dims, lambda *_: (0,) * len(dims))


def tiled(dims):
    return pl.BlockSpec(dims, lambda i, *_: (i,) + (0,) * (len(dims) - 1))


def stepped(kernel, grid, in_specs, outs, out_specs, scratch, *args, limit=LIMIT, scalars=0, cost=1024):
    spec = pltpu.PrefetchScalarGridSpec(
        num_scalar_prefetch=scalars,
        grid=(grid,),
        in_specs=in_specs,
        out_specs=out_specs,
        scratch_shapes=list(scratch),
    )
    return pl.pallas_call(
        kernel,
        grid_spec=spec,
        out_shape=outs,
        compiler_params=pltpu.CompilerParams(vmem_limit_bytes=limit << 20),
        cost_estimate=pl.CostEstimate(flops=cost, transcendentals=0, bytes_accessed=1024),
    )(*args)


def sems(n):
    return pltpu.SemaphoreType.DMA((n,))


def per_device(queries, weights, beam, positives, owner):
    me = lax.axis_index("label")
    y = lax.axis_index("dp")
    rows = SLOTS * ROWS
    ranker = pltpu.with_memory_space_constraint(weights[0], pltpu.HBM)

    def swap(x):
        return lax.all_to_all(x, "label", split_axis=0, concat_axis=0, tiled=True)

    ids = jnp.arange(NDEV, dtype=jnp.int32)
    held = jnp.sum(jnp.where(owner[None, :] == ids[:, None], ids[None, :], 0), axis=1).astype(F32)
    held_rows = jnp.broadcast_to(held[:, None, None], (NDEV, SLOTS, 128)).reshape(256, 128)
    my_block = jnp.sum(jnp.where(owner == me, ids, 0)).astype(F32)
    mine = jnp.where(iota((16, 128), 1) == 0, my_block, me.astype(F32))

    pieces = whole(
        pieces_kernel,
        shape((16, 2, 8, FEAT + ROWS), BF16),
        queries.reshape(2, 16, 8, FEAT),
        positives.reshape(2, ROWS),
        beam,
        hbm=(0, 1, 2),
        scratch=(
            pltpu.VMEM((2, 16, 8, FEAT), BF16),
            pltpu.VMEM((2, ROWS), jnp.int32),
            pltpu.VMEM(beam.shape, jnp.int32),
            sems(4),
        ),
    )
    got = swap(pieces.reshape(NDEV, 8, FEAT + ROWS)).reshape(256, FEAT + ROWS)

    sent = whole(route_kernel, shape((2048, HALF), BF16), got, held_rows, limit=16)
    arrived = swap(sent.reshape(NDEV, 64, HALF))
    sel, mask, col, col_slots = whole(
        table_kernel,
        (
            pltpu.HBM((512, 2048), BF16),
            pltpu.HBM((256, 128), F32),
            shape((8, rows), jnp.int32),
            shape((SLOTS, ROWS), F32),
        ),
        got,
        held_rows,
        mine,
    )
    steps = LABELS // BIG_TILE
    w_spec = tiled((BIG_TILE, FEAT))
    lanes = shape((8, rows), F32)
    positive_rows = stepped(
        positive_kernel,
        steps,
        [fixed((8, rows)), w_spec],
        shape((rows, FEAT), BF16),
        fixed((rows, FEAT)),
        (pltpu.VMEM((FEAT, rows), F32),),
        col,
        ranker,
    )
    arrived, positive_rows, col = lax.optimization_barrier((arrived, positive_rows, col))

    parts_each = BIG_TILE // PART_TILE
    p, q, tops, stats, lse_row = stepped(
        scores_kernel,
        steps,
        [fixed((16, 2, SLOTS, 8, HALF)), fixed((8, rows)), w_spec, tiled((2 * ROWS, FEAT))],
        (
            pltpu.HBM((LABELS, rows), BF16),
            shape((rows, FEAT), BF16),
            pltpu.HBM((LABELS // PART_TILE, 8, rows), F32),
            shape((NDEV, 2 * SLOTS, ROWS), F32),
            lanes,
        ),
        (
            tiled((BIG_TILE, rows)),
            fixed((rows, FEAT)),
            tiled((parts_each, 8, rows)),
            fixed((NDEV, 2 * SLOTS, ROWS)),
            fixed((8, rows)),
        ),
        (
            pltpu.VMEM((BIG_TILE, rows), F32),
            pltpu.VMEM((8, rows), F32),
            pltpu.VMEM((8, rows), F32),
            pltpu.VMEM((SLOTS // 2, 2, ROWS), F32),
        ),
        pltpu.with_memory_space_constraint(arrived.reshape(16, 2, SLOTS, 8, HALF), pltpu.HBM),
        col,
        ranker,
        positive_rows,
    )
    all_stats = swap(stats)
    p = pltpu.with_memory_space_constraint(p, pltpu.HBM)
    tops = pltpu.with_memory_space_constraint(tops, pltpu.HBM)
    others = stepped(
        others_kernel,
        steps,
        [tiled((parts_each, 8, rows)), fixed((8, rows)), w_spec, tiled((BIG_TILE, rows))],
        pltpu.HBM((rows, FEAT), BF16),
        fixed((rows, FEAT)),
        (pltpu.VMEM((FEAT, rows), F32), pltpu.VMEM((BIG_TILE, rows), BF16)),
        tops,
        lse_row,
        ranker,
        p,
    )
    all_stats, others = lax.optimization_barrier((all_stats, others))
    norm, rest, norm_slots, loss = whole(
        normal_kernel,
        (lanes, lanes, shape((SLOTS, ROWS), F32), shape((2, ROWS), F32)),
        all_stats,
        pltpu.with_memory_space_constraint(mask, pltpu.HBM),
        limit=16,
    )

    up = [(i, (i + 1) % 4) for i in range(4)]
    down = [(i, (i + 3) % 4) for i in range(4)]
    across, ahead, behind = (y + 2) % 4 * 2, (y + 1) % 4 * 2, (y + 3) % 4 * 2
    tiles = jnp.stack([across, across + 1, ahead + 1, behind, ahead, behind + 1, y * 2, y * 2 + 1])
    tiles = tiles.astype(jnp.int32)

    def table_grads(first, norm, dtypes, place=pltpu.HBM):
        n = len(dtypes)
        return stepped(
            functools.partial(table_grad_kernel, first),
            1,
            [
                fixed((rows, FEAT)),
                fixed((LABELS // PART_TILE, 8, rows)),
                fixed((8, rows)),
                fixed((8, rows)),
                fixed((8, rows)),
                *(pl.BlockSpec((TILE, rows), lambda _, t, i=i: (t[first + i], 0)) for i in range(n)),
            ],
            tuple(place((TILE, FEAT), d) for d in dtypes),
            tuple(fixed((TILE, FEAT)) for _ in dtypes),
            (),
            tiles,
            q,
            tops,
            norm,
            rest,
            col,
            *([p] * n),
            scalars=1,
        )

    far_a, far_b = table_grads(0, norm, (BF16, BF16))
    far_a, far_b, norm_slots, norm = lax.optimization_barrier((far_a, far_b, norm_slots, norm))
    via_up = lax.ppermute(far_a, "dp", up)
    via_down = lax.ppermute(far_b, "dp", down)
    part = whole(
        part_kernel,
        pltpu.HBM((16, 2, 64, HALF), BF16),
        others,
        positive_rows,
        stats,
        norm_slots,
        col_slots,
        limit=16,
    )
    part, norm = lax.optimization_barrier((part, norm))
    parts = swap(part.reshape(NDEV, 64, HALF)).reshape(2048, HALF)
    next_b, prev_a = table_grads(2, norm, (BF16, BF16))
    next_b, prev_a, norm = lax.optimization_barrier((next_b, prev_a, norm))
    from_prev_b = lax.ppermute(next_b, "dp", up)
    from_next_a = lax.ppermute(prev_a, "dp", down)
    next_a, prev_b = table_grads(4, norm, (F32, F32), shape)

    relay_up, relay_down = whole(
        relay_kernel,
        (shape((TILE, FEAT), BF16), shape((TILE, FEAT), BF16)),
        next_a,
        prev_b,
        via_up,
        via_down,
        limit=16,
        cost=50_000_000_000,
    )
    relay_up, relay_down, norm = lax.optimization_barrier((relay_up, relay_down, norm))
    own_a, own_b = table_grads(6, norm, (F32, F32))
    from_prev_a = lax.ppermute(relay_up, "dp", up)
    from_next_b = lax.ppermute(relay_down, "dp", down)

    sel = pltpu.with_memory_space_constraint(sel, pltpu.HBM)
    homeward = whole(sum_kernel, shape((NDEV, 8, FEAT), BF16), sel, parts, limit=16)
    home = swap(homeward)
    base = whole(
        base_kernel,
        shape((2 * TILE, FEAT), F32),
        own_a,
        own_b,
        from_next_a,
        from_prev_b,
        limit=16,
        cost=8_000_000_000,
    )
    grad_table = whole(
        finish_kernel,
        shape((2 * TILE, FEAT), F32),
        base,
        from_prev_a,
        from_next_b,
        hbm_out=(0,),
        limit=16,
        scratch=(pltpu.VMEM((2 * TILE, FEAT), F32), sems(2)),
    )
    home, grad_table = lax.optimization_barrier((home, grad_table))
    grad_queries = whole(
        home_kernel, shape((2, 16, 8, FEAT), F32), home.reshape(16, 2, 8, FEAT), limit=16
    ).reshape(256, FEAT)
    return loss.reshape(256), grad_queries, grad_table[None]

def solution(mesh):
    placed = (
        P(("dp", "label"), None),
        P("label", None, None),
        P(("dp", "label"), None),
        P(("dp", "label")),
        P(),
    )
    return jax.shard_map(
        per_device,
        mesh=mesh,
        in_specs=placed,
        out_specs=(P(("dp", "label")), P(("dp", "label"), None), P("label", "dp", None)),
        check_vma=False,
    )
```

```python
import functools

import jax
import jax.numpy as jnp
from jax import lax
from jax.experimental import pallas as pl
from jax.experimental.pallas import tpu as pltpu
from jax.sharding import PartitionSpec as P

F32 = jnp.float32
BF16 = jnp.bfloat16
NDEV = 32
SLOTS = 8
ROWS = 128
FEAT = 768
HALF = 384
LABELS = 4096
TILE = 512
BIG_TILE = 1024
PART_TILE = 256
NEG = -1e30
BIG = 1e30
LIMIT = 24

def iota(shape, dim):
    return lax.broadcasted_iota(jnp.int32, shape, dim)

def dot(a, b, dims):
    return lax.dot_general(a, b, (dims, ((), ())), preferred_element_type=F32)

def ones_where(mask):
    return jnp.where(mask, 1.0, 0.0).astype(BF16)

def slot_table(meta, held):
    n = held.shape[0]
    r = iota((256, 64), 0)
    q = iota((256, 64), 1)
    pick = ones_where((r // 8 == q % 32) & (r % 8 == 6 + q // 32))
    beams = dot(meta, pick, ((0,), (0,)))
    hit = held == beams[0:1, :]
    for k in range(1, 4):
        hit = hit | (held == beams[k : k + 1, :])
    hit = hit & (iota((n, 64), 1) >= 0)
    before = ones_where(iota((64, 64), 0) < iota((64, 64), 1))
    rank = dot(ones_where(hit), before, ((1,), (0,)))
    slot = (iota((n, 64), 0) % SLOTS).astype(F32)
    return jnp.where(hit & (rank == slot), 1.0, 0.0)

def piece_matrix(table):
    e = iota((64, 512), 1)
    spread = ones_where(iota((64, 512), 0) == e // 8)
    wide = dot(table.astype(BF16), spread, ((1,), (0,)))
    full = jnp.broadcast_to(wide[:, None, :], (256, 8, 512))
    same = iota((256, 8, 512), 1) == iota((256, 8, 512), 2) % 8
    return jnp.where(same, full, 0.0).reshape(2048, 512).astype(BF16)

def route_kernel(got_ref, held_ref, out_ref):
    got = got_ref[...]
    table = slot_table(got[:, FEAT:], held_ref[...][:, :1])
    m = piece_matrix(table)
    out = dot(m[:, :256], got[:, :HALF], ((1,), (0,)))
    out += dot(m[:, 256:], got[:, HALF:FEAT], ((1,), (0,)))
    out_ref[...] = out.astype(BF16)

def table_kernel(got_ref, held_ref, mine_ref, sel_ref, mask_ref, col_ref, slots_ref):
    meta = got_ref[...][:, FEAT:]
    table = slot_table(meta, held_ref[...][:, :1])
    sel_ref[...] = piece_matrix(table).T
    mine = mine_ref[...]
    own = slot_table(meta, mine[:, 0:1])
    row = iota((16, 64), 0)
    q = iota((16, 64), 1).astype(F32)
    home = jnp.where(q == (row.astype(F32) - 8.0) * 32.0 + mine[:, 1:2], 1.0, 0.0)
    own = jnp.where(row < 8, own, jnp.where(row < 10, home, 0.0)).astype(BF16)
    mask = dot(table.astype(BF16), own, ((1,), (1,)))
    mask_ref[...] = jnp.concatenate([mask, jnp.zeros((256, 112), F32)], axis=1)
    qq = iota((64, 256), 0)
    rr = iota((64, 256), 1)
    part = []
    for c in range(3):
        pick = ones_where((rr // 8 == qq % 32) & (rr % 8 == 3 * (qq // 32) + c))
        where_c = dot(own, pick, ((1,), (0,))).astype(BF16)
        part.append(dot(where_c, meta, ((1,), (0,))))
    inside = part[0] == mine[:, 0:1] + 1.0
    col = jnp.where(inside, part[1] * 64.0 + part[2], -1.0)
    slots_ref[...] = col[:SLOTS]
    for s in range(SLOTS):
        piece = col[s : s + 1].astype(jnp.int32)
        col_ref[:, s * ROWS : (s + 1) * ROWS] = jnp.broadcast_to(piece, (8, ROWS))

def start(copies):
    for c in copies:
        c.start()
    return copies

def pieces_kernel(q_hbm, pos_hbm, beam_hbm, out_ref, q_ref, pos_ref, beam_ref, sems):
    small = start(
        [
            pltpu.make_async_copy(pos_hbm, pos_ref, sems.at[0]),
            pltpu.make_async_copy(beam_hbm, beam_ref, sems.at[1]),
        ]
    )
    large = start(
        [
            pltpu.make_async_copy(q_hbm.at[:, pl.ds(8 * i, 8)], q_ref.at[:, pl.ds(8 * i, 8)], sems.at[2 + i])
            for i in range(2)
        ]
    )
    for c in small:
        c.wait()
    pos = pos_ref[...]
    beam = beam_ref[...]
    high, low = (pos >> 12) + 1, pos & (LABELS - 1)
    codes = (high, low >> 6, low & 63)
    row = iota((8, ROWS), 0)
    lane = iota((8, ROWS), 1)
    meta = jnp.full((8, ROWS), -1, jnp.int32)
    for b in range(2):
        for c in range(3):
            meta = jnp.where(row == 3 * b + c, codes[c][b : b + 1, :], meta)
        for k in range(beam.shape[1]):
            meta = jnp.where((row == 6 + b) & (lane == k), beam[b : b + 1, k : k + 1], meta)
    meta = meta.astype(F32).astype(BF16)
    out_ref[:, :, :, FEAT:] = jnp.broadcast_to(meta[None, None], (16, 2, 8, ROWS))
    for i in range(2):
        large[i].wait()
        g = slice(8 * i, 8 * i + 8)
        for h in range(2):
            for b in range(2):
                out_ref[g, h, :, b * HALF : (b + 1) * HALF] = q_ref[b, g, :, h * HALF : (h + 1) * HALF]

def label_iota(rows):
    return iota((PART_TILE, rows), 0).reshape(PART_TILE // 8, 8, rows)


def by_slot(lanes):
    row = iota((SLOTS, ROWS), 0)
    out = jnp.zeros((SLOTS, ROWS), F32)
    for s in range(SLOTS):
        out = jnp.where(row == s, lanes[:, s * ROWS : (s + 1) * ROWS], out)
    return out

def scores_kernel(got_ref, col_ref, w_ref, p_ref, q_ref, top_ref, stat_ref, row_ref, s_ref, high, total, found):
    step = pl.program_id(0)
    rows = s_ref.shape[1]

    @pl.when(step == 0)
    def _():
        for g in range(16):
            for h in range(2):
                for s in range(SLOTS):
                    here = slice(s * ROWS + g * 8, s * ROWS + g * 8 + 8)
                    q_ref[here, h * HALF : (h + 1) * HALF] = got_ref[g, h, s]
        high[...] = jnp.full_like(high, NEG)
        total[...] = jnp.zeros_like(total)
        found[...] = jnp.zeros_like(found)

    n = BIG_TILE // PART_TILE
    top, tot, pick = high[...], total[...], found[...]
    for k in range(n + 1):
        if k < n:
            here = slice(k * PART_TILE, (k + 1) * PART_TILE)
            s_ref[here, :] = dot(w_ref[here, :], q_ref[...], ((1,), (1,)))
        if k > 0:
            here = slice((k - 1) * PART_TILE, k * PART_TILE)
            s = s_ref[here, :]
            target = iota(s.shape, 0) + (step * BIG_TILE + (k - 1) * PART_TILE) == col_ref[0:1, :]
            pick += jnp.sum(jnp.where(target, s, 0.0).reshape(PART_TILE // 8, 8, rows), axis=0)
            best = jnp.max(jnp.max(s.reshape(PART_TILE // 8, 8, rows), axis=0), axis=0, keepdims=True)
            best = jnp.broadcast_to(best, (8, rows))
            e = jnp.exp(s - best[0:1, :])
            p_ref[here, :] = jnp.where(target, 0.0, e).astype(BF16)
            new = jnp.maximum(top, best)
            add = jnp.sum(e.reshape(PART_TILE // 8, 8, rows), axis=0)
            tot = tot * jnp.exp(top - new) + add * jnp.exp(best - new)
            top = new
            top_ref[k - 1] = best
    high[...], total[...], found[...] = top, tot, pick

    @pl.when(step == pl.num_programs(0) - 1)
    def _():
        lse = top[0:1, :] + jnp.log(jnp.sum(tot, axis=0, keepdims=True))
        row_ref[...] = jnp.broadcast_to(lse, (8, rows))
        chosen = jnp.sum(pick, axis=0, keepdims=True)
        stat_ref[:, :SLOTS, :] = jnp.broadcast_to(by_slot(lse)[None], (NDEV, SLOTS, ROWS))
        stat_ref[:, SLOTS:, :] = jnp.broadcast_to(by_slot(chosen)[None], (NDEV, SLOTS, ROWS))


def normal_kernel(stat_ref, mask_ref, norm_ref, rest_ref, slots_ref, loss_ref):
    lse = stat_ref[:, :SLOTS, :].reshape(NDEV * SLOTS, ROWS)
    found = stat_ref[:, SLOTS:, :].reshape(NDEV * SLOTS, ROWS)
    mask = mask_ref[...]
    for s in range(SLOTS + 2):
        use = mask[:, s : s + 1] > 0.5
        kept = jnp.where(use, lse, NEG)
        high = jnp.max(kept, axis=0, keepdims=True)
        tot = jnp.sum(jnp.where(use, jnp.exp(kept - high), 0.0), axis=0, keepdims=True)
        value = jnp.where(high > 0.5 * NEG, high + jnp.log(tot), BIG)
        positive = jnp.sum(jnp.where(use, found, 0.0), axis=0, keepdims=True)
        if s < SLOTS:
            here = slice(s * ROWS, (s + 1) * ROWS)
            norm_ref[:, here] = jnp.broadcast_to(value, (8, ROWS))
            rest_ref[:, here] = jnp.broadcast_to(jnp.exp(positive - value) - 1.0, (8, ROWS))
            slots_ref[s : s + 1, :] = value
        else:
            loss_ref[s - SLOTS : s - SLOTS + 1, :] = value - positive


def rows_from(acc, out_ref):
    for s in range(SLOTS):
        here = slice(s * ROWS, (s + 1) * ROWS)
        out_ref[here, :] = acc[:, here].T.astype(out_ref.dtype)


def add_to(acc, term, first):
    @pl.when(first)
    def _():
        acc[...] = term

    @pl.when(jnp.logical_not(first))
    def _():
        acc[...] += term


def positive_kernel(col_ref, w_ref, out_ref, acc):
    step = pl.program_id(0)
    target = iota((BIG_TILE, acc.shape[1]), 0) + step * BIG_TILE == col_ref[0:1, :]
    add_to(acc, dot(w_ref[...], ones_where(target), ((0,), (0,))), step == 0)

    @pl.when(step == pl.num_programs(0) - 1)
    def _():
        rows_from(acc, out_ref)


def scaled_tile(p_ref, top_ref, row_ref, out_ref):
    rows = out_ref.shape[1]
    for i in range(BIG_TILE // PART_TILE):
        scale = jnp.exp(top_ref[i] - row_ref[...])
        here = slice(i * PART_TILE, (i + 1) * PART_TILE)
        p = p_ref[here, :].astype(F32).reshape(PART_TILE // 8, 8, rows)
        out_ref[here, :] = (p * scale[None]).reshape(PART_TILE, rows).astype(BF16)


def others_kernel(top_ref, row_ref, w_ref, p_ref, acc_ref, scaled):
    scaled_tile(p_ref, top_ref, row_ref, scaled)
    add_to(acc_ref, dot(w_ref[...], scaled[...], ((0,), (0,))), pl.program_id(0) == 0)


def part_kernel(top_ref, row_ref, w_ref, p_ref, half_ref, r_ref, stat_ref, norm_ref, col_ref, out_ref, acc, scaled):
    step = pl.program_id(0)

    @pl.when(step == 0)
    def _():
        acc[...] = half_ref[...]

    scaled_tile(p_ref, top_ref, row_ref, scaled)
    acc[...] += dot(w_ref[...], scaled[...], ((0,), (0,)))

    @pl.when(step == pl.num_programs(0) - 1)
    def _():
        norm = norm_ref[...]
        scale = jnp.exp(stat_ref[0, :SLOTS, :] - norm).T
        rest = jnp.where(col_ref[...] >= 0.0, jnp.exp(stat_ref[0, SLOTS:, :] - norm) - 1.0, 0.0).T
        for s in range(SLOTS):
            here = slice(s * ROWS, (s + 1) * ROWS)
            u = acc[:, here].T
            r = r_ref[here, :].astype(F32)
            part = (scale[:, s : s + 1] * u + rest[:, s : s + 1] * r).astype(BF16).reshape(16, 8, FEAT)
            for h in range(2):
                out_ref[:, h, s * 8 : (s + 1) * 8, :] = part[:, :, h * HALF : (h + 1) * HALF]


def table_grad_kernel(base, tiles_ref, q_ref, norm_ref, rest_ref, col_ref, *refs):
    n = len(refs) // 3
    for i in range(n):
        p_ref, top_ref, out_ref = refs[i], refs[n + i], refs[2 * n + i]
        tile = tiles_ref[base + i]
        for k in range(TILE // PART_TILE):
            here = slice(k * PART_TILE, (k + 1) * PART_TILE)
            scale = jnp.exp(top_ref[k] - norm_ref[...])
            rows = scale.shape[1]
            p = p_ref[here, :].astype(F32).reshape(PART_TILE // 8, 8, rows)
            target = label_iota(rows) == (col_ref[...] - (tile * TILE + k * PART_TILE))[None]
            slope = jnp.where(target, rest_ref[...][None], p * scale[None])
            slope = slope.reshape(PART_TILE, rows).astype(BF16)
            out_ref[here, :] = dot(slope, q_ref[...], ((1,), (0,))).astype(out_ref.dtype)


def sum_kernel(sel_ref, parts_ref, out_ref):
    out = dot(sel_ref[...], parts_ref[...], ((1,), (0,))).astype(BF16)
    for b in range(2):
        out_ref[:, :, b * HALF : (b + 1) * HALF] = out[b * 256 : (b + 1) * 256].reshape(NDEV, 8, HALF)

def home_kernel(got_ref, out_ref):
    for h in range(2):
        for b in range(2):
            out_ref[b, :, :, h * HALF : (h + 1) * HALF] = got_ref[:, h, :, b * HALF : (b + 1) * HALF].astype(F32)

def relay_kernel(up_ref, down_ref, got_up_ref, got_down_ref, out_up_ref, out_down_ref):
    out_up_ref[...] = (up_ref[...] + got_up_ref[...].astype(F32)).astype(BF16)
    out_down_ref[...] = (down_ref[...] + got_down_ref[...].astype(F32)).astype(BF16)


def base_kernel(own_a_ref, own_b_ref, a_ref, b_ref, out_ref):
    out_ref[:TILE, :] = own_a_ref[...] + a_ref[...].astype(F32)
    out_ref[TILE:, :] = own_b_ref[...] + b_ref[...].astype(F32)


def finish_kernel(base_ref, a_ref, b_ref, out_hbm, out_v, out_sems):
    copies = []
    for i, ref in enumerate((a_ref, b_ref)):
        here = pl.ds(i * TILE, TILE)
        out_v[i * TILE : (i + 1) * TILE, :] = base_ref[i * TILE : (i + 1) * TILE, :] + ref[...].astype(F32)
        c = pltpu.make_async_copy(out_v.at[here], out_hbm.at[here], out_sems.at[i])
        c.start()
        copies.append(c)
    for c in copies:
        c.wait()


def shape(dims, dtype):
    return jax.ShapeDtypeStruct(dims, dtype)

def whole(kernel, out, *args, hbm=(), smem=(), hbm_out=(), limit=60, cost=1024, scratch=()):
    def place(i, far, scalar=()):
        space = pltpu.HBM if i in far else pltpu.SMEM if i in scalar else pltpu.VMEM
        return pl.BlockSpec(memory_space=space)

    single = not isinstance(out, tuple)
    outs = (out,) if single else out
    results = pl.pallas_call(
        kernel,
        out_shape=outs,
        in_specs=[place(i, hbm, smem) for i in range(len(args))],
        out_specs=tuple(place(i, hbm_out) for i in range(len(outs))),
        scratch_shapes=list(scratch),
        compiler_params=pltpu.CompilerParams(vmem_limit_bytes=limit << 20),
        cost_estimate=pl.CostEstimate(flops=cost, transcendentals=0, bytes_accessed=1024),
    )(*args)
    return results[0] if single else results

def fixed(dims):
    return pl.BlockSpec(dims, lambda *_: (0,) * len(dims))


def tiled(dims):
    return pl.BlockSpec(dims, lambda i, *_: (i,) + (0,) * (len(dims) - 1))


def stepped(kernel, grid, in_specs, outs, out_specs, scratch, *args, limit=LIMIT, scalars=0, cost=1024):
    spec = pltpu.PrefetchScalarGridSpec(
        num_scalar_prefetch=scalars,
        grid=(grid,),
        in_specs=in_specs,
        out_specs=out_specs,
        scratch_shapes=list(scratch),
    )
    return pl.pallas_call(
        kernel,
        grid_spec=spec,
        out_shape=outs,
        compiler_params=pltpu.CompilerParams(vmem_limit_bytes=limit << 20),
        cost_estimate=pl.CostEstimate(flops=cost, transcendentals=0, bytes_accessed=1024),
    )(*args)


def sems(n):
    return pltpu.SemaphoreType.DMA((n,))


def per_device(queries, weights, beam, positives, owner):
    me = lax.axis_index("label")
    y = lax.axis_index("dp")
    rows = SLOTS * ROWS
    ranker = pltpu.with_memory_space_constraint(weights[0], pltpu.HBM)

    def swap(x):
        return lax.all_to_all(x, "label", split_axis=0, concat_axis=0, tiled=True)

    ids = jnp.arange(NDEV, dtype=jnp.int32)
    held = jnp.sum(jnp.where(owner[None, :] == ids[:, None], ids[None, :], 0), axis=1).astype(F32)
    held_rows = jnp.broadcast_to(held[:, None, None], (NDEV, SLOTS, 128)).reshape(256, 128)
    my_block = jnp.sum(jnp.where(owner == me, ids, 0)).astype(F32)
    mine = jnp.where(iota((16, 128), 1) == 0, my_block, me.astype(F32))

    pieces = whole(
        pieces_kernel,
        shape((16, 2, 8, FEAT + ROWS), BF16),
        queries.reshape(2, 16, 8, FEAT),
        positives.reshape(2, ROWS),
        beam,
        hbm=(0, 1, 2),
        scratch=(
            pltpu.VMEM((2, 16, 8, FEAT), BF16),
            pltpu.VMEM((2, ROWS), jnp.int32),
            pltpu.VMEM(beam.shape, jnp.int32),
            sems(4),
        ),
    )
    got = swap(pieces.reshape(NDEV, 8, FEAT + ROWS)).reshape(256, FEAT + ROWS)

    sent = whole(route_kernel, shape((2048, HALF), BF16), got, held_rows, limit=16)
    arrived = swap(sent.reshape(NDEV, 64, HALF))
    sel, mask, col, col_slots = whole(
        table_kernel,
        (
            pltpu.HBM((512, 2048), BF16),
            pltpu.HBM((256, 128), F32),
            shape((8, rows), jnp.int32),
            shape((SLOTS, ROWS), F32),
        ),
        got,
        held_rows,
        mine,
    )
    steps = LABELS // BIG_TILE
    w_spec = tiled((BIG_TILE, FEAT))
    lanes = shape((8, rows), F32)
    positive_rows = stepped(
        positive_kernel,
        steps,
        [fixed((8, rows)), w_spec],
        pltpu.HBM((rows, FEAT), BF16),
        fixed((rows, FEAT)),
        (pltpu.VMEM((FEAT, rows), F32),),
        col,
        ranker,
    )
    arrived, positive_rows, col = lax.optimization_barrier((arrived, positive_rows, col))

    parts_each = BIG_TILE // PART_TILE
    p, q, tops, stats, lse_row = stepped(
        scores_kernel,
        steps,
        [fixed((16, 2, SLOTS, 8, HALF)), fixed((8, rows)), w_spec],
        (
            pltpu.HBM((LABELS, rows), BF16),
            shape((rows, FEAT), BF16),
            pltpu.HBM((LABELS // PART_TILE, 8, rows), F32),
            shape((NDEV, 2 * SLOTS, ROWS), F32),
            lanes,
        ),
        (
            tiled((BIG_TILE, rows)),
            fixed((rows, FEAT)),
            tiled((parts_each, 8, rows)),
            fixed((NDEV, 2 * SLOTS, ROWS)),
            fixed((8, rows)),
        ),
        (
            pltpu.VMEM((BIG_TILE, rows), F32),
            pltpu.VMEM((8, rows), F32),
            pltpu.VMEM((8, rows), F32),
            pltpu.VMEM((8, rows), F32),
        ),
        pltpu.with_memory_space_constraint(arrived.reshape(16, 2, SLOTS, 8, HALF), pltpu.HBM),
        col,
        ranker,
    )
    all_stats = swap(stats)
    p = pltpu.with_memory_space_constraint(p, pltpu.HBM)
    tops = pltpu.with_memory_space_constraint(tops, pltpu.HBM)
    later = steps // 2

    def shifted(dims):
        return pl.BlockSpec(dims, lambda i, *_: (i + later,) + (0,) * (len(dims) - 1))

    half_sum = stepped(
        others_kernel,
        later,
        [tiled((parts_each, 8, rows)), fixed((8, rows)), w_spec, tiled((BIG_TILE, rows))],
        pltpu.HBM((FEAT, rows), F32),
        fixed((FEAT, rows)),
        (pltpu.VMEM((BIG_TILE, rows), BF16),),
        tops,
        lse_row,
        ranker,
        p,
    )
    all_stats, half_sum = lax.optimization_barrier((all_stats, half_sum))
    norm, rest, norm_slots, loss = whole(
        normal_kernel,
        (lanes, lanes, shape((SLOTS, ROWS), F32), shape((2, ROWS), F32)),
        all_stats,
        pltpu.with_memory_space_constraint(mask, pltpu.HBM),
        limit=16,
    )

    up = [(i, (i + 1) % 4) for i in range(4)]
    down = [(i, (i + 3) % 4) for i in range(4)]
    across, ahead, behind = (y + 2) % 4 * 2, (y + 1) % 4 * 2, (y + 3) % 4 * 2
    tiles = jnp.stack([across, across + 1, ahead + 1, behind, ahead, behind + 1, y * 2, y * 2 + 1])
    tiles = tiles.astype(jnp.int32)

    def table_grads(first, norm, dtypes, place=pltpu.HBM):
        n = len(dtypes)
        return stepped(
            functools.partial(table_grad_kernel, first),
            1,
            [
                fixed((rows, FEAT)),
                fixed((8, rows)),
                fixed((8, rows)),
                fixed((8, rows)),
                *(pl.BlockSpec((TILE, rows), lambda _, t, i=i: (t[first + i], 0)) for i in range(n)),
                *(
                    pl.BlockSpec((TILE // PART_TILE, 8, rows), lambda _, t, i=i: (t[first + i], 0, 0))
                    for i in range(n)
                ),
            ],
            tuple(place((TILE, FEAT), d) for d in dtypes),
            tuple(fixed((TILE, FEAT)) for _ in dtypes),
            (),
            tiles,
            q,
            norm,
            rest,
            col,
            *([p] * n),
            *([tops] * n),
            scalars=1,
        )

    far_a, far_b = table_grads(0, norm, (BF16, BF16))
    far_a, far_b, norm_slots, norm = lax.optimization_barrier((far_a, far_b, norm_slots, norm))
    via_up = lax.ppermute(far_a, "dp", up)
    via_down = lax.ppermute(far_b, "dp", down)
    part = stepped(
        part_kernel,
        later,
        [
            shifted((parts_each, 8, rows)),
            fixed((8, rows)),
            shifted((BIG_TILE, FEAT)),
            shifted((BIG_TILE, rows)),
            fixed((FEAT, rows)),
            fixed((rows, FEAT)),
            fixed(stats.shape),
            fixed((SLOTS, ROWS)),
            fixed((SLOTS, ROWS)),
        ],
        pltpu.HBM((16, 2, 64, HALF), BF16),
        fixed((16, 2, 64, HALF)),
        (pltpu.VMEM((FEAT, rows), F32), pltpu.VMEM((BIG_TILE, rows), BF16)),
        tops,
        lse_row,
        ranker,
        p,
        pltpu.with_memory_space_constraint(half_sum, pltpu.HBM),
        pltpu.with_memory_space_constraint(positive_rows, pltpu.HBM),
        stats,
        norm_slots,
        col_slots,
        limit=36,
    )
    part, norm = lax.optimization_barrier((part, norm))
    parts = swap(part.reshape(NDEV, 64, HALF)).reshape(2048, HALF)
    next_b, prev_a = table_grads(2, norm, (BF16, BF16))
    next_b, prev_a, norm = lax.optimization_barrier((next_b, prev_a, norm))
    from_prev_b = lax.ppermute(next_b, "dp", up)
    from_next_a = lax.ppermute(prev_a, "dp", down)
    next_a, prev_b = table_grads(4, norm, (F32, F32), shape)

    relay_up, relay_down = whole(
        relay_kernel,
        (shape((TILE, FEAT), BF16), shape((TILE, FEAT), BF16)),
        next_a,
        prev_b,
        via_up,
        via_down,
        limit=16,
        cost=50_000_000_000,
    )
    relay_up, relay_down, norm = lax.optimization_barrier((relay_up, relay_down, norm))
    own_a, own_b = table_grads(6, norm, (F32, F32))
    from_prev_a = lax.ppermute(relay_up, "dp", up)
    from_next_b = lax.ppermute(relay_down, "dp", down)

    sel = pltpu.with_memory_space_constraint(sel, pltpu.HBM)
    homeward = whole(sum_kernel, shape((NDEV, 8, FEAT), BF16), sel, parts, limit=16)
    home = swap(homeward)
    base = whole(
        base_kernel,
        shape((2 * TILE, FEAT), F32),
        own_a,
        own_b,
        from_next_a,
        from_prev_b,
        limit=16,
        cost=8_000_000_000,
    )
    grad_table = whole(
        finish_kernel,
        shape((2 * TILE, FEAT), F32),
        base,
        from_prev_a,
        from_next_b,
        hbm_out=(0,),
        limit=16,
        scratch=(pltpu.VMEM((2 * TILE, FEAT), F32), sems(2)),
    )
    home, grad_table = lax.optimization_barrier((home, grad_table))
    grad_queries = whole(
        home_kernel, shape((2, 16, 8, FEAT), F32), home.reshape(16, 2, 8, FEAT), limit=16
    ).reshape(256, FEAT)
    return loss.reshape(256), grad_queries, grad_table[None]

def solution(mesh):
    placed = (
        P(("dp", "label"), None),
        P("label", None, None),
        P(("dp", "label"), None),
        P(("dp", "label")),
        P(),
    )
    return jax.shard_map(
        per_device,
        mesh=mesh,
        in_specs=placed,
        out_specs=(P(("dp", "label")), P(("dp", "label"), None), P("label", "dp", None)),
        check_vma=False,
    )
```

```python
import functools

import jax
import jax.numpy as jnp
from jax import lax
from jax.experimental import pallas as pl
from jax.experimental.pallas import tpu as pltpu
from jax.sharding import PartitionSpec as P

F32 = jnp.float32
BF16 = jnp.bfloat16
NDEV = 32
SLOTS = 8
ROWS = 128
FEAT = 768
HALF = 384
LABELS = 4096
TILE = 512
BIG_TILE = 1024
PART_TILE = 256
NEG = -1e30
BIG = 1e30
LIMIT = 24

def iota(shape, dim):
    return lax.broadcasted_iota(jnp.int32, shape, dim)

def dot(a, b, dims):
    return lax.dot_general(a, b, (dims, ((), ())), preferred_element_type=F32)

def ones_where(mask):
    return jnp.where(mask, 1.0, 0.0).astype(BF16)

def slot_table(meta, held):
    n = held.shape[0]
    r = iota((256, 64), 0)
    q = iota((256, 64), 1)
    pick = ones_where((r // 8 == q % 32) & (r % 8 == 6 + q // 32))
    beams = dot(meta, pick, ((0,), (0,)))
    hit = held == beams[0:1, :]
    for k in range(1, 4):
        hit = hit | (held == beams[k : k + 1, :])
    hit = hit & (iota((n, 64), 1) >= 0)
    before = ones_where(iota((64, 64), 0) < iota((64, 64), 1))
    rank = dot(ones_where(hit), before, ((1,), (0,)))
    slot = (iota((n, 64), 0) % SLOTS).astype(F32)
    return jnp.where(hit & (rank == slot), 1.0, 0.0)

def piece_matrix(table):
    e = iota((64, 512), 1)
    spread = ones_where(iota((64, 512), 0) == e // 8)
    wide = dot(table.astype(BF16), spread, ((1,), (0,)))
    full = jnp.broadcast_to(wide[:, None, :], (256, 8, 512))
    same = iota((256, 8, 512), 1) == iota((256, 8, 512), 2) % 8
    return jnp.where(same, full, 0.0).reshape(2048, 512).astype(BF16)

def route_kernel(got_ref, held_ref, out_ref):
    got = got_ref[...]
    table = slot_table(got[:, FEAT:], held_ref[...][:, :1])
    m = piece_matrix(table)
    out = dot(m[:, :256], got[:, :HALF], ((1,), (0,)))
    out += dot(m[:, 256:], got[:, HALF:FEAT], ((1,), (0,)))
    out_ref[...] = out.astype(BF16)

def table_kernel(got_ref, held_ref, mine_ref, sel_ref, mask_ref, col_ref, slots_ref):
    meta = got_ref[...][:, FEAT:]
    table = slot_table(meta, held_ref[...][:, :1])
    sel_ref[...] = piece_matrix(table).T
    mine = mine_ref[...]
    own = slot_table(meta, mine[:, 0:1])
    row = iota((16, 64), 0)
    q = iota((16, 64), 1).astype(F32)
    home = jnp.where(q == (row.astype(F32) - 8.0) * 32.0 + mine[:, 1:2], 1.0, 0.0)
    own = jnp.where(row < 8, own, jnp.where(row < 10, home, 0.0)).astype(BF16)
    mask = dot(table.astype(BF16), own, ((1,), (1,)))
    mask_ref[...] = jnp.concatenate([mask, jnp.zeros((256, 112), F32)], axis=1)
    qq = iota((64, 256), 0)
    rr = iota((64, 256), 1)
    part = []
    for c in range(3):
        pick = ones_where((rr // 8 == qq % 32) & (rr % 8 == 3 * (qq // 32) + c))
        where_c = dot(own, pick, ((1,), (0,))).astype(BF16)
        part.append(dot(where_c, meta, ((1,), (0,))))
    inside = part[0] == mine[:, 0:1] + 1.0
    col = jnp.where(inside, part[1] * 64.0 + part[2], -1.0)
    slots_ref[...] = col[:SLOTS]
    for s in range(SLOTS):
        piece = col[s : s + 1].astype(jnp.int32)
        col_ref[:, s * ROWS : (s + 1) * ROWS] = jnp.broadcast_to(piece, (8, ROWS))

def start(copies):
    for c in copies:
        c.start()
    return copies

def pieces_kernel(q_hbm, pos_hbm, beam_hbm, out_ref, q_ref, pos_ref, beam_ref, sems):
    small = start(
        [
            pltpu.make_async_copy(pos_hbm, pos_ref, sems.at[0]),
            pltpu.make_async_copy(beam_hbm, beam_ref, sems.at[1]),
        ]
    )
    large = start(
        [
            pltpu.make_async_copy(q_hbm.at[:, pl.ds(8 * i, 8)], q_ref.at[:, pl.ds(8 * i, 8)], sems.at[2 + i])
            for i in range(2)
        ]
    )
    for c in small:
        c.wait()
    pos = pos_ref[...]
    beam = beam_ref[...]
    high, low = (pos >> 12) + 1, pos & (LABELS - 1)
    codes = (high, low >> 6, low & 63)
    row = iota((8, ROWS), 0)
    lane = iota((8, ROWS), 1)
    meta = jnp.full((8, ROWS), -1, jnp.int32)
    for b in range(2):
        for c in range(3):
            meta = jnp.where(row == 3 * b + c, codes[c][b : b + 1, :], meta)
        for k in range(beam.shape[1]):
            meta = jnp.where((row == 6 + b) & (lane == k), beam[b : b + 1, k : k + 1], meta)
    meta = meta.astype(F32).astype(BF16)
    out_ref[:, :, :, FEAT:] = jnp.broadcast_to(meta[None, None], (16, 2, 8, ROWS))
    for i in range(2):
        large[i].wait()
        g = slice(8 * i, 8 * i + 8)
        for h in range(2):
            for b in range(2):
                out_ref[g, h, :, b * HALF : (b + 1) * HALF] = q_ref[b, g, :, h * HALF : (h + 1) * HALF]

def label_iota(rows):
    return iota((PART_TILE, rows), 0).reshape(PART_TILE // 8, 8, rows)


def by_slot(lanes):
    row = iota((SLOTS, ROWS), 0)
    out = jnp.zeros((SLOTS, ROWS), F32)
    for s in range(SLOTS):
        out = jnp.where(row == s, lanes[:, s * ROWS : (s + 1) * ROWS], out)
    return out

def scores_kernel(got_ref, col_ref, w_ref, p_ref, q_ref, top_ref, stat_ref, row_ref, s_ref, high, total, found):
    step = pl.program_id(0)
    rows = s_ref.shape[1]

    @pl.when(step == 0)
    def _():
        for g in range(16):
            for h in range(2):
                for s in range(SLOTS):
                    here = slice(s * ROWS + g * 8, s * ROWS + g * 8 + 8)
                    q_ref[here, h * HALF : (h + 1) * HALF] = got_ref[g, h, s]
        high[...] = jnp.full_like(high, NEG)
        total[...] = jnp.zeros_like(total)
        found[...] = jnp.zeros_like(found)

    n = BIG_TILE // PART_TILE
    top, tot, pick = high[...], total[...], found[...]
    for k in range(n + 1):
        if k < n:
            here = slice(k * PART_TILE, (k + 1) * PART_TILE)
            s_ref[here, :] = dot(w_ref[here, :], q_ref[...], ((1,), (1,)))
        if k > 0:
            here = slice((k - 1) * PART_TILE, k * PART_TILE)
            s = s_ref[here, :]
            target = iota(s.shape, 0) + (step * BIG_TILE + (k - 1) * PART_TILE) == col_ref[0:1, :]
            pick += jnp.sum(jnp.where(target, s, 0.0).reshape(PART_TILE // 8, 8, rows), axis=0)
            best = jnp.max(jnp.max(s.reshape(PART_TILE // 8, 8, rows), axis=0), axis=0, keepdims=True)
            best = jnp.broadcast_to(best, (8, rows))
            e = jnp.exp(s - best[0:1, :])
            p_ref[here, :] = jnp.where(target, 0.0, e).astype(BF16)
            new = jnp.maximum(top, best)
            add = jnp.sum(e.reshape(PART_TILE // 8, 8, rows), axis=0)
            tot = tot * jnp.exp(top - new) + add * jnp.exp(best - new)
            top = new
            top_ref[k - 1] = best
    high[...], total[...], found[...] = top, tot, pick

    @pl.when(step == pl.num_programs(0) - 1)
    def _():
        lse = top[0:1, :] + jnp.log(jnp.sum(tot, axis=0, keepdims=True))
        row_ref[...] = jnp.broadcast_to(lse, (8, rows))
        chosen = jnp.sum(pick, axis=0, keepdims=True)
        stat_ref[:, :SLOTS, :] = jnp.broadcast_to(by_slot(lse)[None], (NDEV, SLOTS, ROWS))
        stat_ref[:, SLOTS:, :] = jnp.broadcast_to(by_slot(chosen)[None], (NDEV, SLOTS, ROWS))


def normal_kernel(stat_ref, mask_ref, norm_ref, rest_ref, slots_ref, loss_ref):
    lse = stat_ref[:, :SLOTS, :].reshape(NDEV * SLOTS, ROWS)
    found = stat_ref[:, SLOTS:, :].reshape(NDEV * SLOTS, ROWS)
    mask = mask_ref[...]
    for s in range(SLOTS + 2):
        use = mask[:, s : s + 1] > 0.5
        kept = jnp.where(use, lse, NEG)
        high = jnp.max(kept, axis=0, keepdims=True)
        tot = jnp.sum(jnp.where(use, jnp.exp(kept - high), 0.0), axis=0, keepdims=True)
        value = jnp.where(high > 0.5 * NEG, high + jnp.log(tot), BIG)
        positive = jnp.sum(jnp.where(use, found, 0.0), axis=0, keepdims=True)
        if s < SLOTS:
            here = slice(s * ROWS, (s + 1) * ROWS)
            norm_ref[:, here] = jnp.broadcast_to(value, (8, ROWS))
            rest_ref[:, here] = jnp.broadcast_to(jnp.exp(positive - value) - 1.0, (8, ROWS))
            slots_ref[s : s + 1, :] = value
        else:
            loss_ref[s - SLOTS : s - SLOTS + 1, :] = value - positive


def rows_from(acc, out_ref):
    for s in range(SLOTS):
        here = slice(s * ROWS, (s + 1) * ROWS)
        out_ref[here, :] = acc[:, here].T.astype(out_ref.dtype)


def add_to(acc, term, first):
    @pl.when(first)
    def _():
        acc[...] = term

    @pl.when(jnp.logical_not(first))
    def _():
        acc[...] += term


def positive_kernel(col_ref, w_ref, out_ref, acc):
    step = pl.program_id(0)
    target = iota((BIG_TILE, acc.shape[1]), 0) + step * BIG_TILE == col_ref[0:1, :]
    add_to(acc, dot(w_ref[...], ones_where(target), ((0,), (0,))), step == 0)

    @pl.when(step == pl.num_programs(0) - 1)
    def _():
        rows_from(acc, out_ref)


def others_kernel(top_ref, row_ref, w_ref, p_ref, out_ref, acc, scaled):
    step = pl.program_id(0)
    for i in range(BIG_TILE // PART_TILE):
        scale = jnp.exp(top_ref[i] - row_ref[...])
        here = slice(i * PART_TILE, (i + 1) * PART_TILE)
        p = p_ref[here, :].astype(F32).reshape(PART_TILE // 8, 8, scale.shape[1])
        scaled[here, :] = (p * scale[None]).reshape(PART_TILE, scale.shape[1]).astype(BF16)
    add_to(acc, dot(w_ref[...], scaled[...], ((0,), (0,))), step == 0)

    @pl.when(step == pl.num_programs(0) - 1)
    def _():
        rows_from(acc, out_ref)


def part_kernel(u_ref, r_ref, stat_ref, norm_ref, col_ref, out_ref):
    norm = norm_ref[...]
    scale = jnp.exp(stat_ref[0, :SLOTS, :] - norm).T
    rest = jnp.where(col_ref[...] >= 0.0, jnp.exp(stat_ref[0, SLOTS:, :] - norm) - 1.0, 0.0).T
    for s in range(SLOTS):
        u = u_ref[s * ROWS : (s + 1) * ROWS, :].astype(F32)
        r = r_ref[s * ROWS : (s + 1) * ROWS, :].astype(F32)
        part = (scale[:, s : s + 1] * u + rest[:, s : s + 1] * r).astype(BF16).reshape(16, 8, FEAT)
        for h in range(2):
            out_ref[:, h, s * 8 : (s + 1) * 8, :] = part[:, :, h * HALF : (h + 1) * HALF]


def table_grad_kernel(base, tiles_ref, q_ref, norm_ref, rest_ref, col_ref, *refs):
    n = len(refs) // 3
    for i in range(n):
        p_ref, top_ref, out_ref = refs[i], refs[n + i], refs[2 * n + i]
        tile = tiles_ref[base + i]
        for k in range(TILE // PART_TILE):
            here = slice(k * PART_TILE, (k + 1) * PART_TILE)
            scale = jnp.exp(top_ref[k] - norm_ref[...])
            rows = scale.shape[1]
            p = p_ref[here, :].astype(F32).reshape(PART_TILE // 8, 8, rows)
            target = label_iota(rows) == (col_ref[...] - (tile * TILE + k * PART_TILE))[None]
            slope = jnp.where(target, rest_ref[...][None], p * scale[None])
            slope = slope.reshape(PART_TILE, rows).astype(BF16)
            out_ref[here, :] = dot(slope, q_ref[...], ((1,), (0,))).astype(out_ref.dtype)


def sum_kernel(sel_ref, parts_ref, out_ref):
    out = dot(sel_ref[...], parts_ref[...], ((1,), (0,))).astype(BF16)
    for b in range(2):
        out_ref[:, :, b * HALF : (b + 1) * HALF] = out[b * 256 : (b + 1) * 256].reshape(NDEV, 8, HALF)

def home_kernel(got_ref, out_ref):
    for h in range(2):
        for b in range(2):
            out_ref[b, :, :, h * HALF : (h + 1) * HALF] = got_ref[:, h, :, b * HALF : (b + 1) * HALF].astype(F32)

def relay_kernel(up_ref, down_ref, got_up_ref, got_down_ref, out_up_ref, out_down_ref):
    out_up_ref[...] = (up_ref[...] + got_up_ref[...].astype(F32)).astype(BF16)
    out_down_ref[...] = (down_ref[...] + got_down_ref[...].astype(F32)).astype(BF16)


def base_kernel(own_a_ref, own_b_ref, a_ref, b_ref, out_ref):
    out_ref[:TILE, :] = own_a_ref[...] + a_ref[...].astype(F32)
    out_ref[TILE:, :] = own_b_ref[...] + b_ref[...].astype(F32)


def finish_kernel(base_ref, a_ref, b_ref, out_hbm, out_v, out_sems):
    copies = []
    for i, ref in enumerate((a_ref, b_ref)):
        here = pl.ds(i * TILE, TILE)
        out_v[i * TILE : (i + 1) * TILE, :] = base_ref[i * TILE : (i + 1) * TILE, :] + ref[...].astype(F32)
        c = pltpu.make_async_copy(out_v.at[here], out_hbm.at[here], out_sems.at[i])
        c.start()
        copies.append(c)
    for c in copies:
        c.wait()


def shape(dims, dtype):
    return jax.ShapeDtypeStruct(dims, dtype)

def whole(kernel, out, *args, hbm=(), smem=(), hbm_out=(), limit=60, cost=1024, scratch=()):
    def place(i, far, scalar=()):
        space = pltpu.HBM if i in far else pltpu.SMEM if i in scalar else pltpu.VMEM
        return pl.BlockSpec(memory_space=space)

    single = not isinstance(out, tuple)
    outs = (out,) if single else out
    results = pl.pallas_call(
        kernel,
        out_shape=outs,
        in_specs=[place(i, hbm, smem) for i in range(len(args))],
        out_specs=tuple(place(i, hbm_out) for i in range(len(outs))),
        scratch_shapes=list(scratch),
        compiler_params=pltpu.CompilerParams(vmem_limit_bytes=limit << 20),
        cost_estimate=pl.CostEstimate(flops=cost, transcendentals=0, bytes_accessed=1024),
    )(*args)
    return results[0] if single else results

def fixed(dims):
    return pl.BlockSpec(dims, lambda *_: (0,) * len(dims))


def tiled(dims):
    return pl.BlockSpec(dims, lambda i, *_: (i,) + (0,) * (len(dims) - 1))


def stepped(kernel, grid, in_specs, outs, out_specs, scratch, *args, limit=LIMIT, scalars=0, cost=1024):
    spec = pltpu.PrefetchScalarGridSpec(
        num_scalar_prefetch=scalars,
        grid=(grid,),
        in_specs=in_specs,
        out_specs=out_specs,
        scratch_shapes=list(scratch),
    )
    return pl.pallas_call(
        kernel,
        grid_spec=spec,
        out_shape=outs,
        compiler_params=pltpu.CompilerParams(vmem_limit_bytes=limit << 20),
        cost_estimate=pl.CostEstimate(flops=cost, transcendentals=0, bytes_accessed=1024),
    )(*args)


def sems(n):
    return pltpu.SemaphoreType.DMA((n,))


def per_device(queries, weights, beam, positives, owner):
    me = lax.axis_index("label")
    y = lax.axis_index("dp")
    rows = SLOTS * ROWS
    ranker = pltpu.with_memory_space_constraint(weights[0], pltpu.HBM)

    def swap(x):
        return lax.all_to_all(x, "label", split_axis=0, concat_axis=0, tiled=True)

    ids = jnp.arange(NDEV, dtype=jnp.int32)
    held = jnp.sum(jnp.where(owner[None, :] == ids[:, None], ids[None, :], 0), axis=1).astype(F32)
    held_rows = jnp.broadcast_to(held[:, None, None], (NDEV, SLOTS, 128)).reshape(256, 128)
    my_block = jnp.sum(jnp.where(owner == me, ids, 0)).astype(F32)
    mine = jnp.where(iota((16, 128), 1) == 0, my_block, me.astype(F32))

    pieces = whole(
        pieces_kernel,
        shape((16, 2, 8, FEAT + ROWS), BF16),
        queries.reshape(2, 16, 8, FEAT),
        positives.reshape(2, ROWS),
        beam,
        hbm=(0, 1, 2),
        scratch=(
            pltpu.VMEM((2, 16, 8, FEAT), BF16),
            pltpu.VMEM((2, ROWS), jnp.int32),
            pltpu.VMEM(beam.shape, jnp.int32),
            sems(4),
        ),
    )
    got = swap(pieces.reshape(NDEV, 8, FEAT + ROWS)).reshape(256, FEAT + ROWS)

    sent = whole(route_kernel, shape((2048, HALF), BF16), got, held_rows, limit=16)
    arrived = swap(sent.reshape(NDEV, 64, HALF))
    sel, mask, col, col_slots = whole(
        table_kernel,
        (
            pltpu.HBM((512, 2048), BF16),
            pltpu.HBM((256, 128), F32),
            shape((8, rows), jnp.int32),
            shape((SLOTS, ROWS), F32),
        ),
        got,
        held_rows,
        mine,
    )
    steps = LABELS // BIG_TILE
    w_spec = tiled((BIG_TILE, FEAT))
    lanes = shape((8, rows), F32)
    positive_rows = stepped(
        positive_kernel,
        steps,
        [fixed((8, rows)), w_spec],
        shape((rows, FEAT), BF16),
        fixed((rows, FEAT)),
        (pltpu.VMEM((FEAT, rows), F32),),
        col,
        ranker,
    )
    arrived, positive_rows, col = lax.optimization_barrier((arrived, positive_rows, col))

    parts_each = BIG_TILE // PART_TILE
    p, q, tops, stats, lse_row = stepped(
        scores_kernel,
        steps,
        [fixed((16, 2, SLOTS, 8, HALF)), fixed((8, rows)), w_spec],
        (
            pltpu.HBM((LABELS, rows), BF16),
            shape((rows, FEAT), BF16),
            pltpu.HBM((LABELS // PART_TILE, 8, rows), F32),
            shape((NDEV, 2 * SLOTS, ROWS), F32),
            lanes,
        ),
        (
            tiled((BIG_TILE, rows)),
            fixed((rows, FEAT)),
            tiled((parts_each, 8, rows)),
            fixed((NDEV, 2 * SLOTS, ROWS)),
            fixed((8, rows)),
        ),
        (
            pltpu.VMEM((BIG_TILE, rows), F32),
            pltpu.VMEM((8, rows), F32),
            pltpu.VMEM((8, rows), F32),
            pltpu.VMEM((8, rows), F32),
        ),
        pltpu.with_memory_space_constraint(arrived.reshape(16, 2, SLOTS, 8, HALF), pltpu.HBM),
        col,
        ranker,
    )
    all_stats = swap(stats)
    p = pltpu.with_memory_space_constraint(p, pltpu.HBM)
    tops = pltpu.with_memory_space_constraint(tops, pltpu.HBM)
    others = stepped(
        others_kernel,
        steps,
        [tiled((parts_each, 8, rows)), fixed((8, rows)), w_spec, tiled((BIG_TILE, rows))],
        pltpu.HBM((rows, FEAT), BF16),
        fixed((rows, FEAT)),
        (pltpu.VMEM((FEAT, rows), F32), pltpu.VMEM((BIG_TILE, rows), BF16)),
        tops,
        lse_row,
        ranker,
        p,
    )
    all_stats, others = lax.optimization_barrier((all_stats, others))
    norm, rest, norm_slots, loss = whole(
        normal_kernel,
        (lanes, lanes, shape((SLOTS, ROWS), F32), shape((2, ROWS), F32)),
        all_stats,
        pltpu.with_memory_space_constraint(mask, pltpu.HBM),
        limit=16,
    )

    up = [(i, (i + 1) % 4) for i in range(4)]
    down = [(i, (i + 3) % 4) for i in range(4)]
    across, ahead, behind = (y + 2) % 4 * 2, (y + 1) % 4 * 2, (y + 3) % 4 * 2
    tiles = jnp.stack([across, across + 1, ahead + 1, behind, ahead, behind + 1, y * 2, y * 2 + 1])
    tiles = tiles.astype(jnp.int32)

    def table_grads(first, norm, dtypes, place=pltpu.HBM):
        n = len(dtypes)
        return stepped(
            functools.partial(table_grad_kernel, first),
            1,
            [
                fixed((rows, FEAT)),
                fixed((8, rows)),
                fixed((8, rows)),
                fixed((8, rows)),
                *(pl.BlockSpec((TILE, rows), lambda _, t, i=i: (t[first + i], 0)) for i in range(n)),
                *(
                    pl.BlockSpec((TILE // PART_TILE, 8, rows), lambda _, t, i=i: (t[first + i], 0, 0))
                    for i in range(n)
                ),
            ],
            tuple(place((TILE, FEAT), d) for d in dtypes),
            tuple(fixed((TILE, FEAT)) for _ in dtypes),
            (),
            tiles,
            q,
            norm,
            rest,
            col,
            *([p] * n),
            *([tops] * n),
            scalars=1,
        )

    far_a, far_b = table_grads(0, norm, (BF16, BF16))
    far_a, far_b, norm_slots, norm = lax.optimization_barrier((far_a, far_b, norm_slots, norm))
    via_up = lax.ppermute(far_a, "dp", up)
    via_down = lax.ppermute(far_b, "dp", down)
    part = whole(
        part_kernel,
        pltpu.HBM((16, 2, 64, HALF), BF16),
        others,
        positive_rows,
        stats,
        norm_slots,
        col_slots,
        limit=16,
    )
    part, norm = lax.optimization_barrier((part, norm))
    parts = swap(part.reshape(NDEV, 64, HALF)).reshape(2048, HALF)
    next_b, prev_a = table_grads(2, norm, (BF16, BF16))
    next_b, prev_a, norm = lax.optimization_barrier((next_b, prev_a, norm))
    from_prev_b = lax.ppermute(next_b, "dp", up)
    from_next_a = lax.ppermute(prev_a, "dp", down)
    next_a, prev_b = table_grads(4, norm, (F32, F32), shape)

    relay_up, relay_down = whole(
        relay_kernel,
        (shape((TILE, FEAT), BF16), shape((TILE, FEAT), BF16)),
        next_a,
        prev_b,
        via_up,
        via_down,
        limit=16,
        cost=50_000_000_000,
    )
    relay_up, relay_down, norm = lax.optimization_barrier((relay_up, relay_down, norm))
    own_a, own_b = table_grads(6, norm, (F32, F32))
    from_prev_a = lax.ppermute(relay_up, "dp", up)
    from_next_b = lax.ppermute(relay_down, "dp", down)

    sel = pltpu.with_memory_space_constraint(sel, pltpu.HBM)
    homeward = whole(sum_kernel, shape((NDEV, 8, FEAT), BF16), sel, parts, limit=16)
    home = swap(homeward)
    base = whole(
        base_kernel,
        shape((2 * TILE, FEAT), F32),
        own_a,
        own_b,
        from_next_a,
        from_prev_b,
        limit=16,
        cost=8_000_000_000,
    )
    grad_table = whole(
        finish_kernel,
        shape((2 * TILE, FEAT), F32),
        base,
        from_prev_a,
        from_next_b,
        hbm_out=(0,),
        limit=16,
        scratch=(pltpu.VMEM((2 * TILE, FEAT), F32), sems(2)),
    )
    home, grad_table = lax.optimization_barrier((home, grad_table))
    grad_queries = whole(
        home_kernel, shape((2, 16, 8, FEAT), F32), home.reshape(16, 2, 8, FEAT), limit=16
    ).reshape(256, FEAT)
    return loss.reshape(256), grad_queries, grad_table[None]

def solution(mesh):
    placed = (
        P(("dp", "label"), None),
        P("label", None, None),
        P(("dp", "label"), None),
        P(("dp", "label")),
        P(),
    )
    return jax.shard_map(
        per_device,
        mesh=mesh,
        in_specs=placed,
        out_specs=(P(("dp", "label")), P(("dp", "label"), None), P("label", "dp", None)),
        check_vma=False,
    )
```

```python
import functools

import jax
import jax.numpy as jnp
from jax import lax
from jax.experimental import pallas as pl
from jax.experimental.pallas import tpu as pltpu
from jax.sharding import PartitionSpec as P

F32 = jnp.float32
BF16 = jnp.bfloat16
NDEV = 32
SLOTS = 8
ROWS = 128
FEAT = 768
HALF = 384
LABELS = 4096
TILE = 512
BIG_TILE = 1024
PART_TILE = 256
NEG = -1e30
BIG = 1e30
LIMIT = 24

def iota(shape, dim):
    return lax.broadcasted_iota(jnp.int32, shape, dim)

def dot(a, b, dims):
    return lax.dot_general(a, b, (dims, ((), ())), preferred_element_type=F32)

def ones_where(mask):
    return jnp.where(mask, 1.0, 0.0).astype(BF16)

def slot_table(meta, held):
    n = held.shape[0]
    r = iota((256, 64), 0)
    q = iota((256, 64), 1)
    pick = ones_where((r // 8 == q % 32) & (r % 8 == 6 + q // 32))
    beams = dot(meta, pick, ((0,), (0,)))
    hit = held == beams[0:1, :]
    for k in range(1, 4):
        hit = hit | (held == beams[k : k + 1, :])
    hit = hit & (iota((n, 64), 1) >= 0)
    before = ones_where(iota((64, 64), 0) < iota((64, 64), 1))
    rank = dot(ones_where(hit), before, ((1,), (0,)))
    slot = (iota((n, 64), 0) % SLOTS).astype(F32)
    return jnp.where(hit & (rank == slot), 1.0, 0.0)

def piece_matrix(table):
    e = iota((64, 512), 1)
    spread = ones_where(iota((64, 512), 0) == e // 8)
    wide = dot(table.astype(BF16), spread, ((1,), (0,)))
    full = jnp.broadcast_to(wide[:, None, :], (256, 8, 512))
    same = iota((256, 8, 512), 1) == iota((256, 8, 512), 2) % 8
    return jnp.where(same, full, 0.0).reshape(2048, 512).astype(BF16)

def route_kernel(got_ref, held_ref, out_ref):
    got = got_ref[...]
    table = slot_table(got[:, FEAT:], held_ref[...][:, :1])
    m = piece_matrix(table)
    x = jnp.concatenate([got[:, :HALF], got[:, HALF:FEAT]], axis=0)
    out_ref[...] = dot(m, x, ((1,), (0,))).astype(BF16)


def table_kernel(got_ref, held_ref, mine_ref, sel_ref, mask_ref, col_ref, slots_ref):
    meta = got_ref[...][:, FEAT:]
    table = slot_table(meta, held_ref[...][:, :1])
    sel_ref[...] = piece_matrix(table).T
    mine = mine_ref[...]
    own = slot_table(meta, mine[:, 0:1])
    row = iota((16, 64), 0)
    q = iota((16, 64), 1).astype(F32)
    home = jnp.where(q == (row.astype(F32) - 8.0) * 32.0 + mine[:, 1:2], 1.0, 0.0)
    own = jnp.where(row < 8, own, jnp.where(row < 10, home, 0.0)).astype(BF16)
    mask = dot(table.astype(BF16), own, ((1,), (1,)))
    mask_ref[...] = jnp.concatenate([mask, jnp.zeros((256, 112), F32)], axis=1)
    qq = iota((64, 256), 0)
    rr = iota((64, 256), 1)
    part = []
    for c in range(3):
        pick = ones_where((rr // 8 == qq % 32) & (rr % 8 == 3 * (qq // 32) + c))
        where_c = dot(own, pick, ((1,), (0,))).astype(BF16)
        part.append(dot(where_c, meta, ((1,), (0,))))
    inside = part[0] == mine[:, 0:1] + 1.0
    col = jnp.where(inside, part[1] * 64.0 + part[2], -1.0)
    slots_ref[...] = col[:SLOTS]
    for s in range(SLOTS):
        piece = col[s : s + 1].astype(jnp.int32)
        col_ref[:, s * ROWS : (s + 1) * ROWS] = jnp.broadcast_to(piece, (8, ROWS))

def start(copies):
    for c in copies:
        c.start()
    return copies

def pieces_kernel(q_hbm, pos_hbm, beam_hbm, out_ref, q_ref, pos_ref, beam_ref, sems):
    small = start(
        [
            pltpu.make_async_copy(pos_hbm, pos_ref, sems.at[0]),
            pltpu.make_async_copy(beam_hbm, beam_ref, sems.at[1]),
        ]
    )
    large = start(
        [
            pltpu.make_async_copy(q_hbm.at[:, pl.ds(8 * i, 8)], q_ref.at[:, pl.ds(8 * i, 8)], sems.at[2 + i])
            for i in range(2)
        ]
    )
    for c in small:
        c.wait()
    pos = pos_ref[...]
    beam = beam_ref[...]
    high, low = (pos >> 12) + 1, pos & (LABELS - 1)
    codes = (high, low >> 6, low & 63)
    row = iota((8, ROWS), 0)
    lane = iota((8, ROWS), 1)
    meta = jnp.full((8, ROWS), -1, jnp.int32)
    for b in range(2):
        for c in range(3):
            meta = jnp.where(row == 3 * b + c, codes[c][b : b + 1, :], meta)
        for k in range(beam.shape[1]):
            meta = jnp.where((row == 6 + b) & (lane == k), beam[b : b + 1, k : k + 1], meta)
    meta = meta.astype(F32).astype(BF16)
    out_ref[:, :, :, FEAT:] = jnp.broadcast_to(meta[None, None], (16, 2, 8, ROWS))
    for i in range(2):
        large[i].wait()
        g = slice(8 * i, 8 * i + 8)
        for h in range(2):
            for b in range(2):
                out_ref[g, h, :, b * HALF : (b + 1) * HALF] = q_ref[b, g, :, h * HALF : (h + 1) * HALF]

def label_iota(rows):
    return iota((PART_TILE, rows), 0).reshape(PART_TILE // 8, 8, rows)


def by_slot(lanes):
    row = iota((SLOTS, ROWS), 0)
    out = jnp.zeros((SLOTS, ROWS), F32)
    for s in range(SLOTS):
        out = jnp.where(row == s, lanes[:, s * ROWS : (s + 1) * ROWS], out)
    return out

def scores_kernel(got_ref, col_ref, w_ref, p_ref, q_ref, top_ref, stat_ref, row_ref, s_ref, high, total, found):
    step = pl.program_id(0)
    rows = s_ref.shape[1]

    @pl.when(step == 0)
    def _():
        for g in range(16):
            for h in range(2):
                for s in range(SLOTS):
                    here = slice(s * ROWS + g * 8, s * ROWS + g * 8 + 8)
                    q_ref[here, h * HALF : (h + 1) * HALF] = got_ref[g, h, s]
        high[...] = jnp.full_like(high, NEG)
        total[...] = jnp.zeros_like(total)
        found[...] = jnp.zeros_like(found)

    n = BIG_TILE // PART_TILE
    top, tot, pick = high[...], total[...], found[...]
    for k in range(n + 1):
        if k < n:
            here = slice(k * PART_TILE, (k + 1) * PART_TILE)
            s_ref[here, :] = dot(w_ref[here, :], q_ref[...], ((1,), (1,)))
        if k > 0:
            here = slice((k - 1) * PART_TILE, k * PART_TILE)
            s = s_ref[here, :]
            target = iota(s.shape, 0) + (step * BIG_TILE + (k - 1) * PART_TILE) == col_ref[0:1, :]
            pick += jnp.sum(jnp.where(target, s, 0.0).reshape(PART_TILE // 8, 8, rows), axis=0)
            best = jnp.max(jnp.max(s.reshape(PART_TILE // 8, 8, rows), axis=0), axis=0, keepdims=True)
            best = jnp.broadcast_to(best, (8, rows))
            e = jnp.exp(s - best[0:1, :])
            p_ref[here, :] = jnp.where(target, 0.0, e).astype(BF16)
            new = jnp.maximum(top, best)
            add = jnp.sum(e.reshape(PART_TILE // 8, 8, rows), axis=0)
            tot = tot * jnp.exp(top - new) + add * jnp.exp(best - new)
            top = new
            top_ref[k - 1] = best
    high[...], total[...], found[...] = top, tot, pick

    @pl.when(step == pl.num_programs(0) - 1)
    def _():
        lse = top[0:1, :] + jnp.log(jnp.sum(tot, axis=0, keepdims=True))
        row_ref[...] = jnp.broadcast_to(lse, (8, rows))
        chosen = jnp.sum(pick, axis=0, keepdims=True)
        stat_ref[:, :SLOTS, :] = jnp.broadcast_to(by_slot(lse)[None], (NDEV, SLOTS, ROWS))
        stat_ref[:, SLOTS:, :] = jnp.broadcast_to(by_slot(chosen)[None], (NDEV, SLOTS, ROWS))


def normal_kernel(stat_ref, mask_ref, norm_ref, rest_ref, slots_ref, loss_ref):
    lse = stat_ref[:, :SLOTS, :].reshape(NDEV * SLOTS, ROWS)
    found = stat_ref[:, SLOTS:, :].reshape(NDEV * SLOTS, ROWS)
    mask = mask_ref[...]
    for s in range(SLOTS + 2):
        use = mask[:, s : s + 1] > 0.5
        kept = jnp.where(use, lse, NEG)
        high = jnp.max(kept, axis=0, keepdims=True)
        tot = jnp.sum(jnp.where(use, jnp.exp(kept - high), 0.0), axis=0, keepdims=True)
        value = jnp.where(high > 0.5 * NEG, high + jnp.log(tot), BIG)
        positive = jnp.sum(jnp.where(use, found, 0.0), axis=0, keepdims=True)
        if s < SLOTS:
            here = slice(s * ROWS, (s + 1) * ROWS)
            norm_ref[:, here] = jnp.broadcast_to(value, (8, ROWS))
            rest_ref[:, here] = jnp.broadcast_to(jnp.exp(positive - value) - 1.0, (8, ROWS))
            slots_ref[s : s + 1, :] = value
        else:
            loss_ref[s - SLOTS : s - SLOTS + 1, :] = value - positive


def rows_from(acc, out_ref):
    for s in range(SLOTS):
        here = slice(s * ROWS, (s + 1) * ROWS)
        out_ref[here, :] = acc[:, here].T.astype(out_ref.dtype)


def add_to(acc, term, first):
    @pl.when(first)
    def _():
        acc[...] = term

    @pl.when(jnp.logical_not(first))
    def _():
        acc[...] += term


def positive_kernel(col_ref, w_ref, out_ref, acc):
    step = pl.program_id(0)
    target = iota((BIG_TILE, acc.shape[1]), 0) + step * BIG_TILE == col_ref[0:1, :]
    add_to(acc, dot(w_ref[...], ones_where(target), ((0,), (0,))), step == 0)

    @pl.when(step == pl.num_programs(0) - 1)
    def _():
        rows_from(acc, out_ref)


def others_kernel(top_ref, row_ref, w_ref, p_ref, out_ref, acc, scaled):
    step = pl.program_id(0)
    for i in range(BIG_TILE // PART_TILE):
        scale = jnp.exp(top_ref[i] - row_ref[...])
        here = slice(i * PART_TILE, (i + 1) * PART_TILE)
        p = p_ref[here, :].astype(F32).reshape(PART_TILE // 8, 8, scale.shape[1])
        scaled[here, :] = (p * scale[None]).reshape(PART_TILE, scale.shape[1]).astype(BF16)
    add_to(acc, dot(w_ref[...], scaled[...], ((0,), (0,))), step == 0)

    @pl.when(step == pl.num_programs(0) - 1)
    def _():
        rows_from(acc, out_ref)


def part_kernel(u_ref, r_ref, stat_ref, norm_ref, col_ref, out_ref):
    norm = norm_ref[...]
    scale = jnp.exp(stat_ref[0, :SLOTS, :] - norm).T
    rest = jnp.where(col_ref[...] >= 0.0, jnp.exp(stat_ref[0, SLOTS:, :] - norm) - 1.0, 0.0).T
    for s in range(SLOTS):
        u = u_ref[s * ROWS : (s + 1) * ROWS, :].astype(F32)
        r = r_ref[s * ROWS : (s + 1) * ROWS, :].astype(F32)
        part = (scale[:, s : s + 1] * u + rest[:, s : s + 1] * r).astype(BF16).reshape(16, 8, FEAT)
        for h in range(2):
            out_ref[:, h, s * 8 : (s + 1) * 8, :] = part[:, :, h * HALF : (h + 1) * HALF]


def table_grad_kernel(base, tiles_ref, q_ref, norm_ref, rest_ref, col_ref, *refs):
    n = len(refs) // 3
    for i in range(n):
        p_ref, top_ref, out_ref = refs[i], refs[n + i], refs[2 * n + i]
        tile = tiles_ref[base + i]
        for k in range(TILE // PART_TILE):
            here = slice(k * PART_TILE, (k + 1) * PART_TILE)
            scale = jnp.exp(top_ref[k] - norm_ref[...])
            rows = scale.shape[1]
            p = p_ref[here, :].astype(F32).reshape(PART_TILE // 8, 8, rows)
            target = label_iota(rows) == (col_ref[...] - (tile * TILE + k * PART_TILE))[None]
            slope = jnp.where(target, rest_ref[...][None], p * scale[None])
            slope = slope.reshape(PART_TILE, rows).astype(BF16)
            out_ref[here, :] = dot(slope, q_ref[...], ((1,), (0,))).astype(out_ref.dtype)


def sum_kernel(sel_ref, parts_ref, out_ref):
    out = dot(sel_ref[...], parts_ref[...], ((1,), (0,))).astype(BF16)
    for b in range(2):
        out_ref[:, :, b * HALF : (b + 1) * HALF] = out[b * 256 : (b + 1) * 256].reshape(NDEV, 8, HALF)

def relay_kernel(up_ref, down_ref, got_up_ref, got_down_ref, out_up_ref, out_down_ref):
    out_up_ref[...] = (up_ref[...] + got_up_ref[...].astype(F32)).astype(BF16)
    out_down_ref[...] = (down_ref[...] + got_down_ref[...].astype(F32)).astype(BF16)


def base_kernel(own_a_ref, own_b_ref, a_ref, b_ref, out_ref):
    out_ref[:TILE, :] = own_a_ref[...] + a_ref[...].astype(F32)
    out_ref[TILE:, :] = own_b_ref[...] + b_ref[...].astype(F32)


def finish_kernel(base_ref, a_hbm, b_hbm, home_ref, out_hbm, grad_hbm, got, out_v, grad_v, in_sems, out_sems, grad_sem):
    tile = PART_TILE
    per = TILE // tile
    copies = start(
        [
            pltpu.make_async_copy(
                src.at[pl.ds(k * tile, tile)], got.at[pl.ds((i * per + k) * tile, tile)], in_sems.at[i * per + k]
            )
            for i, src in enumerate((a_hbm, b_hbm))
            for k in range(per)
        ]
    )
    for h in range(2):
        for b in range(2):
            piece = home_ref[:, h, :, b * HALF : (b + 1) * HALF].astype(F32)
            grad_v[b, :, :, h * HALF : (h + 1) * HALF] = piece
    grad = pltpu.make_async_copy(grad_v, grad_hbm, grad_sem)
    grad.start()
    out = []
    for j in range(2 * per):
        here = slice(j * tile, (j + 1) * tile)
        copies[j].wait()
        out_v[here, :] = base_ref[here, :] + got[here, :].astype(F32)
        c = pltpu.make_async_copy(out_v.at[pl.ds(j * tile, tile)], out_hbm.at[pl.ds(j * tile, tile)], out_sems.at[j])
        c.start()
        out.append(c)
    grad.wait()
    for c in out:
        c.wait()


def shape(dims, dtype):
    return jax.ShapeDtypeStruct(dims, dtype)

def whole(kernel, out, *args, hbm=(), smem=(), hbm_out=(), limit=60, cost=1024, scratch=()):
    def place(i, far, scalar=()):
        space = pltpu.HBM if i in far else pltpu.SMEM if i in scalar else pltpu.VMEM
        return pl.BlockSpec(memory_space=space)

    single = not isinstance(out, tuple)
    outs = (out,) if single else out
    results = pl.pallas_call(
        kernel,
        out_shape=outs,
        in_specs=[place(i, hbm, smem) for i in range(len(args))],
        out_specs=tuple(place(i, hbm_out) for i in range(len(outs))),
        scratch_shapes=list(scratch),
        compiler_params=pltpu.CompilerParams(vmem_limit_bytes=limit << 20),
        cost_estimate=pl.CostEstimate(flops=cost, transcendentals=0, bytes_accessed=1024),
    )(*args)
    return results[0] if single else results

def fixed(dims):
    return pl.BlockSpec(dims, lambda *_: (0,) * len(dims))


def tiled(dims):
    return pl.BlockSpec(dims, lambda i, *_: (i,) + (0,) * (len(dims) - 1))


def stepped(kernel, grid, in_specs, outs, out_specs, scratch, *args, limit=LIMIT, scalars=0, cost=1024):
    spec = pltpu.PrefetchScalarGridSpec(
        num_scalar_prefetch=scalars,
        grid=(grid,),
        in_specs=in_specs,
        out_specs=out_specs,
        scratch_shapes=list(scratch),
    )
    return pl.pallas_call(
        kernel,
        grid_spec=spec,
        out_shape=outs,
        compiler_params=pltpu.CompilerParams(vmem_limit_bytes=limit << 20),
        cost_estimate=pl.CostEstimate(flops=cost, transcendentals=0, bytes_accessed=1024),
    )(*args)


def sems(n):
    return pltpu.SemaphoreType.DMA((n,))


def per_device(queries, weights, beam, positives, owner):
    me = lax.axis_index("label")
    y = lax.axis_index("dp")
    rows = SLOTS * ROWS
    ranker = pltpu.with_memory_space_constraint(weights[0], pltpu.HBM)

    def swap(x):
        return lax.all_to_all(x, "label", split_axis=0, concat_axis=0, tiled=True)

    ids = jnp.arange(NDEV, dtype=jnp.int32)
    held = jnp.sum(jnp.where(owner[None, :] == ids[:, None], ids[None, :], 0), axis=1).astype(F32)
    held_rows = jnp.broadcast_to(held[:, None, None], (NDEV, SLOTS, 128)).reshape(256, 128)
    my_block = jnp.sum(jnp.where(owner == me, ids, 0)).astype(F32)
    mine = jnp.where(iota((16, 128), 1) == 0, my_block, me.astype(F32))

    pieces = whole(
        pieces_kernel,
        shape((16, 2, 8, FEAT + ROWS), BF16),
        queries.reshape(2, 16, 8, FEAT),
        positives.reshape(2, ROWS),
        beam,
        hbm=(0, 1, 2),
        scratch=(
            pltpu.VMEM((2, 16, 8, FEAT), BF16),
            pltpu.VMEM((2, ROWS), jnp.int32),
            pltpu.VMEM(beam.shape, jnp.int32),
            sems(4),
        ),
    )
    got = swap(pieces.reshape(NDEV, 8, FEAT + ROWS)).reshape(256, FEAT + ROWS)

    sent = whole(route_kernel, shape((2048, HALF), BF16), got, held_rows, limit=16)
    arrived = swap(sent.reshape(NDEV, 64, HALF))
    sel, mask, col, col_slots = whole(
        table_kernel,
        (
            pltpu.HBM((512, 2048), BF16),
            pltpu.HBM((256, 128), F32),
            shape((8, rows), jnp.int32),
            shape((SLOTS, ROWS), F32),
        ),
        got,
        held_rows,
        mine,
    )
    steps = LABELS // BIG_TILE
    w_spec = tiled((BIG_TILE, FEAT))
    lanes = shape((8, rows), F32)
    positive_rows = stepped(
        positive_kernel,
        steps,
        [fixed((8, rows)), w_spec],
        shape((rows, FEAT), BF16),
        fixed((rows, FEAT)),
        (pltpu.VMEM((FEAT, rows), F32),),
        col,
        ranker,
    )
    arrived, positive_rows, col = lax.optimization_barrier((arrived, positive_rows, col))

    parts_each = BIG_TILE // PART_TILE
    p, q, tops, stats, lse_row = stepped(
        scores_kernel,
        steps,
        [fixed((16, 2, SLOTS, 8, HALF)), fixed((8, rows)), w_spec],
        (
            pltpu.HBM((LABELS, rows), BF16),
            shape((rows, FEAT), BF16),
            pltpu.HBM((LABELS // PART_TILE, 8, rows), F32),
            shape((NDEV, 2 * SLOTS, ROWS), F32),
            lanes,
        ),
        (
            tiled((BIG_TILE, rows)),
            fixed((rows, FEAT)),
            tiled((parts_each, 8, rows)),
            fixed((NDEV, 2 * SLOTS, ROWS)),
            fixed((8, rows)),
        ),
        (
            pltpu.VMEM((BIG_TILE, rows), F32),
            pltpu.VMEM((8, rows), F32),
            pltpu.VMEM((8, rows), F32),
            pltpu.VMEM((8, rows), F32),
        ),
        pltpu.with_memory_space_constraint(arrived.reshape(16, 2, SLOTS, 8, HALF), pltpu.HBM),
        col,
        ranker,
    )
    all_stats = swap(stats)
    p = pltpu.with_memory_space_constraint(p, pltpu.HBM)
    tops = pltpu.with_memory_space_constraint(tops, pltpu.HBM)
    others = stepped(
        others_kernel,
        steps,
        [tiled((parts_each, 8, rows)), fixed((8, rows)), w_spec, tiled((BIG_TILE, rows))],
        pltpu.HBM((rows, FEAT), BF16),
        fixed((rows, FEAT)),
        (pltpu.VMEM((FEAT, rows), F32), pltpu.VMEM((BIG_TILE, rows), BF16)),
        tops,
        lse_row,
        ranker,
        p,
    )
    all_stats, others = lax.optimization_barrier((all_stats, others))
    norm, rest, norm_slots, loss = whole(
        normal_kernel,
        (lanes, lanes, shape((SLOTS, ROWS), F32), shape((2, ROWS), F32)),
        all_stats,
        pltpu.with_memory_space_constraint(mask, pltpu.HBM),
        limit=16,
    )

    up = [(i, (i + 1) % 4) for i in range(4)]
    down = [(i, (i + 3) % 4) for i in range(4)]
    across, ahead, behind = (y + 2) % 4 * 2, (y + 1) % 4 * 2, (y + 3) % 4 * 2
    tiles = jnp.stack([across, across + 1, ahead + 1, behind, ahead, behind + 1, y * 2, y * 2 + 1])
    tiles = tiles.astype(jnp.int32)

    def table_grads(first, norm, dtypes, place=pltpu.HBM):
        n = len(dtypes)
        return stepped(
            functools.partial(table_grad_kernel, first),
            1,
            [
                fixed((rows, FEAT)),
                fixed((8, rows)),
                fixed((8, rows)),
                fixed((8, rows)),
                *(pl.BlockSpec((TILE, rows), lambda _, t, i=i: (t[first + i], 0)) for i in range(n)),
                *(
                    pl.BlockSpec((TILE // PART_TILE, 8, rows), lambda _, t, i=i: (t[first + i], 0, 0))
                    for i in range(n)
                ),
            ],
            tuple(place((TILE, FEAT), d) for d in dtypes),
            tuple(fixed((TILE, FEAT)) for _ in dtypes),
            (),
            tiles,
            q,
            norm,
            rest,
            col,
            *([p] * n),
            *([tops] * n),
            scalars=1,
        )

    far_a, far_b = table_grads(0, norm, (BF16, BF16))
    far_a, far_b, norm_slots, norm = lax.optimization_barrier((far_a, far_b, norm_slots, norm))
    via_up = lax.ppermute(far_a, "dp", up)
    via_down = lax.ppermute(far_b, "dp", down)
    part = whole(
        part_kernel,
        pltpu.HBM((16, 2, 64, HALF), BF16),
        others,
        positive_rows,
        stats,
        norm_slots,
        col_slots,
        limit=16,
    )
    part, norm = lax.optimization_barrier((part, norm))
    parts = swap(part.reshape(NDEV, 64, HALF)).reshape(2048, HALF)
    next_b, prev_a = table_grads(2, norm, (BF16, BF16))
    next_b, prev_a, norm = lax.optimization_barrier((next_b, prev_a, norm))
    from_prev_b = lax.ppermute(next_b, "dp", up)
    from_next_a = lax.ppermute(prev_a, "dp", down)
    next_a, prev_b = table_grads(4, norm, (F32, F32), shape)

    relay_up, relay_down = whole(
        relay_kernel,
        (shape((TILE, FEAT), BF16), shape((TILE, FEAT), BF16)),
        next_a,
        prev_b,
        via_up,
        via_down,
        limit=16,
        cost=50_000_000_000,
    )
    relay_up, relay_down, norm = lax.optimization_barrier((relay_up, relay_down, norm))
    own_a, own_b = table_grads(6, norm, (F32, F32))
    from_prev_a = lax.ppermute(relay_up, "dp", up)
    from_next_b = lax.ppermute(relay_down, "dp", down)

    sel = pltpu.with_memory_space_constraint(sel, pltpu.HBM)
    homeward = whole(sum_kernel, shape((NDEV, 8, FEAT), BF16), sel, parts, limit=16)
    home = swap(homeward)
    base = whole(
        base_kernel,
        shape((2 * TILE, FEAT), F32),
        own_a,
        own_b,
        from_next_a,
        from_prev_b,
        limit=16,
        cost=8_000_000_000,
    )
    grad_table, grad_queries = whole(
        finish_kernel,
        (shape((2 * TILE, FEAT), F32), shape((2, 16, 8, FEAT), F32)),
        base,
        from_prev_a,
        from_next_b,
        home.reshape(16, 2, 8, FEAT),
        hbm=(1, 2),
        hbm_out=(0, 1),
        limit=16,
        scratch=(
            pltpu.VMEM((2 * TILE, FEAT), BF16),
            pltpu.VMEM((2 * TILE, FEAT), F32),
            pltpu.VMEM((2, 16, 8, FEAT), F32),
            sems(4),
            sems(4),
            pltpu.SemaphoreType.DMA,
        ),
    )
    grad_queries = grad_queries.reshape(256, FEAT)
    return loss.reshape(256), grad_queries, grad_table[None]

def solution(mesh):
    placed = (
        P(("dp", "label"), None),
        P("label", None, None),
        P(("dp", "label"), None),
        P(("dp", "label")),
        P(),
    )
    return jax.shard_map(
        per_device,
        mesh=mesh,
        in_specs=placed,
        out_specs=(P(("dp", "label")), P(("dp", "label"), None), P("label", "dp", None)),
        check_vma=False,
    )
```

```python
import functools

import jax
import jax.numpy as jnp
from jax import lax
from jax.experimental import pallas as pl
from jax.experimental.pallas import tpu as pltpu
from jax.sharding import PartitionSpec as P

F32 = jnp.float32
BF16 = jnp.bfloat16
NDEV = 32
SLOTS = 8
ROWS = 128
FEAT = 768
HALF = 384
LABELS = 4096
TILE = 512
BIG_TILE = 1024
PART_TILE = 256
NEG = -1e30
BIG = 1e30
LIMIT = 24

def iota(shape, dim):
    return lax.broadcasted_iota(jnp.int32, shape, dim)

def dot(a, b, dims):
    return lax.dot_general(a, b, (dims, ((), ())), preferred_element_type=F32)

def ones_where(mask):
    return jnp.where(mask, 1.0, 0.0).astype(BF16)

def slot_table(meta, held):
    n = held.shape[0]
    r = iota((256, 64), 0)
    q = iota((256, 64), 1)
    pick = ones_where((r // 8 == q % 32) & (r % 8 == 6 + q // 32))
    beams = dot(meta, pick, ((0,), (0,)))
    hit = held == beams[0:1, :]
    for k in range(1, 4):
        hit = hit | (held == beams[k : k + 1, :])
    hit = hit & (iota((n, 64), 1) >= 0)
    before = ones_where(iota((64, 64), 0) < iota((64, 64), 1))
    rank = dot(ones_where(hit), before, ((1,), (0,)))
    slot = (iota((n, 64), 0) % SLOTS).astype(F32)
    return jnp.where(hit & (rank == slot), 1.0, 0.0)

def piece_matrix(table):
    e = iota((64, 512), 1)
    spread = ones_where(iota((64, 512), 0) == e // 8)
    wide = dot(table.astype(BF16), spread, ((1,), (0,)))
    same = jnp.where(iota((8, 512), 0) == (iota((8, 512), 1) & 7), 1.0, 0.0)
    return (wide[:, None, :] * same[None]).reshape(2048, 512).astype(BF16)

def route_kernel(got_ref, held_ref, out_ref):
    got = got_ref[...]
    table = slot_table(got[:, FEAT:], held_ref[...][:, :1])
    m = piece_matrix(table)
    x = jnp.concatenate([got[:, :HALF], got[:, HALF:FEAT]], axis=0)
    out_ref[...] = dot(m, x, ((1,), (0,))).astype(BF16)


def table_kernel(got_ref, held_ref, mine_ref, sel_ref, mask_ref, col_ref, slots_ref):
    meta = got_ref[...][:, FEAT:]
    table = slot_table(meta, held_ref[...][:, :1])
    sel_ref[...] = piece_matrix(table).T
    mine = mine_ref[...]
    own = slot_table(meta, mine[:, 0:1])
    row = iota((16, 64), 0)
    q = iota((16, 64), 1).astype(F32)
    home = jnp.where(q == (row.astype(F32) - 8.0) * 32.0 + mine[:, 1:2], 1.0, 0.0)
    own = jnp.where(row < 8, own, jnp.where(row < 10, home, 0.0)).astype(BF16)
    mask = dot(table.astype(BF16), own, ((1,), (1,)))
    mask_ref[...] = jnp.concatenate([mask, jnp.zeros((256, 112), F32)], axis=1)
    qq = iota((64, 256), 0)
    rr = iota((64, 256), 1)
    part = []
    for c in range(3):
        pick = ones_where((rr // 8 == qq % 32) & (rr % 8 == 3 * (qq // 32) + c))
        where_c = dot(own, pick, ((1,), (0,))).astype(BF16)
        part.append(dot(where_c, meta, ((1,), (0,))))
    inside = part[0] == mine[:, 0:1] + 1.0
    col = jnp.where(inside, part[1] * 64.0 + part[2], -1.0)
    slots_ref[...] = col[:SLOTS]
    for s in range(SLOTS):
        piece = col[s : s + 1].astype(jnp.int32)
        col_ref[:, s * ROWS : (s + 1) * ROWS] = jnp.broadcast_to(piece, (8, ROWS))

def start(copies):
    for c in copies:
        c.start()
    return copies

def pieces_kernel(q_hbm, pos_hbm, beam_hbm, out_ref, q_ref, pos_ref, beam_ref, sems):
    small = start(
        [
            pltpu.make_async_copy(pos_hbm, pos_ref, sems.at[0]),
            pltpu.make_async_copy(beam_hbm, beam_ref, sems.at[1]),
        ]
    )
    large = start(
        [
            pltpu.make_async_copy(q_hbm.at[:, pl.ds(8 * i, 8)], q_ref.at[:, pl.ds(8 * i, 8)], sems.at[2 + i])
            for i in range(2)
        ]
    )
    for c in small:
        c.wait()
    pos = pos_ref[...]
    beam = beam_ref[...]
    high, low = (pos >> 12) + 1, pos & (LABELS - 1)
    codes = (high, low >> 6, low & 63)
    row = iota((8, ROWS), 0)
    lane = iota((8, ROWS), 1)
    meta = jnp.full((8, ROWS), -1, jnp.int32)
    for b in range(2):
        for c in range(3):
            meta = jnp.where(row == 3 * b + c, codes[c][b : b + 1, :], meta)
        for k in range(beam.shape[1]):
            meta = jnp.where((row == 6 + b) & (lane == k), beam[b : b + 1, k : k + 1], meta)
    meta = meta.astype(F32).astype(BF16)
    out_ref[:, :, :, FEAT:] = jnp.broadcast_to(meta[None, None], (16, 2, 8, ROWS))
    for i in range(2):
        large[i].wait()
        g = slice(8 * i, 8 * i + 8)
        for h in range(2):
            for b in range(2):
                out_ref[g, h, :, b * HALF : (b + 1) * HALF] = q_ref[b, g, :, h * HALF : (h + 1) * HALF]

def label_iota(rows):
    return iota((PART_TILE, rows), 0).reshape(PART_TILE // 8, 8, rows)


def by_slot(lanes):
    row = iota((SLOTS, ROWS), 0)
    out = jnp.zeros((SLOTS, ROWS), F32)
    for s in range(SLOTS):
        out = jnp.where(row == s, lanes[:, s * ROWS : (s + 1) * ROWS], out)
    return out

def scores_kernel(got_ref, col_ref, w_ref, p_ref, q_ref, top_ref, stat_ref, row_ref, s_ref, high, total, found):
    step = pl.program_id(0)
    rows = s_ref.shape[1]

    @pl.when(step == 0)
    def _():
        for g in range(16):
            for h in range(2):
                for s in range(SLOTS):
                    here = slice(s * ROWS + g * 8, s * ROWS + g * 8 + 8)
                    q_ref[here, h * HALF : (h + 1) * HALF] = got_ref[g, h, s]
        high[...] = jnp.full_like(high, NEG)
        total[...] = jnp.zeros_like(total)
        found[...] = jnp.zeros_like(found)

    n = BIG_TILE // PART_TILE
    top, tot, pick = high[...], total[...], found[...]
    for k in range(n + 1):
        if k < n:
            here = slice(k * PART_TILE, (k + 1) * PART_TILE)
            s_ref[here, :] = dot(w_ref[here, :], q_ref[...], ((1,), (1,)))
        if k > 0:
            here = slice((k - 1) * PART_TILE, k * PART_TILE)
            s = s_ref[here, :]
            target = iota(s.shape, 0) + (step * BIG_TILE + (k - 1) * PART_TILE) == col_ref[0:1, :]
            pick += jnp.sum(jnp.where(target, s, 0.0).reshape(PART_TILE // 8, 8, rows), axis=0)
            best = jnp.max(jnp.max(s.reshape(PART_TILE // 8, 8, rows), axis=0), axis=0, keepdims=True)
            best = jnp.broadcast_to(best, (8, rows))
            e = jnp.exp(s - best[0:1, :])
            p_ref[here, :] = jnp.where(target, 0.0, e).astype(BF16)
            new = jnp.maximum(top, best)
            add = jnp.sum(e.reshape(PART_TILE // 8, 8, rows), axis=0)
            tot = tot * jnp.exp(top - new) + add * jnp.exp(best - new)
            top = new
            top_ref[k - 1] = best
    high[...], total[...], found[...] = top, tot, pick

    @pl.when(step == pl.num_programs(0) - 1)
    def _():
        lse = top[0:1, :] + jnp.log(jnp.sum(tot, axis=0, keepdims=True))
        row_ref[...] = jnp.broadcast_to(lse, (8, rows))
        chosen = jnp.sum(pick, axis=0, keepdims=True)
        stat_ref[:, :SLOTS, :] = jnp.broadcast_to(by_slot(lse)[None], (NDEV, SLOTS, ROWS))
        stat_ref[:, SLOTS:, :] = jnp.broadcast_to(by_slot(chosen)[None], (NDEV, SLOTS, ROWS))


def normal_kernel(stat_ref, mask_ref, norm_ref, rest_ref, slots_ref, loss_ref):
    lse = stat_ref[:, :SLOTS, :].reshape(NDEV * SLOTS, ROWS)
    found = stat_ref[:, SLOTS:, :].reshape(NDEV * SLOTS, ROWS)
    mask = mask_ref[...]
    for s in range(SLOTS + 2):
        use = mask[:, s : s + 1] > 0.5
        kept = jnp.where(use, lse, NEG)
        high = jnp.max(kept, axis=0, keepdims=True)
        tot = jnp.sum(jnp.where(use, jnp.exp(kept - high), 0.0), axis=0, keepdims=True)
        value = jnp.where(high > 0.5 * NEG, high + jnp.log(tot), BIG)
        positive = jnp.sum(jnp.where(use, found, 0.0), axis=0, keepdims=True)
        if s < SLOTS:
            here = slice(s * ROWS, (s + 1) * ROWS)
            norm_ref[:, here] = jnp.broadcast_to(value, (8, ROWS))
            rest_ref[:, here] = jnp.broadcast_to(jnp.exp(positive - value) - 1.0, (8, ROWS))
            slots_ref[s : s + 1, :] = value
        else:
            loss_ref[s - SLOTS : s - SLOTS + 1, :] = value - positive


def rows_from(acc, out_ref):
    for s in range(SLOTS):
        here = slice(s * ROWS, (s + 1) * ROWS)
        out_ref[here, :] = acc[:, here].T.astype(out_ref.dtype)


def add_to(acc, term, first):
    @pl.when(first)
    def _():
        acc[...] = term

    @pl.when(jnp.logical_not(first))
    def _():
        acc[...] += term


def positive_kernel(col_ref, w_ref, out_ref, acc):
    step = pl.program_id(0)
    target = iota((BIG_TILE, acc.shape[1]), 0) + step * BIG_TILE == col_ref[0:1, :]
    add_to(acc, dot(w_ref[...], ones_where(target), ((0,), (0,))), step == 0)

    @pl.when(step == pl.num_programs(0) - 1)
    def _():
        rows_from(acc, out_ref)


def others_kernel(top_ref, row_ref, w_ref, p_ref, out_ref, acc, scaled):
    step = pl.program_id(0)
    for i in range(BIG_TILE // PART_TILE):
        scale = jnp.exp(top_ref[i] - row_ref[...])
        here = slice(i * PART_TILE, (i + 1) * PART_TILE)
        p = p_ref[here, :].astype(F32).reshape(PART_TILE // 8, 8, scale.shape[1])
        scaled[here, :] = (p * scale[None]).reshape(PART_TILE, scale.shape[1]).astype(BF16)
    add_to(acc, dot(w_ref[...], scaled[...], ((0,), (0,))), step == 0)

    @pl.when(step == pl.num_programs(0) - 1)
    def _():
        rows_from(acc, out_ref)


def part_kernel(u_ref, r_ref, stat_ref, norm_ref, col_ref, out_ref):
    norm = norm_ref[...]
    scale = jnp.exp(stat_ref[0, :SLOTS, :] - norm).T
    rest = jnp.where(col_ref[...] >= 0.0, jnp.exp(stat_ref[0, SLOTS:, :] - norm) - 1.0, 0.0).T
    for s in range(SLOTS):
        u = u_ref[s * ROWS : (s + 1) * ROWS, :].astype(F32)
        r = r_ref[s * ROWS : (s + 1) * ROWS, :].astype(F32)
        part = (scale[:, s : s + 1] * u + rest[:, s : s + 1] * r).astype(BF16).reshape(16, 8, FEAT)
        for h in range(2):
            out_ref[:, h, s * 8 : (s + 1) * 8, :] = part[:, :, h * HALF : (h + 1) * HALF]


def table_grad_kernel(base, tiles_ref, q_ref, norm_ref, rest_ref, col_ref, *refs):
    n = len(refs) // 3
    for i in range(n):
        p_ref, top_ref, out_ref = refs[i], refs[n + i], refs[2 * n + i]
        tile = tiles_ref[base + i]
        for k in range(TILE // PART_TILE):
            here = slice(k * PART_TILE, (k + 1) * PART_TILE)
            scale = jnp.exp(top_ref[k] - norm_ref[...])
            rows = scale.shape[1]
            p = p_ref[here, :].astype(F32).reshape(PART_TILE // 8, 8, rows)
            target = label_iota(rows) == (col_ref[...] - (tile * TILE + k * PART_TILE))[None]
            slope = jnp.where(target, rest_ref[...][None], p * scale[None])
            slope = slope.reshape(PART_TILE, rows).astype(BF16)
            out_ref[here, :] = dot(slope, q_ref[...], ((1,), (0,))).astype(out_ref.dtype)


def sum_kernel(sel_ref, parts_ref, out_ref):
    out = dot(sel_ref[...], parts_ref[...], ((1,), (0,))).astype(BF16)
    for b in range(2):
        out_ref[:, :, b * HALF : (b + 1) * HALF] = out[b * 256 : (b + 1) * 256].reshape(NDEV, 8, HALF)

def relay_kernel(up_ref, down_ref, got_up_ref, got_down_ref, out_up_ref, out_down_ref):
    out_up_ref[...] = (up_ref[...] + got_up_ref[...].astype(F32)).astype(BF16)
    out_down_ref[...] = (down_ref[...] + got_down_ref[...].astype(F32)).astype(BF16)


def base_kernel(own_a_ref, own_b_ref, a_ref, b_ref, out_ref):
    out_ref[:TILE, :] = own_a_ref[...] + a_ref[...].astype(F32)
    out_ref[TILE:, :] = own_b_ref[...] + b_ref[...].astype(F32)


def finish_kernel(base_ref, a_hbm, b_hbm, home_ref, out_hbm, grad_hbm, got, out_v, grad_v, in_sems, out_sems, grad_sem):
    tile = PART_TILE
    per = TILE // tile
    copies = start(
        [
            pltpu.make_async_copy(
                src.at[pl.ds(k * tile, tile)], got.at[pl.ds((i * per + k) * tile, tile)], in_sems.at[i * per + k]
            )
            for i, src in enumerate((a_hbm, b_hbm))
            for k in range(per)
        ]
    )
    for h in range(2):
        for b in range(2):
            piece = home_ref[:, h, :, b * HALF : (b + 1) * HALF].astype(F32)
            grad_v[b, :, :, h * HALF : (h + 1) * HALF] = piece
    grad = pltpu.make_async_copy(grad_v, grad_hbm, grad_sem)
    grad.start()
    out = []
    for j in range(2 * per):
        here = slice(j * tile, (j + 1) * tile)
        copies[j].wait()
        out_v[here, :] = base_ref[here, :] + got[here, :].astype(F32)
        c = pltpu.make_async_copy(out_v.at[pl.ds(j * tile, tile)], out_hbm.at[pl.ds(j * tile, tile)], out_sems.at[j])
        c.start()
        out.append(c)
    grad.wait()
    for c in out:
        c.wait()


def shape(dims, dtype):
    return jax.ShapeDtypeStruct(dims, dtype)

def whole(kernel, out, *args, hbm=(), smem=(), hbm_out=(), limit=60, cost=1024, scratch=()):
    def place(i, far, scalar=()):
        space = pltpu.HBM if i in far else pltpu.SMEM if i in scalar else pltpu.VMEM
        return pl.BlockSpec(memory_space=space)

    single = not isinstance(out, tuple)
    outs = (out,) if single else out
    results = pl.pallas_call(
        kernel,
        out_shape=outs,
        in_specs=[place(i, hbm, smem) for i in range(len(args))],
        out_specs=tuple(place(i, hbm_out) for i in range(len(outs))),
        scratch_shapes=list(scratch),
        compiler_params=pltpu.CompilerParams(vmem_limit_bytes=limit << 20),
        cost_estimate=pl.CostEstimate(flops=cost, transcendentals=0, bytes_accessed=1024),
    )(*args)
    return results[0] if single else results

def fixed(dims):
    return pl.BlockSpec(dims, lambda *_: (0,) * len(dims))


def tiled(dims):
    return pl.BlockSpec(dims, lambda i, *_: (i,) + (0,) * (len(dims) - 1))


def stepped(kernel, grid, in_specs, outs, out_specs, scratch, *args, limit=LIMIT, scalars=0, cost=1024):
    spec = pltpu.PrefetchScalarGridSpec(
        num_scalar_prefetch=scalars,
        grid=(grid,),
        in_specs=in_specs,
        out_specs=out_specs,
        scratch_shapes=list(scratch),
    )
    return pl.pallas_call(
        kernel,
        grid_spec=spec,
        out_shape=outs,
        compiler_params=pltpu.CompilerParams(vmem_limit_bytes=limit << 20),
        cost_estimate=pl.CostEstimate(flops=cost, transcendentals=0, bytes_accessed=1024),
    )(*args)


def sems(n):
    return pltpu.SemaphoreType.DMA((n,))


def per_device(queries, weights, beam, positives, owner):
    me = lax.axis_index("label")
    y = lax.axis_index("dp")
    rows = SLOTS * ROWS
    ranker = pltpu.with_memory_space_constraint(weights[0], pltpu.HBM)

    def swap(x):
        return lax.all_to_all(x, "label", split_axis=0, concat_axis=0, tiled=True)

    ids = jnp.arange(NDEV, dtype=jnp.int32)
    held = jnp.sum(jnp.where(owner[None, :] == ids[:, None], ids[None, :], 0), axis=1).astype(F32)
    held_rows = jnp.broadcast_to(held[:, None, None], (NDEV, SLOTS, 128)).reshape(256, 128)
    my_block = jnp.sum(jnp.where(owner == me, ids, 0)).astype(F32)
    mine = jnp.where(iota((16, 128), 1) == 0, my_block, me.astype(F32))

    pieces = whole(
        pieces_kernel,
        shape((16, 2, 8, FEAT + ROWS), BF16),
        queries.reshape(2, 16, 8, FEAT),
        positives.reshape(2, ROWS),
        beam,
        hbm=(0, 1, 2),
        scratch=(
            pltpu.VMEM((2, 16, 8, FEAT), BF16),
            pltpu.VMEM((2, ROWS), jnp.int32),
            pltpu.VMEM(beam.shape, jnp.int32),
            sems(4),
        ),
    )
    got = swap(pieces.reshape(NDEV, 8, FEAT + ROWS)).reshape(256, FEAT + ROWS)

    sent = whole(route_kernel, shape((2048, HALF), BF16), got, held_rows, limit=16)
    arrived = swap(sent.reshape(NDEV, 64, HALF))
    sel, mask, col, col_slots = whole(
        table_kernel,
        (
            pltpu.HBM((512, 2048), BF16),
            pltpu.HBM((256, 128), F32),
            shape((8, rows), jnp.int32),
            shape((SLOTS, ROWS), F32),
        ),
        got,
        held_rows,
        mine,
    )
    steps = LABELS // BIG_TILE
    w_spec = tiled((BIG_TILE, FEAT))
    lanes = shape((8, rows), F32)
    positive_rows = stepped(
        positive_kernel,
        steps,
        [fixed((8, rows)), w_spec],
        shape((rows, FEAT), BF16),
        fixed((rows, FEAT)),
        (pltpu.VMEM((FEAT, rows), F32),),
        col,
        ranker,
    )
    arrived, positive_rows, col = lax.optimization_barrier((arrived, positive_rows, col))

    parts_each = BIG_TILE // PART_TILE
    p, q, tops, stats, lse_row = stepped(
        scores_kernel,
        steps,
        [fixed((16, 2, SLOTS, 8, HALF)), fixed((8, rows)), w_spec],
        (
            pltpu.HBM((LABELS, rows), BF16),
            shape((rows, FEAT), BF16),
            pltpu.HBM((LABELS // PART_TILE, 8, rows), F32),
            shape((NDEV, 2 * SLOTS, ROWS), F32),
            lanes,
        ),
        (
            tiled((BIG_TILE, rows)),
            fixed((rows, FEAT)),
            tiled((parts_each, 8, rows)),
            fixed((NDEV, 2 * SLOTS, ROWS)),
            fixed((8, rows)),
        ),
        (
            pltpu.VMEM((BIG_TILE, rows), F32),
            pltpu.VMEM((8, rows), F32),
            pltpu.VMEM((8, rows), F32),
            pltpu.VMEM((8, rows), F32),
        ),
        pltpu.with_memory_space_constraint(arrived.reshape(16, 2, SLOTS, 8, HALF), pltpu.HBM),
        col,
        ranker,
    )
    all_stats = swap(stats)
    p = pltpu.with_memory_space_constraint(p, pltpu.HBM)
    tops = pltpu.with_memory_space_constraint(tops, pltpu.HBM)
    others = stepped(
        others_kernel,
        steps,
        [tiled((parts_each, 8, rows)), fixed((8, rows)), w_spec, tiled((BIG_TILE, rows))],
        pltpu.HBM((rows, FEAT), BF16),
        fixed((rows, FEAT)),
        (pltpu.VMEM((FEAT, rows), F32), pltpu.VMEM((BIG_TILE, rows), BF16)),
        tops,
        lse_row,
        ranker,
        p,
    )
    all_stats, others = lax.optimization_barrier((all_stats, others))
    norm, rest, norm_slots, loss = whole(
        normal_kernel,
        (lanes, lanes, shape((SLOTS, ROWS), F32), shape((2, ROWS), F32)),
        all_stats,
        pltpu.with_memory_space_constraint(mask, pltpu.HBM),
        limit=16,
    )

    up = [(i, (i + 1) % 4) for i in range(4)]
    down = [(i, (i + 3) % 4) for i in range(4)]
    across, ahead, behind = (y + 2) % 4 * 2, (y + 1) % 4 * 2, (y + 3) % 4 * 2
    tiles = jnp.stack([across, across + 1, ahead + 1, behind, ahead, behind + 1, y * 2, y * 2 + 1])
    tiles = tiles.astype(jnp.int32)

    def table_grads(first, norm, dtypes, place=pltpu.HBM):
        n = len(dtypes)
        return stepped(
            functools.partial(table_grad_kernel, first),
            1,
            [
                fixed((rows, FEAT)),
                fixed((8, rows)),
                fixed((8, rows)),
                fixed((8, rows)),
                *(pl.BlockSpec((TILE, rows), lambda _, t, i=i: (t[first + i], 0)) for i in range(n)),
                *(
                    pl.BlockSpec((TILE // PART_TILE, 8, rows), lambda _, t, i=i: (t[first + i], 0, 0))
                    for i in range(n)
                ),
            ],
            tuple(place((TILE, FEAT), d) for d in dtypes),
            tuple(fixed((TILE, FEAT)) for _ in dtypes),
            (),
            tiles,
            q,
            norm,
            rest,
            col,
            *([p] * n),
            *([tops] * n),
            scalars=1,
        )

    far_a, far_b = table_grads(0, norm, (BF16, BF16))
    far_a, far_b, norm_slots, norm = lax.optimization_barrier((far_a, far_b, norm_slots, norm))
    via_up = lax.ppermute(far_a, "dp", up)
    via_down = lax.ppermute(far_b, "dp", down)
    part = whole(
        part_kernel,
        pltpu.HBM((16, 2, 64, HALF), BF16),
        others,
        positive_rows,
        stats,
        norm_slots,
        col_slots,
        limit=16,
    )
    part, norm = lax.optimization_barrier((part, norm))
    parts = swap(part.reshape(NDEV, 64, HALF)).reshape(2048, HALF)
    next_b, prev_a = table_grads(2, norm, (BF16, BF16))
    next_b, prev_a, norm = lax.optimization_barrier((next_b, prev_a, norm))
    from_prev_b = lax.ppermute(next_b, "dp", up)
    from_next_a = lax.ppermute(prev_a, "dp", down)
    next_a, prev_b = table_grads(4, norm, (F32, F32), shape)

    relay_up, relay_down = whole(
        relay_kernel,
        (shape((TILE, FEAT), BF16), shape((TILE, FEAT), BF16)),
        next_a,
        prev_b,
        via_up,
        via_down,
        limit=16,
        cost=50_000_000_000,
    )
    relay_up, relay_down, norm = lax.optimization_barrier((relay_up, relay_down, norm))
    own_a, own_b = table_grads(6, norm, (F32, F32))
    from_prev_a = lax.ppermute(relay_up, "dp", up)
    from_next_b = lax.ppermute(relay_down, "dp", down)

    sel = pltpu.with_memory_space_constraint(sel, pltpu.HBM)
    homeward = whole(sum_kernel, shape((NDEV, 8, FEAT), BF16), sel, parts, limit=16)
    home = swap(homeward)
    base = whole(
        base_kernel,
        shape((2 * TILE, FEAT), F32),
        own_a,
        own_b,
        from_next_a,
        from_prev_b,
        limit=16,
        cost=8_000_000_000,
    )
    grad_table, grad_queries = whole(
        finish_kernel,
        (shape((2 * TILE, FEAT), F32), shape((2, 16, 8, FEAT), F32)),
        base,
        from_prev_a,
        from_next_b,
        home.reshape(16, 2, 8, FEAT),
        hbm=(1, 2),
        hbm_out=(0, 1),
        limit=16,
        scratch=(
            pltpu.VMEM((2 * TILE, FEAT), BF16),
            pltpu.VMEM((2 * TILE, FEAT), F32),
            pltpu.VMEM((2, 16, 8, FEAT), F32),
            sems(4),
            sems(4),
            pltpu.SemaphoreType.DMA,
        ),
    )
    grad_queries = grad_queries.reshape(256, FEAT)
    return loss.reshape(256), grad_queries, grad_table[None]

def solution(mesh):
    placed = (
        P(("dp", "label"), None),
        P("label", None, None),
        P(("dp", "label"), None),
        P(("dp", "label")),
        P(),
    )
    return jax.shard_map(
        per_device,
        mesh=mesh,
        in_specs=placed,
        out_specs=(P(("dp", "label")), P(("dp", "label"), None), P("label", "dp", None)),
        check_vma=False,
    )
```
